128 devices in a mesh: lon: 16 (over x_hi, z, core), lat: 8 (over y, x_lo).
Axes of the slice: x: 4 (x_hi: 2, x_lo: 2; x = x_hi * 2 + x_lo), y: 4, z: 4, core: 2. Of those that a mesh axis runs over, the one named last changes fastest.
Arguments:
- state: float32 [150, 256, 2048], P(None, 'lat', 'lon'), may hold values from -6 to 6
- diffusivity: float32 [150, 256, 2048], P(None, 'lat', 'lon'), may hold values from 0.02 to 0.24
- sea_mask: int32 [75, 256, 2048], P(None, 'lat', 'lon'), may hold values 0 or 1
- send_cols: int32 [128, 3072], P(('lon', 'lat')), may hold values from 0 to 4096, as said below
- obs_slots: int32 [4, 262144], P(None, ('lon', 'lat')), may hold values from 0 to 3071, as said below
- obs_weights: float32 [4, 262144], P(None, ('lon', 'lat')), may hold values from 0.05 to 0.5
- obs_precision: float32 [150, 262144], P(None, ('lon', 'lat')), may hold values from 0.25 to 4
Outputs:
- product: float32 [150, 256, 2048], P(None, 'lat', 'lon')
- equivalents: float32 [150, 262144], P(None, ('lon', 'lat'))
The draws below stay inside these ranges and needn't reach their ends.
Inputs may be any that keep to these rules, and one draw needn't show every extreme that they name: `send_cols`: for each device s and owner o the first n entries of the owner's 24 entries are local column indices below 4096, the rest are 4096; n is at least 1 and at most 24; every device has some owner with n = 24, and some owner receives 24 columns from every device. `obs_slots`: every slot named refers to a live entry: for owner o, slot s * 24 + p with p below the number of live entries of device s for owner o.
All inputs are finite; a program needn't handle non-finite values. No bound on the sum of `sea_mask` on one device may be relied on, other than what follows from the above.
Results may differ from the reference program's by a relative error of at most 0.00002.
Values sent between devices are 32-bit elements; how exact they have to be, the bound alone decides.
A program may use at most 128 MiB of HBM per device.

```python
import math
import jax
import jax.numpy as jnp
from jax import lax

LEVELS = 75
VALS = 150
CLAT = 32
CLON = 128
SWEEPS = 2
CAP = 24
OBS_DEV = 2048
OWNERS = 128
CELLS = 4096
NLAT = 256
NLON = 2048
NOBS = 262144
N_LON = 16
N_LAT = 8


def pair_counts(key):
    base = jax.random.fold_in(key, 11)
    first, second, third = jax.random.split(base, 3)
    counts = jax.random.randint(first, (OWNERS, OWNERS), CAP // 3, CAP + 1)
    order = jax.random.permutation(second, OWNERS)
    counts = counts.at[jnp.arange(OWNERS), order].set(CAP)
    full_owner = jax.random.randint(third, (), 0, OWNERS)
    counts = counts.at[:, full_owner].set(CAP)
    sparse_owner = jnp.where(order[1] == full_owner, order[2], order[1])
    counts = counts.at[0, sparse_owner].set(1)
    return counts


def draw_send_cols(key, part):
    counts = pair_counts(key)
    cell_ids = jax.random.randint(jax.random.fold_in(key, 12), (OWNERS, OWNERS, CAP), 0, CELLS)
    cell_ids = cell_ids.at[0, :, 0].set(0)
    position = jnp.arange(CAP)
    live = position[None, None, :] < counts[:, :, None]
    return jnp.where(live, cell_ids, CELLS).reshape(OWNERS, OWNERS * CAP).astype(jnp.int32)


def draw_obs_slots(key, part):
    counts = pair_counts(key)
    base = jax.random.fold_in(key, 13)
    first, second = jax.random.split(base, 2)
    source = jax.random.randint(first, (4, OWNERS, OBS_DEV), 0, OWNERS)
    owner_ids = jnp.arange(OWNERS)[None, :, None]
    limits = counts[source, owner_ids]
    position = jax.random.randint(second, (4, OWNERS, OBS_DEV), 0, limits)
    slot_ids = source * CAP + position
    slot_ids = slot_ids.at[0, :, 0].set((OWNERS - 1) * CAP + counts[OWNERS - 1, :] - 1)
    slot_ids = slot_ids.at[1, :, 0].set(0)
    return slot_ids.reshape(4, OWNERS * OBS_DEV).astype(jnp.int32)


def touch_ends(values, rng, least, largest):
    longest = values.shape.index(max(values.shape))
    spots = []
    for shift in (0, 1):
        where = [jax.random.randint(jax.random.fold_in(rng, axis), (), 0, length) for axis, length in enumerate(values.shape)]
        where[longest] = (where[longest] + shift) % values.shape[longest]
        spots.append(tuple(where))
    return values.at[spots[0]].set(least).at[spots[1]].set(largest)


def block_scale(own_key, extent, cuts, smallest, high):
    def one(dim, parts):
        steps = jax.random.uniform(jax.random.fold_in(jax.random.fold_in(own_key, 6), dim), (parts,), jnp.float32, smallest / len(cuts), high / len(cuts))
        return jnp.repeat(jnp.exp(steps), extent[dim] // parts).reshape((-1,) + (1,) * (len(extent) - dim - 1))

    loudness = one(*cuts[0])
    for cut in cuts[1:]:
        loudness = loudness * one(*cut)
    return loudness


def noise(own_key, extent, deviation, bound, cuts=(), held_as=jnp.bfloat16):
    array = deviation * jax.random.normal(own_key, extent, jnp.float32)
    if cuts:
        array = array * block_scale(own_key, extent, cuts, -0.22, 0.18)
    return jnp.clip(array, -bound, bound).astype(held_as)


def setup_inputs(seed: int = 0) -> dict:
    arg_keys = jax.random.split(jax.random.key(seed), 8)
    return {
        "state": noise(arg_keys[0], (VALS, NLAT, NLON), 1.0, 6.0, ((1, 8), (2, 16)), jnp.float32),
        "diffusivity": jnp.clip(0.02 + 0.22 * jax.random.uniform(arg_keys[1], (VALS, NLAT, NLON), jnp.float32) ** block_scale(arg_keys[1], (VALS, NLAT, NLON), ((1, 8), (2, 16)), -0.2, 0.2), 0.02, 0.24),
        "sea_mask": touch_ends((jax.random.randint(arg_keys[2], (LEVELS, NLAT, NLON), 0, 10) < 9).astype(jnp.int32), jax.random.fold_in(arg_keys[2], 1), 0, 1),
        "send_cols": draw_send_cols(jax.random.fold_in(arg_keys[7], 71), 0),
        "obs_slots": draw_obs_slots(jax.random.fold_in(arg_keys[7], 71), 0),
        "obs_weights": jnp.clip(0.05 + 0.45 * jax.random.uniform(arg_keys[5], (4, NOBS), jnp.float32) ** block_scale(arg_keys[5], (4, NOBS), ((1, 128),), -0.2, 0.2), 0.05, 0.5),
        "obs_precision": jnp.clip(jnp.exp(math.log(4.0) - 2.7725887 * jax.random.uniform(arg_keys[6], (VALS, NOBS), jnp.float32) ** block_scale(arg_keys[6], (VALS, NOBS), ((1, 128),), -0.2, 0.2)), 0.25, 4.0),
    }


def widen(field):
    field = jnp.concatenate([field[:, :, -1:], field, field[:, :, :1]], axis=2)
    return jnp.pad(field, ((0, 0), (1, 1), (0, 0)))


def relax_step(wide_field, wide_coef):
    centre = wide_field[:, 1:-1, 1:-1]
    centre_coef = wide_coef[:, 1:-1, 1:-1]
    total = jnp.minimum(centre_coef, wide_coef[:, 2:, 1:-1]) * (wide_field[:, 2:, 1:-1] - centre)
    total = total + jnp.minimum(centre_coef, wide_coef[:, :-2, 1:-1]) * (wide_field[:, :-2, 1:-1] - centre)
    total = total + jnp.minimum(centre_coef, wide_coef[:, 1:-1, :-2]) * (wide_field[:, 1:-1, :-2] - centre)
    total = total + jnp.minimum(centre_coef, wide_coef[:, 1:-1, 2:]) * (wide_field[:, 1:-1, 2:] - centre)
    return centre + total


def diffuse(field, conduct):
    wide_coef = widen(conduct)
    for sweep in range(SWEEPS):
        field = relax_step(widen(field), wide_coef)
    return field


def to_blocks(field):
    vals = field.shape[0]
    shaped = field.reshape(vals, N_LAT, CLAT, N_LON, CLON).transpose(0, 3, 1, 2, 4)
    return shaped.reshape(vals, OWNERS, CLAT * CLON)


def from_blocks(blocks):
    vals = blocks.shape[0]
    shaped = blocks.reshape(vals, N_LON, N_LAT, CLAT, CLON).transpose(0, 2, 3, 1, 4)
    return shaped.reshape(vals, NLAT, NLON)


def reference(state, diffusivity, sea_mask, send_cols, obs_slots, obs_weights, obs_precision):
    vals = state.shape[0]
    sea_float = sea_mask.astype(jnp.float32)
    conduct = diffusivity * jnp.concatenate([sea_float, sea_float], axis=0)
    smooth = diffuse(state, conduct)
    blocks = to_blocks(smooth)
    padded = jnp.concatenate([blocks, jnp.zeros((vals, OWNERS, 1), jnp.float32)], axis=2)
    sources = jnp.arange(OWNERS, dtype=jnp.int32)[:, None]

    def per_owner(adjoint_sum, owner):
        picked = lax.dynamic_slice_in_dim(send_cols, owner * CAP, CAP, 1)
        gathered = padded[:, sources, picked].reshape(vals, OWNERS * CAP)
        slot_ids = lax.dynamic_slice_in_dim(obs_slots, owner * OBS_DEV, OBS_DEV, 1)
        weights = lax.dynamic_slice_in_dim(obs_weights, owner * OBS_DEV, OBS_DEV, 1)
        inverse_var = lax.dynamic_slice_in_dim(obs_precision, owner * OBS_DEV, OBS_DEV, 1)
        equivalent = jnp.zeros((vals, OBS_DEV), jnp.float32)
        for tap in range(obs_slots.shape[0]):
            equivalent = equivalent + weights[tap][None, :] * gathered[:, slot_ids[tap]]
        weighted = inverse_var * equivalent
        returned = jnp.zeros((vals, OWNERS * CAP), jnp.float32)
        for tap in range(obs_slots.shape[0]):
            returned = returned.at[:, slot_ids[tap]].add(weights[tap][None, :] * weighted)
        adjoint_sum = adjoint_sum.at[:, sources, picked].add(returned.reshape(vals, OWNERS, CAP))
        return adjoint_sum, equivalent

    start_sum = jnp.zeros((vals, OWNERS, CLAT * CLON + 1), jnp.float32)
    adjoint_sum, stacked = lax.scan(per_owner, start_sum, jnp.arange(OWNERS, dtype=jnp.int32))
    equivalents = stacked.transpose(1, 0, 2).reshape(vals, OWNERS * OBS_DEV)
    adjoint = from_blocks(adjoint_sum[:, :, :CLAT * CLON])
    product = state + diffuse(adjoint, conduct)
    return product, equivalents
```

```python
import functools

import jax
import jax.numpy as jnp
from jax import lax
from jax.experimental import pallas as pl
from jax.experimental.pallas import tpu as pltpu
from jax.sharding import PartitionSpec as P

SWEEPS = 2
GROUP = 30


def shift_lat(edge, down):
    count = lax.axis_size("lat")
    if down:
        pairs = [(i, i + 1) for i in range(count - 1)]
    else:
        pairs = [(i + 1, i) for i in range(count - 1)]
    return lax.ppermute(edge, "lat", pairs)


def shift_lon(edge, east):
    count = lax.axis_size("lon")
    if east:
        pairs = [(i, (i + 1) % count) for i in range(count)]
    else:
        pairs = [((i + 1) % count, i) for i in range(count)]
    return lax.ppermute(edge, "lon", pairs)


def halos(top, bottom, left, right):
    return (
        shift_lat(bottom, True),
        shift_lat(top, False),
        shift_lon(right, True),
        shift_lon(left, False),
    )


def sweep_kernel(rows, v_ref, c_ref, vn_ref, vs_ref, vw_ref, ve_ref, cn_ref, cs_ref, cw_ref, ce_ref,
                 w_ref, top_ref, bot_ref, left_ref, right_ref):
    group = vn_ref.shape[1]
    lanes = v_ref.shape[2]
    lane = lax.broadcasted_iota(jnp.int32, (group, lanes), 1)
    col = lax.broadcasted_iota(jnp.int32, (group, rows), 1)

    def slab(ref, r):
        return ref[0, pl.ds(r, group, stride=rows), :]

    vw = vw_ref[0]
    ve = ve_ref[0]
    cw = cw_ref[0]
    ce = ce_ref[0]
    left = jnp.zeros((group, rows), jnp.float32)
    right = jnp.zeros((group, rows), jnp.float32)
    x_up, c_up = vn_ref[0], cn_ref[0]
    x_mid, c_mid = slab(v_ref, 0), slab(c_ref, 0)
    for r in range(rows):
        if r + 1 < rows:
            x_dn, c_dn = slab(v_ref, r + 1), slab(c_ref, r + 1)
        else:
            x_dn, c_dn = vs_ref[0], cs_ref[0]
        x_w = jnp.where(lane == 0, vw[:, r : r + 1], pltpu.roll(x_mid, 1, 1))
        x_e = jnp.where(lane == lanes - 1, ve[:, r : r + 1], pltpu.roll(x_mid, lanes - 1, 1))
        c_w = jnp.where(lane == 0, cw[:, r : r + 1], pltpu.roll(c_mid, 1, 1))
        c_e = jnp.where(lane == lanes - 1, ce[:, r : r + 1], pltpu.roll(c_mid, lanes - 1, 1))
        total = jnp.minimum(c_mid, c_up) * (x_up - x_mid)
        total = total + jnp.minimum(c_mid, c_dn) * (x_dn - x_mid)
        total = total + jnp.minimum(c_mid, c_w) * (x_w - x_mid)
        total = total + jnp.minimum(c_mid, c_e) * (x_e - x_mid)
        out = x_mid + total
        w_ref[0, pl.ds(r, group, stride=rows), :] = out
        if r == 0:
            top_ref[0] = out
        if r == rows - 1:
            bot_ref[0] = out
        left = jnp.where(col == r, out[:, 0:1], left)
        right = jnp.where(col == r, out[:, lanes - 1 : lanes], right)
        x_up, c_up = x_mid, c_mid
        x_mid, c_mid = x_dn, c_dn
    left_ref[0] = left
    right_ref[0] = right


def sweep(field, conduct, field_halos, coef_halos):
    steps, span, lanes = field.shape
    rows = span // GROUP
    big = pl.BlockSpec((1, span, lanes), lambda i: (i, 0, 0))
    row_edge = pl.BlockSpec((1, GROUP, lanes), lambda i: (i, 0, 0))
    col_edge = pl.BlockSpec((1, GROUP, rows), lambda i: (i, 0, 0))
    edge_specs = [row_edge, row_edge, col_edge, col_edge]
    return pl.pallas_call(
        functools.partial(sweep_kernel, rows),
        grid=(steps,),
        in_specs=[big, big] + edge_specs + edge_specs,
        out_specs=[big] + edge_specs,
        out_shape=[
            jax.ShapeDtypeStruct(field.shape, jnp.float32),
            jax.ShapeDtypeStruct((steps, GROUP, lanes), jnp.float32),
            jax.ShapeDtypeStruct((steps, GROUP, lanes), jnp.float32),
            jax.ShapeDtypeStruct((steps, GROUP, rows), jnp.float32),
            jax.ShapeDtypeStruct((steps, GROUP, rows), jnp.float32),
        ],
        cost_estimate=pl.CostEstimate(
            flops=20 * field.size, bytes_accessed=12 * field.size, transcendentals=0
        ),
    )(field, conduct, *field_halos, *coef_halos)


def edges_of(field):
    vals, rows, lanes = field.shape
    steps = vals // GROUP
    top = field[:, 0, :].reshape(steps, GROUP, lanes)
    bottom = field[:, rows - 1, :].reshape(steps, GROUP, lanes)
    left = field[:, :, 0].reshape(steps, GROUP, rows)
    right = field[:, :, lanes - 1].reshape(steps, GROUP, rows)
    return top, bottom, left, right


def diffuse(field, conduct_blocks, coef_halos):
    vals, rows, lanes = field.shape
    steps = vals // GROUP
    edges = edges_of(field)
    current = field.reshape(steps, GROUP * rows, lanes)
    for _ in range(SWEEPS):
        current, *edges = sweep(current, conduct_blocks, halos(*edges), coef_halos)
    return current.reshape(vals, rows, lanes)


def to_owners(outgoing):
    return lax.all_to_all(outgoing, ("lon", "lat"), split_axis=1, concat_axis=1, tiled=True)


def to_sources(returned):
    return lax.all_to_all(returned, ("lon", "lat"), split_axis=1, concat_axis=1, tiled=True)


def on_device(state, diffusivity, sea_mask, send_cols, obs_slots, obs_weights, obs_precision):
    vals, rows, lanes = state.shape
    cell_count = rows * lanes
    steps = vals // GROUP
    sea_float = sea_mask.astype(jnp.float32)
    conduct = diffusivity * jnp.concatenate([sea_float, sea_float], axis=0)
    coef_halos = halos(*edges_of(conduct))
    conduct_blocks = conduct.reshape(steps, GROUP * rows, lanes)
    smooth = diffuse(state, conduct_blocks, coef_halos)
    flat_cols = jnp.concatenate(
        [smooth.reshape(vals, cell_count), jnp.zeros((vals, 1), jnp.float32)], axis=1
    )
    send_index = send_cols[0]
    outgoing = jnp.take(flat_cols, send_index, axis=1)
    received = to_owners(outgoing)
    slot_count = outgoing.shape[1]
    taps, obs_count = obs_slots.shape
    all_slots = obs_slots.reshape(taps * obs_count)
    picked = jnp.take(received, all_slots, axis=1).reshape(vals, taps, obs_count)
    equivalents = jnp.sum(picked * obs_weights[None, :, :], axis=1)
    weighted = obs_precision * equivalents
    spread = (weighted[:, None, :] * obs_weights[None, :, :]).reshape(vals, taps * obs_count)
    returned = jnp.zeros((vals, slot_count), jnp.float32).at[:, all_slots].add(spread)
    incoming = to_sources(returned)
    adjoint_cols = jnp.zeros((vals, cell_count + 1), jnp.float32).at[:, send_index].add(incoming)
    adjoint_field = adjoint_cols[:, :cell_count].reshape(state.shape)
    product = state + diffuse(adjoint_field, conduct_blocks, coef_halos)
    return (product, equivalents)


def solution(mesh):
    placed = (
        P(None, "lat", "lon"),
        P(None, "lat", "lon"),
        P(None, "lat", "lon"),
        P(("lon", "lat"), None),
        P(None, ("lon", "lat")),
        P(None, ("lon", "lat")),
        P(None, ("lon", "lat")),
    )
    return jax.shard_map(
        on_device,
        mesh=mesh,
        in_specs=placed,
        out_specs=(P(None, "lat", "lon"), P(None, ("lon", "lat"))),
        check_vma=False,
    )
```

```python
import functools

import jax
import jax.numpy as jnp
from jax import lax
from jax.experimental import pallas as pl
from jax.experimental.pallas import tpu as pltpu
from jax.sharding import PartitionSpec as P

SWEEPS = 2
GROUP = 30


def shift_lat(edge, down):
    count = lax.axis_size("lat")
    if down:
        pairs = [(i, i + 1) for i in range(count - 1)]
    else:
        pairs = [(i + 1, i) for i in range(count - 1)]
    return lax.ppermute(edge, "lat", pairs)


def shift_lon(edge, east):
    count = lax.axis_size("lon")
    if east:
        pairs = [(i, (i + 1) % count) for i in range(count)]
    else:
        pairs = [((i + 1) % count, i) for i in range(count)]
    return lax.ppermute(edge, "lon", pairs)


def halos(top, bottom, left, right):
    return (
        shift_lat(bottom, True),
        shift_lat(top, False),
        shift_lon(right, True),
        shift_lon(left, False),
    )


def sweep_kernel(rows, v_ref, c_ref, vn_ref, vs_ref, vw_ref, ve_ref, cn_ref, cs_ref, cw_ref, ce_ref,
                 w_ref, top_ref, bot_ref, left_ref, right_ref):
    group = vn_ref.shape[1]
    lanes = v_ref.shape[2]
    lane = lax.broadcasted_iota(jnp.int32, (group, lanes), 1)
    col = lax.broadcasted_iota(jnp.int32, (group, rows), 1)

    def slab(ref, r):
        return ref[0, pl.ds(r, group, stride=rows), :]

    vw = vw_ref[0]
    ve = ve_ref[0]
    cw = cw_ref[0]
    ce = ce_ref[0]
    left = jnp.zeros((group, rows), jnp.float32)
    right = jnp.zeros((group, rows), jnp.float32)
    x_up, c_up = vn_ref[0], cn_ref[0]
    x_mid, c_mid = slab(v_ref, 0), slab(c_ref, 0)
    for r in range(rows):
        if r + 1 < rows:
            x_dn, c_dn = slab(v_ref, r + 1), slab(c_ref, r + 1)
        else:
            x_dn, c_dn = vs_ref[0], cs_ref[0]
        x_w = jnp.where(lane == 0, vw[:, r : r + 1], pltpu.roll(x_mid, 1, 1))
        x_e = jnp.where(lane == lanes - 1, ve[:, r : r + 1], pltpu.roll(x_mid, lanes - 1, 1))
        c_w = jnp.where(lane == 0, cw[:, r : r + 1], pltpu.roll(c_mid, 1, 1))
        c_e = jnp.where(lane == lanes - 1, ce[:, r : r + 1], pltpu.roll(c_mid, lanes - 1, 1))
        total = jnp.minimum(c_mid, c_up) * (x_up - x_mid)
        total = total + jnp.minimum(c_mid, c_dn) * (x_dn - x_mid)
        total = total + jnp.minimum(c_mid, c_w) * (x_w - x_mid)
        total = total + jnp.minimum(c_mid, c_e) * (x_e - x_mid)
        out = x_mid + total
        w_ref[0, pl.ds(r, group, stride=rows), :] = out
        if r == 0:
            top_ref[0] = out
        if r == rows - 1:
            bot_ref[0] = out
        left = jnp.where(col == r, out[:, 0:1], left)
        right = jnp.where(col == r, out[:, lanes - 1 : lanes], right)
        x_up, c_up = x_mid, c_mid
        x_mid, c_mid = x_dn, c_dn
    left_ref[0] = left
    right_ref[0] = right


def sweep(field, conduct, field_halos, coef_halos):
    steps, span, lanes = field.shape
    rows = span // GROUP
    big = pl.BlockSpec((1, span, lanes), lambda i: (i, 0, 0))
    row_edge = pl.BlockSpec((1, GROUP, lanes), lambda i: (i, 0, 0))
    col_edge = pl.BlockSpec((1, GROUP, rows), lambda i: (i, 0, 0))
    edge_specs = [row_edge, row_edge, col_edge, col_edge]
    return pl.pallas_call(
        functools.partial(sweep_kernel, rows),
        grid=(steps,),
        in_specs=[big, big] + edge_specs + edge_specs,
        out_specs=[big] + edge_specs,
        out_shape=[
            jax.ShapeDtypeStruct(field.shape, jnp.float32),
            jax.ShapeDtypeStruct((steps, GROUP, lanes), jnp.float32),
            jax.ShapeDtypeStruct((steps, GROUP, lanes), jnp.float32),
            jax.ShapeDtypeStruct((steps, GROUP, rows), jnp.float32),
            jax.ShapeDtypeStruct((steps, GROUP, rows), jnp.float32),
        ],
        cost_estimate=pl.CostEstimate(
            flops=20 * field.size, bytes_accessed=12 * field.size, transcendentals=0
        ),
    )(field, conduct, *field_halos, *coef_halos)


def edges_of(field):
    vals, rows, lanes = field.shape
    steps = vals // GROUP
    top = field[:, 0, :].reshape(steps, GROUP, lanes)
    bottom = field[:, rows - 1, :].reshape(steps, GROUP, lanes)
    left = field[:, :, 0].reshape(steps, GROUP, rows)
    right = field[:, :, lanes - 1].reshape(steps, GROUP, rows)
    return top, bottom, left, right


def diffuse(field, conduct_blocks, coef_halos):
    vals, rows, lanes = field.shape
    steps = vals // GROUP
    edges = edges_of(field)
    current = field.reshape(steps, GROUP * rows, lanes)
    for _ in range(SWEEPS):
        current, *edges = sweep(current, conduct_blocks, halos(*edges), coef_halos)
    return current.reshape(vals, rows, lanes)


def to_owners(outgoing):
    return lax.all_to_all(outgoing, ("lon", "lat"), split_axis=0, concat_axis=0, tiled=True)


def to_sources(returned):
    return lax.all_to_all(returned, ("lon", "lat"), split_axis=0, concat_axis=0, tiled=True)


def on_device(state, diffusivity, sea_mask, send_cols, obs_slots, obs_weights, obs_precision):
    vals, rows, lanes = state.shape
    cell_count = rows * lanes
    steps = vals // GROUP
    sea_float = sea_mask.astype(jnp.float32)
    conduct = diffusivity * jnp.concatenate([sea_float, sea_float], axis=0)
    coef_halos = halos(*edges_of(conduct))
    conduct_blocks = conduct.reshape(steps, GROUP * rows, lanes)
    smooth = diffuse(state, conduct_blocks, coef_halos)
    rows_of = smooth.reshape(vals, cell_count).T
    send_index = send_cols[0]
    outgoing = jnp.take(rows_of, send_index, axis=0, mode="fill", fill_value=0.0)
    received = to_owners(outgoing)
    slot_count = outgoing.shape[0]
    taps, obs_count = obs_slots.shape
    all_slots = obs_slots.reshape(taps * obs_count)
    picked = jnp.take(received, all_slots, axis=0, mode="clip").reshape(taps, obs_count, vals)
    equivalent_rows = jnp.sum(picked * obs_weights[:, :, None], axis=0)
    equivalents = equivalent_rows.T
    weighted_rows = obs_precision.T * equivalent_rows
    spread = (weighted_rows[None, :, :] * obs_weights[:, :, None]).reshape(taps * obs_count, vals)
    returned = jnp.zeros((slot_count, vals), jnp.float32).at[all_slots].add(spread, mode="drop")
    incoming = to_sources(returned)
    adjoint_rows = jnp.zeros((cell_count, vals), jnp.float32).at[send_index].add(incoming, mode="drop")
    adjoint_field = adjoint_rows.T.reshape(state.shape)
    product = state + diffuse(adjoint_field, conduct_blocks, coef_halos)
    return (product, equivalents)


def solution(mesh):
    placed = (
        P(None, "lat", "lon"),
        P(None, "lat", "lon"),
        P(None, "lat", "lon"),
        P(("lon", "lat"), None),
        P(None, ("lon", "lat")),
        P(None, ("lon", "lat")),
        P(None, ("lon", "lat")),
    )
    return jax.shard_map(
        on_device,
        mesh=mesh,
        in_specs=placed,
        out_specs=(P(None, "lat", "lon"), P(None, ("lon", "lat"))),
        check_vma=False,
    )
```

```python
import functools

import jax
import jax.numpy as jnp
from jax import lax
from jax.experimental import pallas as pl
from jax.experimental.pallas import tpu as pltpu
from jax.sharding import PartitionSpec as P

SWEEPS = 2
GROUP = 30


def shift_lat(edge, down):
    count = lax.axis_size("lat")
    if down:
        pairs = [(i, i + 1) for i in range(count - 1)]
    else:
        pairs = [(i + 1, i) for i in range(count - 1)]
    return lax.ppermute(edge, "lat", pairs)


def shift_lon(edge, east):
    count = lax.axis_size("lon")
    if east:
        pairs = [(i, (i + 1) % count) for i in range(count)]
    else:
        pairs = [((i + 1) % count, i) for i in range(count)]
    return lax.ppermute(edge, "lon", pairs)


def halos(top, bottom, left, right):
    return (
        shift_lat(bottom, True),
        shift_lat(top, False),
        shift_lon(right, True),
        shift_lon(left, False),
    )


def sweep_kernel(rows, v_ref, c_ref, vn_ref, vs_ref, vw_ref, ve_ref, cn_ref, cs_ref, cw_ref, ce_ref,
                 w_ref, top_ref, bot_ref, left_ref, right_ref):
    group = vn_ref.shape[1]
    lanes = v_ref.shape[2]
    lane = lax.broadcasted_iota(jnp.int32, (group, lanes), 1)
    col = lax.broadcasted_iota(jnp.int32, (group, rows), 1)

    def slab(ref, r):
        return ref[0, pl.ds(r, group, stride=rows), :]

    vw = vw_ref[0]
    ve = ve_ref[0]
    cw = cw_ref[0]
    ce = ce_ref[0]
    left = jnp.zeros((group, rows), jnp.float32)
    right = jnp.zeros((group, rows), jnp.float32)
    x_up, c_up = vn_ref[0], cn_ref[0]
    x_mid, c_mid = slab(v_ref, 0), slab(c_ref, 0)
    for r in range(rows):
        if r + 1 < rows:
            x_dn, c_dn = slab(v_ref, r + 1), slab(c_ref, r + 1)
        else:
            x_dn, c_dn = vs_ref[0], cs_ref[0]
        x_w = jnp.where(lane == 0, vw[:, r : r + 1], pltpu.roll(x_mid, 1, 1))
        x_e = jnp.where(lane == lanes - 1, ve[:, r : r + 1], pltpu.roll(x_mid, lanes - 1, 1))
        c_w = jnp.where(lane == 0, cw[:, r : r + 1], pltpu.roll(c_mid, 1, 1))
        c_e = jnp.where(lane == lanes - 1, ce[:, r : r + 1], pltpu.roll(c_mid, lanes - 1, 1))
        total = jnp.minimum(c_mid, c_up) * (x_up - x_mid)
        total = total + jnp.minimum(c_mid, c_dn) * (x_dn - x_mid)
        total = total + jnp.minimum(c_mid, c_w) * (x_w - x_mid)
        total = total + jnp.minimum(c_mid, c_e) * (x_e - x_mid)
        out = x_mid + total
        w_ref[0, pl.ds(r, group, stride=rows), :] = out
        if r == 0:
            top_ref[0] = out
        if r == rows - 1:
            bot_ref[0] = out
        left = jnp.where(col == r, out[:, 0:1], left)
        right = jnp.where(col == r, out[:, lanes - 1 : lanes], right)
        x_up, c_up = x_mid, c_mid
        x_mid, c_mid = x_dn, c_dn
    left_ref[0] = left
    right_ref[0] = right


def sweep(field, conduct, field_halos, coef_halos):
    steps, span, lanes = field.shape
    rows = span // GROUP
    big = pl.BlockSpec((1, span, lanes), lambda i: (i, 0, 0))
    row_edge = pl.BlockSpec((1, GROUP, lanes), lambda i: (i, 0, 0))
    col_edge = pl.BlockSpec((1, GROUP, rows), lambda i: (i, 0, 0))
    edge_specs = [row_edge, row_edge, col_edge, col_edge]
    return pl.pallas_call(
        functools.partial(sweep_kernel, rows),
        grid=(steps,),
        in_specs=[big, big] + edge_specs + edge_specs,
        out_specs=[big] + edge_specs,
        out_shape=[
            jax.ShapeDtypeStruct(field.shape, jnp.float32),
            jax.ShapeDtypeStruct((steps, GROUP, lanes), jnp.float32),
            jax.ShapeDtypeStruct((steps, GROUP, lanes), jnp.float32),
            jax.ShapeDtypeStruct((steps, GROUP, rows), jnp.float32),
            jax.ShapeDtypeStruct((steps, GROUP, rows), jnp.float32),
        ],
        cost_estimate=pl.CostEstimate(
            flops=20 * field.size, bytes_accessed=12 * field.size, transcendentals=0
        ),
    )(field, conduct, *field_halos, *coef_halos)


def edges_of(field):
    vals, rows, lanes = field.shape
    steps = vals // GROUP
    top = field[:, 0, :].reshape(steps, GROUP, lanes)
    bottom = field[:, rows - 1, :].reshape(steps, GROUP, lanes)
    left = field[:, :, 0].reshape(steps, GROUP, rows)
    right = field[:, :, lanes - 1].reshape(steps, GROUP, rows)
    return top, bottom, left, right


def diffuse(field, conduct_blocks, coef_halos):
    vals, rows, lanes = field.shape
    steps = vals // GROUP
    edges = edges_of(field)
    current = field.reshape(steps, GROUP * rows, lanes)
    for _ in range(SWEEPS):
        current, *edges = sweep(current, conduct_blocks, halos(*edges), coef_halos)
    return current.reshape(vals, rows, lanes)


def select_kernel(index_ref, rows_ref, out_ref):
    cells = rows_ref.shape[0]

    def body(q, carry):
        source = index_ref[q]
        row = rows_ref[pl.ds(jnp.minimum(source, cells - 1), 1), :]
        out_ref[pl.ds(q, 1), :] = jnp.where(source < cells, row, 0.0)
        return carry

    lax.fori_loop(0, out_ref.shape[0], body, 0, unroll=8)


def place_kernel(index_ref, rows_ref, out_ref):
    cells = out_ref.shape[0]
    out_ref[...] = jnp.zeros_like(out_ref)

    def body(q, carry):
        target = index_ref[q]
        spot = pl.ds(jnp.minimum(target, cells - 1), 1)
        row = rows_ref[pl.ds(q, 1), :]
        out_ref[spot, :] = out_ref[spot, :] + jnp.where(target < cells, row, 0.0)
        return carry

    lax.fori_loop(0, rows_ref.shape[0], body, 0, unroll=8)


def interp_kernel(slot_ref, weight_ref, received_ref, precision_ref, equiv_ref, returned_ref):
    taps, obs_count = slot_ref.shape
    returned_ref[...] = jnp.zeros_like(returned_ref)

    def body(j, carry):
        slots = [slot_ref[k, j] for k in range(taps)]
        weights = [weight_ref[k, j] for k in range(taps)]
        total = received_ref[pl.ds(slots[0], 1), :] * weights[0]
        for k in range(1, taps):
            total = total + received_ref[pl.ds(slots[k], 1), :] * weights[k]
        equiv_ref[pl.ds(j, 1), :] = total
        weighted = precision_ref[pl.ds(j, 1), :] * total
        for k in range(taps):
            spot = pl.ds(slots[k], 1)
            returned_ref[spot, :] = returned_ref[spot, :] + weighted * weights[k]
        return carry

    lax.fori_loop(0, obs_count, body, 0, unroll=4)


SMEM = pl.BlockSpec(memory_space=pltpu.SMEM)
VMEM = pl.BlockSpec(memory_space=pltpu.VMEM)


def select_rows(index, rows, count):
    return pl.pallas_call(
        select_kernel,
        in_specs=[SMEM, VMEM],
        out_specs=VMEM,
        out_shape=jax.ShapeDtypeStruct((count, rows.shape[1]), jnp.float32),
    )(index, rows)


def place_rows(index, rows, cells):
    return pl.pallas_call(
        place_kernel,
        in_specs=[SMEM, VMEM],
        out_specs=VMEM,
        out_shape=jax.ShapeDtypeStruct((cells, rows.shape[1]), jnp.float32),
    )(index, rows)


def interpolate(obs_slots, obs_weights, received, precision_rows):
    obs_count = obs_slots.shape[1]
    return pl.pallas_call(
        interp_kernel,
        in_specs=[SMEM, SMEM, VMEM, VMEM],
        out_specs=[VMEM, VMEM],
        out_shape=[
            jax.ShapeDtypeStruct((obs_count, received.shape[1]), jnp.float32),
            jax.ShapeDtypeStruct(received.shape, jnp.float32),
        ],
    )(obs_slots, obs_weights, received, precision_rows)


def to_owners(outgoing):
    return lax.all_to_all(outgoing, ("lon", "lat"), split_axis=0, concat_axis=0, tiled=True)


def to_sources(returned):
    return lax.all_to_all(returned, ("lon", "lat"), split_axis=0, concat_axis=0, tiled=True)


def on_device(state, diffusivity, sea_mask, send_cols, obs_slots, obs_weights, obs_precision):
    vals, rows, lanes = state.shape
    cell_count = rows * lanes
    steps = vals // GROUP
    sea_float = sea_mask.astype(jnp.float32)
    conduct = diffusivity * jnp.concatenate([sea_float, sea_float], axis=0)
    coef_halos = halos(*edges_of(conduct))
    conduct_blocks = conduct.reshape(steps, GROUP * rows, lanes)
    smooth = diffuse(state, conduct_blocks, coef_halos)
    rows_of = smooth.reshape(vals, cell_count).T
    send_index = send_cols[0]
    outgoing = select_rows(send_index, rows_of, send_index.shape[0])
    received = to_owners(outgoing)
    equivalent_rows, returned = interpolate(obs_slots, obs_weights, received, obs_precision.T)
    equivalents = equivalent_rows.T
    incoming = to_sources(returned)
    adjoint_rows = place_rows(send_index, incoming, cell_count)
    adjoint_field = adjoint_rows.T.reshape(state.shape)
    product = state + diffuse(adjoint_field, conduct_blocks, coef_halos)
    return (product, equivalents)


def solution(mesh):
    placed = (
        P(None, "lat", "lon"),
        P(None, "lat", "lon"),
        P(None, "lat", "lon"),
        P(("lon", "lat"), None),
        P(None, ("lon", "lat")),
        P(None, ("lon", "lat")),
        P(None, ("lon", "lat")),
    )
    return jax.shard_map(
        on_device,
        mesh=mesh,
        in_specs=placed,
        out_specs=(P(None, "lat", "lon"), P(None, ("lon", "lat"))),
        check_vma=False,
    )
```

```python
import functools

import jax
import jax.numpy as jnp
from jax import lax
from jax.experimental import pallas as pl
from jax.experimental.pallas import tpu as pltpu
from jax.sharding import PartitionSpec as P

SWEEPS = 2
GROUP = 30
SMEM = pl.BlockSpec(memory_space=pltpu.SMEM)
VMEM = pl.BlockSpec(memory_space=pltpu.VMEM)


def slab_pass(rows, src_ref, conduct_ref, field_halo, coef_halo, scales, dst_ref, edges):
    groups, span, lanes = src_ref.shape
    group = span // rows
    north_ok, south_ok = scales
    row_halo, col_halo = field_halo
    coef_rows, coef_cols = coef_halo

    def body(g, carry):
        lane = lax.broadcasted_iota(jnp.int32, (group, lanes), 1)
        col = lax.broadcasted_iota(jnp.int32, (group, rows), 1)

        def slab(ref, r):
            return ref[g, pl.ds(r, group, stride=rows), :]

        vw = col_halo[0, g]
        ve = col_halo[1, g]
        cw = coef_cols[0, g]
        ce = coef_cols[1, g]
        left = jnp.zeros((group, rows), jnp.float32)
        right = jnp.zeros((group, rows), jnp.float32)
        x_up = row_halo[0, g] * north_ok
        c_up = coef_rows[0, g] * north_ok
        x_mid, c_mid = slab(src_ref, 0), slab(conduct_ref, 0)
        for r in range(rows):
            if r + 1 < rows:
                x_dn, c_dn = slab(src_ref, r + 1), slab(conduct_ref, r + 1)
            else:
                x_dn = row_halo[1, g] * south_ok
                c_dn = coef_rows[1, g] * south_ok
            x_w = jnp.where(lane == 0, vw[:, r : r + 1], pltpu.roll(x_mid, 1, 1))
            x_e = jnp.where(lane == lanes - 1, ve[:, r : r + 1], pltpu.roll(x_mid, lanes - 1, 1))
            c_w = jnp.where(lane == 0, cw[:, r : r + 1], pltpu.roll(c_mid, 1, 1))
            c_e = jnp.where(lane == lanes - 1, ce[:, r : r + 1], pltpu.roll(c_mid, lanes - 1, 1))
            total = jnp.minimum(c_mid, c_up) * (x_up - x_mid)
            total = total + jnp.minimum(c_mid, c_dn) * (x_dn - x_mid)
            total = total + jnp.minimum(c_mid, c_w) * (x_w - x_mid)
            total = total + jnp.minimum(c_mid, c_e) * (x_e - x_mid)
            out = x_mid + total
            dst_ref[g, pl.ds(r, group, stride=rows), :] = out
            if edges is not None:
                if r == 0:
                    edges[0][0, g] = out
                if r == rows - 1:
                    edges[0][1, g] = out
                left = jnp.where(col == r, out[:, 0:1], left)
                right = jnp.where(col == r, out[:, lanes - 1 : lanes], right)
            x_up, c_up = x_mid, c_mid
            x_mid, c_mid = x_dn, c_dn
        if edges is not None:
            edges[1][0, g] = left
            edges[1][1, g] = right
        return carry

    lax.fori_loop(0, groups, body, 0)


def edge_pass(rows, src_ref, row_out, col_out):
    groups, span, lanes = src_ref.shape
    group = span // rows

    def body(g, carry):
        col = lax.broadcasted_iota(jnp.int32, (group, rows), 1)
        left = jnp.zeros((group, rows), jnp.float32)
        right = jnp.zeros((group, rows), jnp.float32)
        for r in range(rows):
            x = src_ref[g, pl.ds(r, group, stride=rows), :]
            if r == 0:
                row_out[0, g] = x
            if r == rows - 1:
                row_out[1, g] = x
            left = jnp.where(col == r, x[:, 0:1], left)
            right = jnp.where(col == r, x[:, lanes - 1 : lanes], right)
        col_out[0, g] = left
        col_out[1, g] = right
        return carry

    lax.fori_loop(0, groups, body, 0)


def diffuse_kernel(rows, v_ref, c_ref, out_ref, mid_ref, row_edge, col_edge, row_halo, col_halo,
                   send_sem, recv_sem):
    lon = lax.axis_index("lon")
    lat = lax.axis_index("lat")
    n_lon = lax.axis_size("lon")
    n_lat = lax.axis_size("lat")
    north = {"lat": (lat + n_lat - 1) % n_lat}
    south = {"lat": (lat + 1) % n_lat}
    west = {"lon": (lon + n_lon - 1) % n_lon}
    east = {"lon": (lon + 1) % n_lon}
    mesh_id = pl.DeviceIdType.MESH

    barrier = pltpu.get_barrier_semaphore()
    for peer in (north, south, west, east):
        pl.semaphore_signal(barrier, inc=1, device_id=peer, device_id_type=mesh_id)
    pl.semaphore_wait(barrier, 4)

    def exchange(rd):
        plan = [
            (row_edge.at[rd, 0], row_halo.at[rd, 1], north, 0),
            (row_edge.at[rd, 1], row_halo.at[rd, 0], south, 1),
            (col_edge.at[rd, 0], col_halo.at[rd, 1], west, 2),
            (col_edge.at[rd, 1], col_halo.at[rd, 0], east, 3),
        ]
        copies = []
        for src, dst, peer, k in plan:
            copy = pltpu.make_async_remote_copy(
                src_ref=src, dst_ref=dst, send_sem=send_sem.at[rd, k], recv_sem=recv_sem.at[rd, k],
                device_id=peer, device_id_type=mesh_id,
            )
            copy.start()
            copies.append(copy)
        return copies

    edge_pass(rows, c_ref, row_edge.at[0], col_edge.at[0])
    edge_pass(rows, v_ref, row_edge.at[1], col_edge.at[1])
    first = exchange(0) + exchange(1)
    for copy in first:
        copy.wait()
    north_ok = jnp.minimum(lat, 1).astype(jnp.float32)
    south_ok = jnp.minimum(n_lat - 1 - lat, 1).astype(jnp.float32)
    scales = (north_ok, south_ok)
    coef_halo = (row_halo.at[0], col_halo.at[0])
    slab_pass(rows, v_ref, c_ref, (row_halo.at[1], col_halo.at[1]), coef_halo, scales, mid_ref,
              (row_edge.at[2], col_edge.at[2]))
    for copy in exchange(2):
        copy.wait()
    slab_pass(rows, mid_ref, c_ref, (row_halo.at[2], col_halo.at[2]), coef_halo, scales, out_ref, None)


def diffuse(field, conduct_blocks):
    vals, rows, lanes = field.shape
    groups = vals // GROUP
    blocks = field.reshape(groups, GROUP * rows, lanes)
    rounds = SWEEPS + 1
    out = pl.pallas_call(
        functools.partial(diffuse_kernel, rows),
        in_specs=[VMEM, VMEM],
        out_specs=VMEM,
        out_shape=jax.ShapeDtypeStruct(blocks.shape, jnp.float32),
        scratch_shapes=[
            pltpu.VMEM(blocks.shape, jnp.float32),
            pltpu.VMEM((rounds, 2, groups, GROUP, lanes), jnp.float32),
            pltpu.VMEM((rounds, 2, groups, GROUP, rows), jnp.float32),
            pltpu.VMEM((rounds, 2, groups, GROUP, lanes), jnp.float32),
            pltpu.VMEM((rounds, 2, groups, GROUP, rows), jnp.float32),
            pltpu.SemaphoreType.DMA((rounds, 4)),
            pltpu.SemaphoreType.DMA((rounds, 4)),
        ],
        compiler_params=pltpu.CompilerParams(collective_id=0, has_side_effects=True),
        cost_estimate=pl.CostEstimate(
            flops=50 * field.size, bytes_accessed=12 * field.size, transcendentals=0
        ),
    )(blocks, conduct_blocks)
    return out.reshape(vals, rows, lanes)


def select_kernel(index_ref, rows_ref, out_ref):
    cells = rows_ref.shape[0]

    def body(q, carry):
        source = index_ref[q]
        row = rows_ref[pl.ds(jnp.minimum(source, cells - 1), 1), :]
        out_ref[pl.ds(q, 1), :] = jnp.where(source < cells, row, 0.0)
        return carry

    lax.fori_loop(0, out_ref.shape[0], body, 0, unroll=8)


def place_kernel(index_ref, rows_ref, out_ref):
    cells = out_ref.shape[0]
    out_ref[...] = jnp.zeros_like(out_ref)

    def body(q, carry):
        target = index_ref[q]
        spot = pl.ds(jnp.minimum(target, cells - 1), 1)
        row = rows_ref[pl.ds(q, 1), :]
        out_ref[spot, :] = out_ref[spot, :] + jnp.where(target < cells, row, 0.0)
        return carry

    lax.fori_loop(0, rows_ref.shape[0], body, 0, unroll=8)


def interp_kernel(slot_ref, weight_ref, received_ref, precision_ref, equiv_ref, returned_ref):
    taps, obs_count = slot_ref.shape
    returned_ref[...] = jnp.zeros_like(returned_ref)

    def body(j, carry):
        slots = [slot_ref[k, j] for k in range(taps)]
        weights = [weight_ref[k, j] for k in range(taps)]
        total = received_ref[pl.ds(slots[0], 1), :] * weights[0]
        for k in range(1, taps):
            total = total + received_ref[pl.ds(slots[k], 1), :] * weights[k]
        equiv_ref[pl.ds(j, 1), :] = total
        weighted = precision_ref[pl.ds(j, 1), :] * total
        for k in range(taps):
            spot = pl.ds(slots[k], 1)
            returned_ref[spot, :] = returned_ref[spot, :] + weighted * weights[k]
        return carry

    lax.fori_loop(0, obs_count, body, 0, unroll=4)


def select_rows(index, rows, count):
    return pl.pallas_call(
        select_kernel,
        in_specs=[SMEM, VMEM],
        out_specs=VMEM,
        out_shape=jax.ShapeDtypeStruct((count, rows.shape[1]), jnp.float32),
    )(index, rows)


def place_rows(index, rows, cells):
    return pl.pallas_call(
        place_kernel,
        in_specs=[SMEM, VMEM],
        out_specs=VMEM,
        out_shape=jax.ShapeDtypeStruct((cells, rows.shape[1]), jnp.float32),
    )(index, rows)


def interpolate(obs_slots, obs_weights, received, precision_rows):
    obs_count = obs_slots.shape[1]
    return pl.pallas_call(
        interp_kernel,
        in_specs=[SMEM, SMEM, VMEM, VMEM],
        out_specs=[VMEM, VMEM],
        out_shape=[
            jax.ShapeDtypeStruct((obs_count, received.shape[1]), jnp.float32),
            jax.ShapeDtypeStruct(received.shape, jnp.float32),
        ],
    )(obs_slots, obs_weights, received, precision_rows)


def to_owners(outgoing):
    return lax.all_to_all(outgoing, ("lon", "lat"), split_axis=0, concat_axis=0, tiled=True)


def to_sources(returned):
    return lax.all_to_all(returned, ("lon", "lat"), split_axis=0, concat_axis=0, tiled=True)


def on_device(state, diffusivity, sea_mask, send_cols, obs_slots, obs_weights, obs_precision):
    vals, rows, lanes = state.shape
    cell_count = rows * lanes
    steps = vals // GROUP
    sea_float = sea_mask.astype(jnp.float32)
    conduct = diffusivity * jnp.concatenate([sea_float, sea_float], axis=0)
    conduct_blocks = conduct.reshape(steps, GROUP * rows, lanes)
    smooth = diffuse(state, conduct_blocks)
    rows_of = smooth.reshape(vals, cell_count).T
    send_index = send_cols[0]
    outgoing = select_rows(send_index, rows_of, send_index.shape[0])
    received = to_owners(outgoing)
    equivalent_rows, returned = interpolate(obs_slots, obs_weights, received, obs_precision.T)
    equivalents = equivalent_rows.T
    incoming = to_sources(returned)
    adjoint_rows = place_rows(send_index, incoming, cell_count)
    adjoint_field = adjoint_rows.T.reshape(state.shape)
    product = state + diffuse(adjoint_field, conduct_blocks)
    return (product, equivalents)


def solution(mesh):
    placed = (
        P(None, "lat", "lon"),
        P(None, "lat", "lon"),
        P(None, "lat", "lon"),
        P(("lon", "lat"), None),
        P(None, ("lon", "lat")),
        P(None, ("lon", "lat")),
        P(None, ("lon", "lat")),
    )
    return jax.shard_map(
        on_device,
        mesh=mesh,
        in_specs=placed,
        out_specs=(P(None, "lat", "lon"), P(None, ("lon", "lat"))),
        check_vma=False,
    )
```

```python
import functools

import jax
import jax.numpy as jnp
from jax import lax
from jax.experimental import pallas as pl
from jax.experimental.pallas import tpu as pltpu
from jax.sharding import PartitionSpec as P

SWEEPS = 2
GROUP = 30
SMEM = pl.BlockSpec(memory_space=pltpu.SMEM)
VMEM = pl.BlockSpec(memory_space=pltpu.VMEM)


def slab_pass(rows, src_ref, conduct_ref, field_halo, coef_halo, scales, dst_ref, edges):
    groups, span, lanes = src_ref.shape
    group = span // rows
    north_ok, south_ok = scales
    row_halo, col_halo = field_halo
    coef_rows, coef_cols = coef_halo

    def body(g, carry):
        lane = lax.broadcasted_iota(jnp.int32, (group, lanes), 1)
        col = lax.broadcasted_iota(jnp.int32, (group, rows), 1)

        def slab(ref, r):
            return ref[g, pl.ds(r, group, stride=rows), :]

        vw = col_halo[0, g]
        ve = col_halo[1, g]
        cw = coef_cols[0, g]
        ce = coef_cols[1, g]
        left = jnp.zeros((group, rows), jnp.float32)
        right = jnp.zeros((group, rows), jnp.float32)
        x_up = row_halo[0, g] * north_ok
        c_up = coef_rows[0, g] * north_ok
        x_mid, c_mid = slab(src_ref, 0), slab(conduct_ref, 0)
        for r in range(rows):
            if r + 1 < rows:
                x_dn, c_dn = slab(src_ref, r + 1), slab(conduct_ref, r + 1)
            else:
                x_dn = row_halo[1, g] * south_ok
                c_dn = coef_rows[1, g] * south_ok
            x_w = jnp.where(lane == 0, vw[:, r : r + 1], pltpu.roll(x_mid, 1, 1))
            x_e = jnp.where(lane == lanes - 1, ve[:, r : r + 1], pltpu.roll(x_mid, lanes - 1, 1))
            c_w = jnp.where(lane == 0, cw[:, r : r + 1], pltpu.roll(c_mid, 1, 1))
            c_e = jnp.where(lane == lanes - 1, ce[:, r : r + 1], pltpu.roll(c_mid, lanes - 1, 1))
            total = jnp.minimum(c_mid, c_up) * (x_up - x_mid)
            total = total + jnp.minimum(c_mid, c_dn) * (x_dn - x_mid)
            total = total + jnp.minimum(c_mid, c_w) * (x_w - x_mid)
            total = total + jnp.minimum(c_mid, c_e) * (x_e - x_mid)
            out = x_mid + total
            dst_ref[g, pl.ds(r, group, stride=rows), :] = out
            if edges is not None:
                if r == 0:
                    edges[0][0, g] = out
                if r == rows - 1:
                    edges[0][1, g] = out
                left = jnp.where(col == r, out[:, 0:1], left)
                right = jnp.where(col == r, out[:, lanes - 1 : lanes], right)
            x_up, c_up = x_mid, c_mid
            x_mid, c_mid = x_dn, c_dn
        if edges is not None:
            edges[1][0, g] = left
            edges[1][1, g] = right
        return carry

    lax.fori_loop(0, groups, body, 0)


def edge_pass(rows, src_ref, row_out, col_out):
    groups, span, lanes = src_ref.shape
    group = span // rows

    def body(g, carry):
        col = lax.broadcasted_iota(jnp.int32, (group, rows), 1)
        left = jnp.zeros((group, rows), jnp.float32)
        right = jnp.zeros((group, rows), jnp.float32)
        for r in range(rows):
            x = src_ref[g, pl.ds(r, group, stride=rows), :]
            if r == 0:
                row_out[0, g] = x
            if r == rows - 1:
                row_out[1, g] = x
            left = jnp.where(col == r, x[:, 0:1], left)
            right = jnp.where(col == r, x[:, lanes - 1 : lanes], right)
        col_out[0, g] = left
        col_out[1, g] = right
        return carry

    lax.fori_loop(0, groups, body, 0)


def diffuse_kernel(rows, v_ref, c_ref, out_ref, mid_ref, row_edge, col_edge, row_halo, col_halo,
                   send_sem, recv_sem):
    lon = lax.axis_index("lon")
    lat = lax.axis_index("lat")
    n_lon = lax.axis_size("lon")
    n_lat = lax.axis_size("lat")
    north = {"lat": (lat + n_lat - 1) % n_lat}
    south = {"lat": (lat + 1) % n_lat}
    west = {"lon": (lon + n_lon - 1) % n_lon}
    east = {"lon": (lon + 1) % n_lon}
    mesh_id = pl.DeviceIdType.MESH

    barrier = pltpu.get_barrier_semaphore()
    for peer in (north, south, west, east):
        pl.semaphore_signal(barrier, inc=1, device_id=peer, device_id_type=mesh_id)
    pl.semaphore_wait(barrier, 4)

    def exchange(rd):
        plan = [
            (row_edge.at[rd, 0], row_halo.at[rd, 1], north, 0),
            (row_edge.at[rd, 1], row_halo.at[rd, 0], south, 1),
            (col_edge.at[rd, 0], col_halo.at[rd, 1], west, 2),
            (col_edge.at[rd, 1], col_halo.at[rd, 0], east, 3),
        ]
        copies = []
        for src, dst, peer, k in plan:
            copy = pltpu.make_async_remote_copy(
                src_ref=src, dst_ref=dst, send_sem=send_sem.at[rd, k], recv_sem=recv_sem.at[rd, k],
                device_id=peer, device_id_type=mesh_id,
            )
            copy.start()
            copies.append(copy)
        return copies

    edge_pass(rows, c_ref, row_edge.at[0], col_edge.at[0])
    edge_pass(rows, v_ref, row_edge.at[1], col_edge.at[1])
    first = exchange(0) + exchange(1)
    for copy in first:
        copy.wait()
    north_ok = jnp.minimum(lat, 1).astype(jnp.float32)
    south_ok = jnp.minimum(n_lat - 1 - lat, 1).astype(jnp.float32)
    scales = (north_ok, south_ok)
    coef_halo = (row_halo.at[0], col_halo.at[0])
    slab_pass(rows, v_ref, c_ref, (row_halo.at[1], col_halo.at[1]), coef_halo, scales, mid_ref,
              (row_edge.at[2], col_edge.at[2]))
    for copy in exchange(2):
        copy.wait()
    slab_pass(rows, mid_ref, c_ref, (row_halo.at[2], col_halo.at[2]), coef_halo, scales, out_ref, None)


def diffuse(field, conduct_blocks):
    vals, rows, lanes = field.shape
    groups = vals // GROUP
    blocks = field.reshape(groups, GROUP * rows, lanes)
    rounds = SWEEPS + 1
    out = pl.pallas_call(
        functools.partial(diffuse_kernel, rows),
        in_specs=[VMEM, VMEM],
        out_specs=VMEM,
        out_shape=jax.ShapeDtypeStruct(blocks.shape, jnp.float32),
        scratch_shapes=[
            pltpu.VMEM(blocks.shape, jnp.float32),
            pltpu.VMEM((rounds, 2, groups, GROUP, lanes), jnp.float32),
            pltpu.VMEM((rounds, 2, groups, GROUP, rows), jnp.float32),
            pltpu.VMEM((rounds, 2, groups, GROUP, lanes), jnp.float32),
            pltpu.VMEM((rounds, 2, groups, GROUP, rows), jnp.float32),
            pltpu.SemaphoreType.DMA((rounds, 4)),
            pltpu.SemaphoreType.DMA((rounds, 4)),
        ],
        compiler_params=pltpu.CompilerParams(collective_id=0, has_side_effects=True),
        cost_estimate=pl.CostEstimate(
            flops=50 * field.size, bytes_accessed=12 * field.size, transcendentals=0
        ),
    )(blocks, conduct_blocks)
    return out.reshape(vals, rows, lanes)


def load_row(ref, index):
    return ref[pl.ds(index, 1), :]


def add_row(ref, index, value):
    spot = pl.ds(index, 1)
    ref[spot, :] = ref[spot, :] + value


def select_kernel(index_ref, rows_ref, out_ref):
    cells = rows_ref.shape[0]
    width = out_ref.shape[1]
    sub = lax.broadcasted_iota(jnp.int32, (8, width), 0)

    def body(t, carry):
        tile = jnp.zeros((8, width), jnp.float32)
        for i in range(8):
            source = index_ref[t * 8 + i]
            row = load_row(rows_ref, jnp.minimum(source, cells - 1))
            tile = jnp.where((sub == i) & (source < cells), jnp.broadcast_to(row, (8, width)), tile)
        out_ref[pl.ds(pl.multiple_of(t * 8, 8), 8), :] = tile
        return carry

    lax.fori_loop(0, out_ref.shape[0] // 8, body, 0, unroll=2)


def place_kernel(index_ref, rows_ref, out_ref, *parts):
    cells = out_ref.shape[0]
    for part in parts:
        part[...] = jnp.zeros_like(part)

    def body(t, carry):
        for i, part in enumerate(parts):
            q = t * len(parts) + i
            target = index_ref[q]
            row = load_row(rows_ref, q)
            add_row(part, jnp.minimum(target, cells - 1), jnp.where(target < cells, row, 0.0))
        return carry

    lax.fori_loop(0, rows_ref.shape[0] // len(parts), body, 0, unroll=2)
    total = parts[0][...]
    for part in parts[1:]:
        total = total + part[...]
    out_ref[...] = total


def interp_kernel(slot_ref, weight_ref, received_ref, precision_ref, equiv_ref, returned_ref, *parts):
    taps, obs_count = slot_ref.shape
    width = equiv_ref.shape[1]
    sub = lax.broadcasted_iota(jnp.int32, (8, width), 0)
    for part in parts:
        part[...] = jnp.zeros_like(part)

    def body(t, carry):
        tile = jnp.zeros((8, width), jnp.float32)
        for i in range(8):
            j = t * 8 + i
            slots = [slot_ref[k, j] for k in range(taps)]
            weights = [weight_ref[k, j] for k in range(taps)]
            total = load_row(received_ref, slots[0]) * weights[0]
            for k in range(1, taps):
                total = total + load_row(received_ref, slots[k]) * weights[k]
            tile = jnp.where(sub == i, jnp.broadcast_to(total, (8, width)), tile)
            weighted = load_row(precision_ref, j) * total
            for k in range(taps):
                add_row(parts[(i % 2) * taps + k], slots[k], weighted * weights[k])
        equiv_ref[pl.ds(pl.multiple_of(t * 8, 8), 8), :] = tile
        return carry

    lax.fori_loop(0, obs_count // 8, body, 0)
    total = parts[0][...]
    for part in parts[1:]:
        total = total + part[...]
    returned_ref[...] = total


def select_rows(index, rows, count):
    return pl.pallas_call(
        select_kernel,
        in_specs=[SMEM, VMEM],
        out_specs=VMEM,
        out_shape=jax.ShapeDtypeStruct((count, rows.shape[1]), jnp.float32),
    )(index, rows)


def place_rows(index, rows, cells):
    return pl.pallas_call(
        place_kernel,
        in_specs=[SMEM, VMEM],
        out_specs=VMEM,
        out_shape=jax.ShapeDtypeStruct((cells, rows.shape[1]), jnp.float32),
        scratch_shapes=[pltpu.VMEM((cells, rows.shape[1]), jnp.float32) for _ in range(4)],
        compiler_params=pltpu.CompilerParams(vmem_limit_bytes=60 * 1024 * 1024),
    )(index, rows)


def interpolate(obs_slots, obs_weights, received, precision_rows):
    obs_count = obs_slots.shape[1]
    return pl.pallas_call(
        interp_kernel,
        in_specs=[SMEM, SMEM, VMEM, VMEM],
        out_specs=[VMEM, VMEM],
        out_shape=[
            jax.ShapeDtypeStruct((obs_count, received.shape[1]), jnp.float32),
            jax.ShapeDtypeStruct(received.shape, jnp.float32),
        ],
        scratch_shapes=[
            pltpu.VMEM(received.shape, jnp.float32) for _ in range(2 * obs_slots.shape[0])
        ],
        compiler_params=pltpu.CompilerParams(vmem_limit_bytes=60 * 1024 * 1024),
    )(obs_slots, obs_weights, received, precision_rows)


def to_owners(outgoing):
    return lax.all_to_all(outgoing, ("lon", "lat"), split_axis=0, concat_axis=0, tiled=True)


def to_sources(returned):
    return lax.all_to_all(returned, ("lon", "lat"), split_axis=0, concat_axis=0, tiled=True)


def on_device(state, diffusivity, sea_mask, send_cols, obs_slots, obs_weights, obs_precision):
    vals, rows, lanes = state.shape
    cell_count = rows * lanes
    steps = vals // GROUP
    sea_float = sea_mask.astype(jnp.float32)
    conduct = diffusivity * jnp.concatenate([sea_float, sea_float], axis=0)
    conduct_blocks = conduct.reshape(steps, GROUP * rows, lanes)
    smooth = diffuse(state, conduct_blocks)
    rows_of = smooth.reshape(vals, cell_count).T
    send_index = send_cols[0]
    outgoing = select_rows(send_index, rows_of, send_index.shape[0])
    received = to_owners(outgoing)
    equivalent_rows, returned = interpolate(obs_slots, obs_weights, received, obs_precision.T)
    equivalents = equivalent_rows.T
    incoming = to_sources(returned)
    adjoint_rows = place_rows(send_index, incoming, cell_count)
    adjoint_field = adjoint_rows.T.reshape(state.shape)
    product = state + diffuse(adjoint_field, conduct_blocks)
    return (product, equivalents)


def solution(mesh):
    placed = (
        P(None, "lat", "lon"),
        P(None, "lat", "lon"),
        P(None, "lat", "lon"),
        P(("lon", "lat"), None),
        P(None, ("lon", "lat")),
        P(None, ("lon", "lat")),
        P(None, ("lon", "lat")),
    )
    return jax.shard_map(
        on_device,
        mesh=mesh,
        in_specs=placed,
        out_specs=(P(None, "lat", "lon"), P(None, ("lon", "lat"))),
        check_vma=False,
    )
```

```python
import functools

import jax
import jax.numpy as jnp
from jax import lax
from jax.experimental import pallas as pl
from jax.experimental.pallas import tpu as pltpu
from jax.sharding import PartitionSpec as P

SWEEPS = 2
GROUP = 30
SMEM = pl.BlockSpec(memory_space=pltpu.SMEM)
VMEM = pl.BlockSpec(memory_space=pltpu.VMEM)


def slab_pass(rows, src_ref, conduct_ref, field_halo, coef_halo, scales, dst_ref, edges):
    groups, span, lanes = src_ref.shape
    group = span // rows
    north_ok, south_ok = scales
    row_halo, col_halo = field_halo
    coef_rows, coef_cols = coef_halo

    def body(g, carry):
        lane = lax.broadcasted_iota(jnp.int32, (group, lanes), 1)
        col = lax.broadcasted_iota(jnp.int32, (group, rows), 1)

        def slab(ref, r):
            return ref[g, pl.ds(r, group, stride=rows), :]

        vw = col_halo[0, g]
        ve = col_halo[1, g]
        cw = coef_cols[0, g]
        ce = coef_cols[1, g]
        left = jnp.zeros((group, rows), jnp.float32)
        right = jnp.zeros((group, rows), jnp.float32)
        x_up = row_halo[0, g] * north_ok
        c_up = coef_rows[0, g] * north_ok
        x_mid, c_mid = slab(src_ref, 0), slab(conduct_ref, 0)
        for r in range(rows):
            if r + 1 < rows:
                x_dn, c_dn = slab(src_ref, r + 1), slab(conduct_ref, r + 1)
            else:
                x_dn = row_halo[1, g] * south_ok
                c_dn = coef_rows[1, g] * south_ok
            x_w = jnp.where(lane == 0, vw[:, r : r + 1], pltpu.roll(x_mid, 1, 1))
            x_e = jnp.where(lane == lanes - 1, ve[:, r : r + 1], pltpu.roll(x_mid, lanes - 1, 1))
            c_w = jnp.where(lane == 0, cw[:, r : r + 1], pltpu.roll(c_mid, 1, 1))
            c_e = jnp.where(lane == lanes - 1, ce[:, r : r + 1], pltpu.roll(c_mid, lanes - 1, 1))
            total = jnp.minimum(c_mid, c_up) * (x_up - x_mid)
            total = total + jnp.minimum(c_mid, c_dn) * (x_dn - x_mid)
            total = total + jnp.minimum(c_mid, c_w) * (x_w - x_mid)
            total = total + jnp.minimum(c_mid, c_e) * (x_e - x_mid)
            out = x_mid + total
            dst_ref[g, pl.ds(r, group, stride=rows), :] = out
            if edges is not None:
                if r == 0:
                    edges[0][0, g] = out
                if r == rows - 1:
                    edges[0][1, g] = out
                left = jnp.where(col == r, out[:, 0:1], left)
                right = jnp.where(col == r, out[:, lanes - 1 : lanes], right)
            x_up, c_up = x_mid, c_mid
            x_mid, c_mid = x_dn, c_dn
        if edges is not None:
            edges[1][0, g] = left
            edges[1][1, g] = right
        return carry

    lax.fori_loop(0, groups, body, 0)


def edge_pass(rows, src_ref, row_out, col_out):
    groups, span, lanes = src_ref.shape
    group = span // rows

    def body(g, carry):
        col = lax.broadcasted_iota(jnp.int32, (group, rows), 1)
        left = jnp.zeros((group, rows), jnp.float32)
        right = jnp.zeros((group, rows), jnp.float32)
        for r in range(rows):
            x = src_ref[g, pl.ds(r, group, stride=rows), :]
            if r == 0:
                row_out[0, g] = x
            if r == rows - 1:
                row_out[1, g] = x
            left = jnp.where(col == r, x[:, 0:1], left)
            right = jnp.where(col == r, x[:, lanes - 1 : lanes], right)
        col_out[0, g] = left
        col_out[1, g] = right
        return carry

    lax.fori_loop(0, groups, body, 0)


def diffuse_kernel(rows, v_ref, c_ref, out_ref, mid_ref, row_edge, col_edge, row_halo, col_halo,
                   send_sem, recv_sem):
    lon = lax.axis_index("lon")
    lat = lax.axis_index("lat")
    n_lon = lax.axis_size("lon")
    n_lat = lax.axis_size("lat")
    north = {"lat": (lat + n_lat - 1) % n_lat}
    south = {"lat": (lat + 1) % n_lat}
    west = {"lon": (lon + n_lon - 1) % n_lon}
    east = {"lon": (lon + 1) % n_lon}
    mesh_id = pl.DeviceIdType.MESH

    barrier = pltpu.get_barrier_semaphore()
    for peer in (north, south, west, east):
        pl.semaphore_signal(barrier, inc=1, device_id=peer, device_id_type=mesh_id)
    pl.semaphore_wait(barrier, 4)

    def exchange(rd):
        plan = [
            (row_edge.at[rd, 0], row_halo.at[rd, 1], north, 0),
            (row_edge.at[rd, 1], row_halo.at[rd, 0], south, 1),
            (col_edge.at[rd, 0], col_halo.at[rd, 1], west, 2),
            (col_edge.at[rd, 1], col_halo.at[rd, 0], east, 3),
        ]
        copies = []
        for src, dst, peer, k in plan:
            copy = pltpu.make_async_remote_copy(
                src_ref=src, dst_ref=dst, send_sem=send_sem.at[rd, k], recv_sem=recv_sem.at[rd, k],
                device_id=peer, device_id_type=mesh_id,
            )
            copy.start()
            copies.append(copy)
        return copies

    edge_pass(rows, c_ref, row_edge.at[0], col_edge.at[0])
    edge_pass(rows, v_ref, row_edge.at[1], col_edge.at[1])
    first = exchange(0) + exchange(1)
    for copy in first:
        copy.wait()
    north_ok = jnp.minimum(lat, 1).astype(jnp.float32)
    south_ok = jnp.minimum(n_lat - 1 - lat, 1).astype(jnp.float32)
    scales = (north_ok, south_ok)
    coef_halo = (row_halo.at[0], col_halo.at[0])
    slab_pass(rows, v_ref, c_ref, (row_halo.at[1], col_halo.at[1]), coef_halo, scales, mid_ref,
              (row_edge.at[2], col_edge.at[2]))
    for copy in exchange(2):
        copy.wait()
    slab_pass(rows, mid_ref, c_ref, (row_halo.at[2], col_halo.at[2]), coef_halo, scales, out_ref, None)


def diffuse(field, conduct_blocks):
    vals, rows, lanes = field.shape
    groups = vals // GROUP
    blocks = field.reshape(groups, GROUP * rows, lanes)
    rounds = SWEEPS + 1
    out = pl.pallas_call(
        functools.partial(diffuse_kernel, rows),
        in_specs=[VMEM, VMEM],
        out_specs=VMEM,
        out_shape=jax.ShapeDtypeStruct(blocks.shape, jnp.float32),
        scratch_shapes=[
            pltpu.VMEM(blocks.shape, jnp.float32),
            pltpu.VMEM((rounds, 2, groups, GROUP, lanes), jnp.float32),
            pltpu.VMEM((rounds, 2, groups, GROUP, rows), jnp.float32),
            pltpu.VMEM((rounds, 2, groups, GROUP, lanes), jnp.float32),
            pltpu.VMEM((rounds, 2, groups, GROUP, rows), jnp.float32),
            pltpu.SemaphoreType.DMA((rounds, 4)),
            pltpu.SemaphoreType.DMA((rounds, 4)),
        ],
        compiler_params=pltpu.CompilerParams(collective_id=0, has_side_effects=True),
        cost_estimate=pl.CostEstimate(
            flops=50 * field.size, bytes_accessed=12 * field.size, transcendentals=0
        ),
    )(blocks, conduct_blocks)
    return out.reshape(vals, rows, lanes)


def load_row(ref, index):
    return ref[pl.ds(index, 1), :]


def add_row(ref, index, value):
    spot = pl.ds(index, 1)
    ref[spot, :] = ref[spot, :] + value


def select_kernel(index_ref, rows_ref, out_ref):
    cells = rows_ref.shape[0]
    width = out_ref.shape[1]
    sub = lax.broadcasted_iota(jnp.int32, (8, width), 0)

    def body(t, carry):
        tile = jnp.zeros((8, width), jnp.float32)
        for i in range(8):
            source = index_ref[t * 8 + i]
            row = load_row(rows_ref, jnp.minimum(source, cells - 1))
            tile = jnp.where((sub == i) & (source < cells), jnp.broadcast_to(row, (8, width)), tile)
        out_ref[pl.ds(pl.multiple_of(t * 8, 8), 8), :] = tile
        return carry

    lax.fori_loop(0, out_ref.shape[0] // 8, body, 0, unroll=2)


def place_kernel(index_ref, rows_ref, out_ref, *parts):
    cells = out_ref.shape[0]
    for part in parts:
        part[...] = jnp.zeros_like(part)

    def body(t, carry):
        for i, part in enumerate(parts):
            q = t * len(parts) + i
            target = index_ref[q]
            row = load_row(rows_ref, q)
            add_row(part, jnp.minimum(target, cells - 1), jnp.where(target < cells, row, 0.0))
        return carry

    lax.fori_loop(0, rows_ref.shape[0] // len(parts), body, 0, unroll=2)
    total = parts[0][...]
    for part in parts[1:]:
        total = total + part[...]
    out_ref[...] = total


def interp_kernel(slot_ref, weight_ref, received_ref, precision_ref, equiv_ref, returned_ref, *parts):
    taps, obs_count = slot_ref.shape
    width = equiv_ref.shape[1]
    sub = lax.broadcasted_iota(jnp.int32, (8, width), 0)
    for part in parts:
        part[...] = jnp.zeros_like(part)

    def body(t, carry):
        tile = jnp.zeros((8, width), jnp.float32)
        for i in range(8):
            j = t * 8 + i
            slots = [slot_ref[k, j] for k in range(taps)]
            weights = [weight_ref[k, j] for k in range(taps)]
            total = load_row(received_ref, slots[0]) * weights[0]
            for k in range(1, taps):
                total = total + load_row(received_ref, slots[k]) * weights[k]
            tile = jnp.where(sub == i, jnp.broadcast_to(total, (8, width)), tile)
            weighted = load_row(precision_ref, j) * total
            for k in range(taps):
                add_row(parts[(i % 2) * taps + k], slots[k], weighted * weights[k])
        equiv_ref[pl.ds(pl.multiple_of(t * 8, 8), 8), :] = tile
        return carry

    lax.fori_loop(0, obs_count // 8, body, 0)
    total = parts[0][...]
    for part in parts[1:]:
        total = total + part[...]
    returned_ref[...] = total


def select_rows(index, rows, count):
    return pl.pallas_call(
        select_kernel,
        in_specs=[SMEM, VMEM],
        out_specs=VMEM,
        out_shape=jax.ShapeDtypeStruct((count, rows.shape[1]), jnp.float32),
    )(index, rows)


def place_rows(index, rows, cells):
    return pl.pallas_call(
        place_kernel,
        in_specs=[SMEM, VMEM],
        out_specs=VMEM,
        out_shape=jax.ShapeDtypeStruct((cells, rows.shape[1]), jnp.float32),
        scratch_shapes=[pltpu.VMEM((cells, rows.shape[1]), jnp.float32) for _ in range(4)],
        compiler_params=pltpu.CompilerParams(vmem_limit_bytes=60 * 1024 * 1024),
    )(index, rows)


def interpolate(obs_slots, obs_weights, received, precision_rows):
    obs_count = obs_slots.shape[1]
    return pl.pallas_call(
        interp_kernel,
        in_specs=[SMEM, SMEM, VMEM, VMEM],
        out_specs=[VMEM, VMEM],
        out_shape=[
            jax.ShapeDtypeStruct((obs_count, received.shape[1]), jnp.float32),
            jax.ShapeDtypeStruct(received.shape, jnp.float32),
        ],
        scratch_shapes=[
            pltpu.VMEM(received.shape, jnp.float32) for _ in range(2 * obs_slots.shape[0])
        ],
        compiler_params=pltpu.CompilerParams(vmem_limit_bytes=60 * 1024 * 1024),
    )(obs_slots, obs_weights, received, precision_rows)


def exchange_kernel(x_ref, out_ref, landed, send_sem, recv_sem, local_sem):
    n_lat = lax.axis_size("lat")
    count = lax.axis_size("lon") * n_lat
    chunk = x_ref.shape[0] // count
    me = lax.axis_index("lon") * n_lat + lax.axis_index("lat")
    mine = pl.ds(me * chunk, chunk)
    local = pltpu.make_async_copy(x_ref.at[mine], landed.at[mine], local_sem)
    local.start()

    def body(step, carry):
        peer = (me + step) % count
        pltpu.make_async_remote_copy(
            src_ref=x_ref.at[pl.ds(peer * chunk, chunk)],
            dst_ref=landed.at[mine],
            send_sem=send_sem,
            recv_sem=recv_sem,
            device_id={"lon": peer // n_lat, "lat": peer % n_lat},
            device_id_type=pl.DeviceIdType.MESH,
        ).start()
        return carry

    lax.fori_loop(1, count, body, 0)
    others = pl.ds(0, (count - 1) * chunk)
    pltpu.make_async_remote_copy(
        src_ref=x_ref.at[others],
        dst_ref=landed.at[others],
        send_sem=send_sem,
        recv_sem=recv_sem,
        device_id={"lon": 0, "lat": 0},
        device_id_type=pl.DeviceIdType.MESH,
    ).wait()
    local.wait()
    out_ref[...] = landed[...]


def exchange(x):
    return pl.pallas_call(
        exchange_kernel,
        in_specs=[VMEM],
        out_specs=VMEM,
        out_shape=jax.ShapeDtypeStruct(x.shape, jnp.float32),
        scratch_shapes=[
            pltpu.VMEM(x.shape, jnp.float32),
            pltpu.SemaphoreType.DMA(()),
            pltpu.SemaphoreType.DMA(()),
            pltpu.SemaphoreType.DMA(()),
        ],
        compiler_params=pltpu.CompilerParams(has_side_effects=True),
    )(x)


def on_device(state, diffusivity, sea_mask, send_cols, obs_slots, obs_weights, obs_precision):
    vals, rows, lanes = state.shape
    cell_count = rows * lanes
    steps = vals // GROUP
    sea_float = sea_mask.astype(jnp.float32)
    conduct = diffusivity * jnp.concatenate([sea_float, sea_float], axis=0)
    conduct_blocks = conduct.reshape(steps, GROUP * rows, lanes)
    smooth = diffuse(state, conduct_blocks)
    rows_of = smooth.reshape(vals, cell_count).T
    send_index = send_cols[0]
    outgoing = select_rows(send_index, rows_of, send_index.shape[0])
    received = exchange(outgoing)
    equivalent_rows, returned = interpolate(obs_slots, obs_weights, received, obs_precision.T)
    equivalents = equivalent_rows.T
    incoming = exchange(returned)
    adjoint_rows = place_rows(send_index, incoming, cell_count)
    adjoint_field = adjoint_rows.T.reshape(state.shape)
    product = state + diffuse(adjoint_field, conduct_blocks)
    return (product, equivalents)


def solution(mesh):
    placed = (
        P(None, "lat", "lon"),
        P(None, "lat", "lon"),
        P(None, "lat", "lon"),
        P(("lon", "lat"), None),
        P(None, ("lon", "lat")),
        P(None, ("lon", "lat")),
        P(None, ("lon", "lat")),
    )
    return jax.shard_map(
        on_device,
        mesh=mesh,
        in_specs=placed,
        out_specs=(P(None, "lat", "lon"), P(None, ("lon", "lat"))),
        check_vma=False,
    )
```

```python
import functools

import jax
import jax.numpy as jnp
from jax import lax
from jax.experimental import pallas as pl
from jax.experimental.pallas import tpu as pltpu
from jax.sharding import PartitionSpec as P

SWEEPS = 2
GROUP = 30
SMEM = pl.BlockSpec(memory_space=pltpu.SMEM)
VMEM = pl.BlockSpec(memory_space=pltpu.VMEM)


def slab_pass(rows, src_ref, conduct_ref, field_halo, coef_halo, scales, dst_ref, edges):
    groups, rows, group, lanes = src_ref.shape
    north_ok, south_ok = scales
    row_halo, col_halo = field_halo
    coef_rows, coef_cols = coef_halo

    def body(g, carry):
        lane = lax.broadcasted_iota(jnp.int32, (group, lanes), 1)
        col = lax.broadcasted_iota(jnp.int32, (group, rows), 1)

        def slab(ref, r):
            return ref[g, r]

        vw = col_halo[0, g]
        ve = col_halo[1, g]
        cw = coef_cols[0, g]
        ce = coef_cols[1, g]
        left = jnp.zeros((group, rows), jnp.float32)
        right = jnp.zeros((group, rows), jnp.float32)
        x_up = row_halo[0, g] * north_ok
        c_up = coef_rows[0, g] * north_ok
        x_mid, c_mid = slab(src_ref, 0), slab(conduct_ref, 0)
        for r in range(rows):
            if r + 1 < rows:
                x_dn, c_dn = slab(src_ref, r + 1), slab(conduct_ref, r + 1)
            else:
                x_dn = row_halo[1, g] * south_ok
                c_dn = coef_rows[1, g] * south_ok
            x_w = jnp.where(lane == 0, vw[:, r : r + 1], pltpu.roll(x_mid, 1, 1))
            x_e = jnp.where(lane == lanes - 1, ve[:, r : r + 1], pltpu.roll(x_mid, lanes - 1, 1))
            c_w = jnp.where(lane == 0, cw[:, r : r + 1], pltpu.roll(c_mid, 1, 1))
            c_e = jnp.where(lane == lanes - 1, ce[:, r : r + 1], pltpu.roll(c_mid, lanes - 1, 1))
            total = jnp.minimum(c_mid, c_up) * (x_up - x_mid)
            total = total + jnp.minimum(c_mid, c_dn) * (x_dn - x_mid)
            total = total + jnp.minimum(c_mid, c_w) * (x_w - x_mid)
            total = total + jnp.minimum(c_mid, c_e) * (x_e - x_mid)
            out = x_mid + total
            dst_ref[g, r] = out
            if edges is not None:
                if r == 0:
                    edges[0][0, g] = out
                if r == rows - 1:
                    edges[0][1, g] = out
                left = jnp.where(col == r, out[:, 0:1], left)
                right = jnp.where(col == r, out[:, lanes - 1 : lanes], right)
            x_up, c_up = x_mid, c_mid
            x_mid, c_mid = x_dn, c_dn
        if edges is not None:
            edges[1][0, g] = left
            edges[1][1, g] = right
        return carry

    lax.fori_loop(0, groups, body, 0)


def edge_pass(rows, src_ref, row_out, col_out):
    groups, rows, group, lanes = src_ref.shape

    def body(g, carry):
        col = lax.broadcasted_iota(jnp.int32, (group, rows), 1)
        left = jnp.zeros((group, rows), jnp.float32)
        right = jnp.zeros((group, rows), jnp.float32)
        for r in range(rows):
            x = src_ref[g, r]
            if r == 0:
                row_out[0, g] = x
            if r == rows - 1:
                row_out[1, g] = x
            left = jnp.where(col == r, x[:, 0:1], left)
            right = jnp.where(col == r, x[:, lanes - 1 : lanes], right)
        col_out[0, g] = left
        col_out[1, g] = right
        return carry

    lax.fori_loop(0, groups, body, 0)


def diffuse_kernel(rows, v_ref, c_ref, out_ref, mid_ref, row_edge, col_edge, row_halo, col_halo,
                   send_sem, recv_sem):
    lon = lax.axis_index("lon")
    lat = lax.axis_index("lat")
    n_lon = lax.axis_size("lon")
    n_lat = lax.axis_size("lat")
    north = {"lat": (lat + n_lat - 1) % n_lat}
    south = {"lat": (lat + 1) % n_lat}
    west = {"lon": (lon + n_lon - 1) % n_lon}
    east = {"lon": (lon + 1) % n_lon}
    mesh_id = pl.DeviceIdType.MESH

    barrier = pltpu.get_barrier_semaphore()
    for peer in (north, south, west, east):
        pl.semaphore_signal(barrier, inc=1, device_id=peer, device_id_type=mesh_id)
    pl.semaphore_wait(barrier, 4)

    def exchange(rd):
        plan = [
            (row_edge.at[rd, 0], row_halo.at[rd, 1], north, 0),
            (row_edge.at[rd, 1], row_halo.at[rd, 0], south, 1),
            (col_edge.at[rd, 0], col_halo.at[rd, 1], west, 2),
            (col_edge.at[rd, 1], col_halo.at[rd, 0], east, 3),
        ]
        copies = []
        for src, dst, peer, k in plan:
            copy = pltpu.make_async_remote_copy(
                src_ref=src, dst_ref=dst, send_sem=send_sem.at[rd, k], recv_sem=recv_sem.at[rd, k],
                device_id=peer, device_id_type=mesh_id,
            )
            copy.start()
            copies.append(copy)
        return copies

    edge_pass(rows, c_ref, row_edge.at[0], col_edge.at[0])
    edge_pass(rows, v_ref, row_edge.at[1], col_edge.at[1])
    first = exchange(0) + exchange(1)
    for copy in first:
        copy.wait()
    north_ok = jnp.minimum(lat, 1).astype(jnp.float32)
    south_ok = jnp.minimum(n_lat - 1 - lat, 1).astype(jnp.float32)
    scales = (north_ok, south_ok)
    coef_halo = (row_halo.at[0], col_halo.at[0])
    slab_pass(rows, v_ref, c_ref, (row_halo.at[1], col_halo.at[1]), coef_halo, scales, mid_ref,
              (row_edge.at[2], col_edge.at[2]))
    for copy in exchange(2):
        copy.wait()
    slab_pass(rows, mid_ref, c_ref, (row_halo.at[2], col_halo.at[2]), coef_halo, scales, out_ref, None)


def to_slabs(field):
    vals, rows, lanes = field.shape
    groups = vals // GROUP
    return field.reshape(groups, GROUP, rows, lanes).transpose(0, 2, 1, 3)


def from_slabs(slabs):
    groups, rows, group, lanes = slabs.shape
    return slabs.transpose(0, 2, 1, 3).reshape(groups * group, rows, lanes)


def slabs_to_rows(slabs):
    groups, rows, group, lanes = slabs.shape
    return slabs.transpose(1, 3, 0, 2).reshape(rows * lanes, groups * group)


def rows_to_slabs(cell_rows, rows, lanes):
    vals = cell_rows.shape[1]
    return cell_rows.reshape(rows, lanes, vals // GROUP, GROUP).transpose(2, 0, 3, 1)


def diffuse(blocks, conduct_blocks):
    groups, rows, group, lanes = blocks.shape
    rounds = SWEEPS + 1
    return pl.pallas_call(
        functools.partial(diffuse_kernel, rows),
        in_specs=[VMEM, VMEM],
        out_specs=VMEM,
        out_shape=jax.ShapeDtypeStruct(blocks.shape, jnp.float32),
        scratch_shapes=[
            pltpu.VMEM(blocks.shape, jnp.float32),
            pltpu.VMEM((rounds, 2, groups, GROUP, lanes), jnp.float32),
            pltpu.VMEM((rounds, 2, groups, GROUP, rows), jnp.float32),
            pltpu.VMEM((rounds, 2, groups, GROUP, lanes), jnp.float32),
            pltpu.VMEM((rounds, 2, groups, GROUP, rows), jnp.float32),
            pltpu.SemaphoreType.DMA((rounds, 4)),
            pltpu.SemaphoreType.DMA((rounds, 4)),
        ],
        compiler_params=pltpu.CompilerParams(collective_id=0, has_side_effects=True),
        cost_estimate=pl.CostEstimate(
            flops=50 * blocks.size, bytes_accessed=12 * blocks.size, transcendentals=0
        ),
    )(blocks, conduct_blocks)


def load_row(ref, index):
    return ref[pl.ds(index, 1), :]


def add_row(ref, index, value):
    spot = pl.ds(index, 1)
    ref[spot, :] = ref[spot, :] + value


def select_kernel(index_ref, rows_ref, out_ref):
    cells = rows_ref.shape[0]
    width = out_ref.shape[1]
    sub = lax.broadcasted_iota(jnp.int32, (8, width), 0)

    def body(t, carry):
        tile = jnp.zeros((8, width), jnp.float32)
        for i in range(8):
            source = index_ref[t * 8 + i]
            row = load_row(rows_ref, jnp.minimum(source, cells - 1))
            tile = jnp.where((sub == i) & (source < cells), jnp.broadcast_to(row, (8, width)), tile)
        out_ref[pl.ds(pl.multiple_of(t * 8, 8), 8), :] = tile
        return carry

    lax.fori_loop(0, out_ref.shape[0] // 8, body, 0, unroll=2)


def place_kernel(index_ref, rows_ref, out_ref, *parts):
    cells = out_ref.shape[0]
    for part in parts:
        part[...] = jnp.zeros_like(part)

    def body(t, carry):
        for i, part in enumerate(parts):
            q = t * len(parts) + i
            target = index_ref[q]
            row = load_row(rows_ref, q)
            add_row(part, jnp.minimum(target, cells - 1), jnp.where(target < cells, row, 0.0))
        return carry

    lax.fori_loop(0, rows_ref.shape[0] // len(parts), body, 0, unroll=2)
    total = parts[0][...]
    for part in parts[1:]:
        total = total + part[...]
    out_ref[...] = total


def interp_kernel(slot_ref, weight_ref, received_ref, precision_ref, equiv_ref, returned_ref, *parts):
    taps, obs_count = slot_ref.shape
    width = equiv_ref.shape[1]
    sub = lax.broadcasted_iota(jnp.int32, (8, width), 0)
    for part in parts:
        part[...] = jnp.zeros_like(part)

    def body(t, carry):
        tile = jnp.zeros((8, width), jnp.float32)
        for i in range(8):
            j = t * 8 + i
            slots = [slot_ref[k, j] for k in range(taps)]
            weights = [weight_ref[k, j] for k in range(taps)]
            total = load_row(received_ref, slots[0]) * weights[0]
            for k in range(1, taps):
                total = total + load_row(received_ref, slots[k]) * weights[k]
            tile = jnp.where(sub == i, jnp.broadcast_to(total, (8, width)), tile)
            weighted = load_row(precision_ref, j) * total
            for k in range(taps):
                add_row(parts[(i % 2) * taps + k], slots[k], weighted * weights[k])
        equiv_ref[pl.ds(pl.multiple_of(t * 8, 8), 8), :] = tile
        return carry

    lax.fori_loop(0, obs_count // 8, body, 0)
    total = parts[0][...]
    for part in parts[1:]:
        total = total + part[...]
    returned_ref[...] = total


def select_rows(index, rows, count):
    return pl.pallas_call(
        select_kernel,
        in_specs=[SMEM, VMEM],
        out_specs=VMEM,
        out_shape=jax.ShapeDtypeStruct((count, rows.shape[1]), jnp.float32),
    )(index, rows)


def place_rows(index, rows, cells):
    return pl.pallas_call(
        place_kernel,
        in_specs=[SMEM, VMEM],
        out_specs=VMEM,
        out_shape=jax.ShapeDtypeStruct((cells, rows.shape[1]), jnp.float32),
        scratch_shapes=[pltpu.VMEM((cells, rows.shape[1]), jnp.float32) for _ in range(4)],
        compiler_params=pltpu.CompilerParams(vmem_limit_bytes=60 * 1024 * 1024),
    )(index, rows)


def interpolate(obs_slots, obs_weights, received, precision_rows):
    obs_count = obs_slots.shape[1]
    return pl.pallas_call(
        interp_kernel,
        in_specs=[SMEM, SMEM, VMEM, VMEM],
        out_specs=[VMEM, VMEM],
        out_shape=[
            jax.ShapeDtypeStruct((obs_count, received.shape[1]), jnp.float32),
            jax.ShapeDtypeStruct(received.shape, jnp.float32),
        ],
        scratch_shapes=[
            pltpu.VMEM(received.shape, jnp.float32) for _ in range(2 * obs_slots.shape[0])
        ],
        compiler_params=pltpu.CompilerParams(vmem_limit_bytes=60 * 1024 * 1024),
    )(obs_slots, obs_weights, received, precision_rows)


def to_owners(outgoing):
    return lax.all_to_all(outgoing, ("lon", "lat"), split_axis=0, concat_axis=0, tiled=True)


def to_sources(returned):
    return lax.all_to_all(returned, ("lon", "lat"), split_axis=0, concat_axis=0, tiled=True)


def on_device(state, diffusivity, sea_mask, send_cols, obs_slots, obs_weights, obs_precision):
    vals, rows, lanes = state.shape
    cell_count = rows * lanes
    sea_float = sea_mask.astype(jnp.float32)
    conduct = diffusivity * jnp.concatenate([sea_float, sea_float], axis=0)
    conduct_blocks = to_slabs(conduct)
    smooth = diffuse(to_slabs(state), conduct_blocks)
    rows_of = slabs_to_rows(smooth)
    send_index = send_cols[0]
    outgoing = select_rows(send_index, rows_of, send_index.shape[0])
    received = to_owners(outgoing)
    equivalent_rows, returned = interpolate(obs_slots, obs_weights, received, obs_precision.T)
    equivalents = equivalent_rows.T
    incoming = to_sources(returned)
    adjoint_rows = place_rows(send_index, incoming, cell_count)
    adjoint_field = rows_to_slabs(adjoint_rows, rows, lanes)
    product = state + from_slabs(diffuse(adjoint_field, conduct_blocks))
    return (product, equivalents)


def solution(mesh):
    placed = (
        P(None, "lat", "lon"),
        P(None, "lat", "lon"),
        P(None, "lat", "lon"),
        P(("lon", "lat"), None),
        P(None, ("lon", "lat")),
        P(None, ("lon", "lat")),
        P(None, ("lon", "lat")),
    )
    return jax.shard_map(
        on_device,
        mesh=mesh,
        in_specs=placed,
        out_specs=(P(None, "lat", "lon"), P(None, ("lon", "lat"))),
        check_vma=False,
    )
```

```python
import functools

import jax
import jax.numpy as jnp
from jax import lax
from jax.experimental import pallas as pl
from jax.experimental.pallas import tpu as pltpu
from jax.sharding import PartitionSpec as P

SWEEPS = 2
GROUP = 30
SMEM = pl.BlockSpec(memory_space=pltpu.SMEM)
VMEM = pl.BlockSpec(memory_space=pltpu.VMEM)


def slab(ref, g, r, rows, group):
    return ref[g, pl.ds(r, group, stride=rows), :]


def edge_pass(rows, src_ref, row_out, col_out):
    groups, span, lanes = src_ref.shape
    group = span // rows

    def body(g, carry):
        col = lax.broadcasted_iota(jnp.int32, (group, rows), 1)
        left = jnp.zeros((group, rows), jnp.float32)
        right = jnp.zeros((group, rows), jnp.float32)
        for r in range(rows):
            x = slab(src_ref, g, r, rows, group)
            if r == 0:
                row_out[0, g] = x
            if r == rows - 1:
                row_out[1, g] = x
            left = jnp.where(col == r, x[:, 0:1], left)
            right = jnp.where(col == r, x[:, lanes - 1 : lanes], right)
        col_out[0, g] = left
        col_out[1, g] = right
        return carry

    lax.fori_loop(0, groups, body, 0)


def neighbours():
    lon = lax.axis_index("lon")
    lat = lax.axis_index("lat")
    n_lon = lax.axis_size("lon")
    n_lat = lax.axis_size("lat")
    north = {"lat": (lat + n_lat - 1) % n_lat}
    south = {"lat": (lat + 1) % n_lat}
    west = {"lon": (lon + n_lon - 1) % n_lon}
    east = {"lon": (lon + 1) % n_lon}
    north_ok = jnp.minimum(lat, 1).astype(jnp.float32)
    south_ok = jnp.minimum(n_lat - 1 - lat, 1).astype(jnp.float32)
    return (north, south, west, east), (north_ok, south_ok)


def enter(peers):
    barrier = pltpu.get_barrier_semaphore()
    for peer in peers:
        pl.semaphore_signal(barrier, inc=1, device_id=peer, device_id_type=pl.DeviceIdType.MESH)
    pl.semaphore_wait(barrier, len(peers))


def swap(peers, row_edge, col_edge, row_halo, col_halo, send_sem, recv_sem, rd):
    north, south, west, east = peers
    plan = [
        (row_edge.at[rd, 0], row_halo.at[rd, 1], north, 0),
        (row_edge.at[rd, 1], row_halo.at[rd, 0], south, 1),
        (col_edge.at[rd, 0], col_halo.at[rd, 1], west, 2),
        (col_edge.at[rd, 1], col_halo.at[rd, 0], east, 3),
    ]
    copies = []
    for src, dst, peer, k in plan:
        copy = pltpu.make_async_remote_copy(
            src_ref=src, dst_ref=dst, send_sem=send_sem.at[rd, k], recv_sem=recv_sem.at[rd, k],
            device_id=peer, device_id_type=pl.DeviceIdType.MESH,
        )
        copy.start()
        copies.append(copy)
    for copy in copies:
        copy.wait()


def coef_kernel(rows, c_ref, k_ref, row_edge, col_edge, row_halo, col_halo, send_sem, recv_sem):
    peers, (north_ok, south_ok) = neighbours()
    enter(peers)
    edge_pass(rows, c_ref, row_edge.at[0], col_edge.at[0])
    swap(peers, row_edge, col_edge, row_halo, col_halo, send_sem, recv_sem, 0)
    groups, span, lanes = c_ref.shape
    group = span // rows

    def body(g, carry):
        lane = lax.broadcasted_iota(jnp.int32, (group, lanes), 1)
        cw = col_halo[0, 0, g]
        ce = col_halo[0, 1, g]
        c_up = row_halo[0, 0, g] * north_ok
        c_mid = slab(c_ref, g, 0, rows, group)
        for r in range(rows):
            if r + 1 < rows:
                c_dn = slab(c_ref, g, r + 1, rows, group)
            else:
                c_dn = row_halo[0, 1, g] * south_ok
            c_w = jnp.where(lane == 0, cw[:, r : r + 1], pltpu.roll(c_mid, 1, 1))
            c_e = jnp.where(lane == lanes - 1, ce[:, r : r + 1], pltpu.roll(c_mid, lanes - 1, 1))
            spot = pl.ds(r, group, stride=rows)
            k_ref[0, g, spot, :] = jnp.minimum(c_mid, c_up)
            k_ref[1, g, spot, :] = jnp.minimum(c_mid, c_dn)
            k_ref[2, g, spot, :] = jnp.minimum(c_mid, c_w)
            k_ref[3, g, spot, :] = jnp.minimum(c_mid, c_e)
            c_up, c_mid = c_mid, c_dn
        return carry

    lax.fori_loop(0, groups, body, 0)


def sweep_pass(rows, src_ref, k_ref, row_halo, col_halo, scales, dst_ref, edges):
    groups, span, lanes = src_ref.shape
    group = span // rows
    north_ok, south_ok = scales

    def body(g, carry):
        lane = lax.broadcasted_iota(jnp.int32, (group, lanes), 1)
        col = lax.broadcasted_iota(jnp.int32, (group, rows), 1)
        vw = col_halo[0, g]
        ve = col_halo[1, g]
        left = jnp.zeros((group, rows), jnp.float32)
        right = jnp.zeros((group, rows), jnp.float32)
        x_up = row_halo[0, g] * north_ok
        x_mid = slab(src_ref, g, 0, rows, group)
        for r in range(rows):
            if r + 1 < rows:
                x_dn = slab(src_ref, g, r + 1, rows, group)
            else:
                x_dn = row_halo[1, g] * south_ok
            x_w = jnp.where(lane == 0, vw[:, r : r + 1], pltpu.roll(x_mid, 1, 1))
            x_e = jnp.where(lane == lanes - 1, ve[:, r : r + 1], pltpu.roll(x_mid, lanes - 1, 1))
            total = slab(k_ref.at[0], g, r, rows, group) * (x_up - x_mid)
            total = total + slab(k_ref.at[1], g, r, rows, group) * (x_dn - x_mid)
            total = total + slab(k_ref.at[2], g, r, rows, group) * (x_w - x_mid)
            total = total + slab(k_ref.at[3], g, r, rows, group) * (x_e - x_mid)
            out = x_mid + total
            dst_ref[g, pl.ds(r, group, stride=rows), :] = out
            if edges is not None:
                if r == 0:
                    edges[0][0, g] = out
                if r == rows - 1:
                    edges[0][1, g] = out
                left = jnp.where(col == r, out[:, 0:1], left)
                right = jnp.where(col == r, out[:, lanes - 1 : lanes], right)
            x_up, x_mid = x_mid, x_dn
        if edges is not None:
            edges[1][0, g] = left
            edges[1][1, g] = right
        return carry

    lax.fori_loop(0, groups, body, 0)


def diffuse_kernel(rows, v_ref, k_ref, out_ref, mid_ref, row_edge, col_edge, row_halo, col_halo,
                   send_sem, recv_sem):
    peers, scales = neighbours()
    enter(peers)
    edge_pass(rows, v_ref, row_edge.at[0], col_edge.at[0])
    swap(peers, row_edge, col_edge, row_halo, col_halo, send_sem, recv_sem, 0)
    sweep_pass(rows, v_ref, k_ref, row_halo.at[0], col_halo.at[0], scales, mid_ref,
               (row_edge.at[1], col_edge.at[1]))
    swap(peers, row_edge, col_edge, row_halo, col_halo, send_sem, recv_sem, 1)
    sweep_pass(rows, mid_ref, k_ref, row_halo.at[1], col_halo.at[1], scales, out_ref, None)


def edge_scratch(rounds, groups, rows, lanes):
    return [
        pltpu.VMEM((rounds, 2, groups, GROUP, lanes), jnp.float32),
        pltpu.VMEM((rounds, 2, groups, GROUP, rows), jnp.float32),
        pltpu.VMEM((rounds, 2, groups, GROUP, lanes), jnp.float32),
        pltpu.VMEM((rounds, 2, groups, GROUP, rows), jnp.float32),
        pltpu.SemaphoreType.DMA((rounds, 4)),
        pltpu.SemaphoreType.DMA((rounds, 4)),
    ]


def coefficients(conduct_blocks, rows):
    groups, span, lanes = conduct_blocks.shape
    return pl.pallas_call(
        functools.partial(coef_kernel, rows),
        in_specs=[VMEM],
        out_specs=VMEM,
        out_shape=jax.ShapeDtypeStruct((4,) + conduct_blocks.shape, jnp.float32),
        scratch_shapes=edge_scratch(1, groups, rows, lanes),
        compiler_params=pltpu.CompilerParams(collective_id=1, has_side_effects=True),
    )(conduct_blocks)


def diffuse(field, coef):
    vals, rows, lanes = field.shape
    groups = vals // GROUP
    blocks = field.reshape(groups, GROUP * rows, lanes)
    out = pl.pallas_call(
        functools.partial(diffuse_kernel, rows),
        in_specs=[VMEM, VMEM],
        out_specs=VMEM,
        out_shape=jax.ShapeDtypeStruct(blocks.shape, jnp.float32),
        scratch_shapes=[pltpu.VMEM(blocks.shape, jnp.float32)] + edge_scratch(SWEEPS, groups, rows, lanes),
        compiler_params=pltpu.CompilerParams(collective_id=0, has_side_effects=True),
        cost_estimate=pl.CostEstimate(
            flops=30 * field.size, bytes_accessed=28 * field.size, transcendentals=0
        ),
    )(blocks, coef)
    return out.reshape(vals, rows, lanes)


def load_row(ref, index):
    return ref[pl.ds(index, 1), :]


def add_row(ref, index, value):
    spot = pl.ds(index, 1)
    ref[spot, :] = ref[spot, :] + value


def select_kernel(index_ref, rows_ref, out_ref):
    cells = rows_ref.shape[0]
    width = out_ref.shape[1]
    sub = lax.broadcasted_iota(jnp.int32, (8, width), 0)

    def body(t, carry):
        tile = jnp.zeros((8, width), jnp.float32)
        for i in range(8):
            source = index_ref[t * 8 + i]
            row = load_row(rows_ref, jnp.minimum(source, cells - 1))
            tile = jnp.where((sub == i) & (source < cells), jnp.broadcast_to(row, (8, width)), tile)
        out_ref[pl.ds(pl.multiple_of(t * 8, 8), 8), :] = tile
        return carry

    lax.fori_loop(0, out_ref.shape[0] // 8, body, 0, unroll=2)


def place_kernel(index_ref, rows_ref, out_ref, *parts):
    cells = out_ref.shape[0]
    for part in parts:
        part[...] = jnp.zeros_like(part)

    def body(t, carry):
        for i, part in enumerate(parts):
            q = t * len(parts) + i
            target = index_ref[q]
            row = load_row(rows_ref, q)
            add_row(part, jnp.minimum(target, cells - 1), jnp.where(target < cells, row, 0.0))
        return carry

    lax.fori_loop(0, rows_ref.shape[0] // len(parts), body, 0, unroll=2)
    total = parts[0][...]
    for part in parts[1:]:
        total = total + part[...]
    out_ref[...] = total


def interp_kernel(slot_ref, weight_ref, received_ref, precision_ref, equiv_ref, returned_ref, *parts):
    taps, obs_count = slot_ref.shape
    width = equiv_ref.shape[1]
    sub = lax.broadcasted_iota(jnp.int32, (8, width), 0)
    for part in parts:
        part[...] = jnp.zeros_like(part)

    def body(t, carry):
        tile = jnp.zeros((8, width), jnp.float32)
        for i in range(8):
            j = t * 8 + i
            slots = [slot_ref[k, j] for k in range(taps)]
            weights = [weight_ref[k, j] for k in range(taps)]
            total = load_row(received_ref, slots[0]) * weights[0]
            for k in range(1, taps):
                total = total + load_row(received_ref, slots[k]) * weights[k]
            tile = jnp.where(sub == i, jnp.broadcast_to(total, (8, width)), tile)
            weighted = load_row(precision_ref, j) * total
            for k in range(taps):
                add_row(parts[(i % 2) * taps + k], slots[k], weighted * weights[k])
        equiv_ref[pl.ds(pl.multiple_of(t * 8, 8), 8), :] = tile
        return carry

    lax.fori_loop(0, obs_count // 8, body, 0)
    total = parts[0][...]
    for part in parts[1:]:
        total = total + part[...]
    returned_ref[...] = total


def select_rows(index, rows, count):
    return pl.pallas_call(
        select_kernel,
        in_specs=[SMEM, VMEM],
        out_specs=VMEM,
        out_shape=jax.ShapeDtypeStruct((count, rows.shape[1]), jnp.float32),
    )(index, rows)


def place_rows(index, rows, cells):
    return pl.pallas_call(
        place_kernel,
        in_specs=[SMEM, VMEM],
        out_specs=VMEM,
        out_shape=jax.ShapeDtypeStruct((cells, rows.shape[1]), jnp.float32),
        scratch_shapes=[pltpu.VMEM((cells, rows.shape[1]), jnp.float32) for _ in range(4)],
        compiler_params=pltpu.CompilerParams(vmem_limit_bytes=60 * 1024 * 1024),
    )(index, rows)


def interpolate(obs_slots, obs_weights, received, precision_rows):
    obs_count = obs_slots.shape[1]
    return pl.pallas_call(
        interp_kernel,
        in_specs=[SMEM, SMEM, VMEM, VMEM],
        out_specs=[VMEM, VMEM],
        out_shape=[
            jax.ShapeDtypeStruct((obs_count, received.shape[1]), jnp.float32),
            jax.ShapeDtypeStruct(received.shape, jnp.float32),
        ],
        scratch_shapes=[
            pltpu.VMEM(received.shape, jnp.float32) for _ in range(2 * obs_slots.shape[0])
        ],
        compiler_params=pltpu.CompilerParams(vmem_limit_bytes=60 * 1024 * 1024),
    )(obs_slots, obs_weights, received, precision_rows)


def to_owners(outgoing):
    return lax.all_to_all(outgoing, ("lon", "lat"), split_axis=0, concat_axis=0, tiled=True)


def to_sources(returned):
    return lax.all_to_all(returned, ("lon", "lat"), split_axis=0, concat_axis=0, tiled=True)


def on_device(state, diffusivity, sea_mask, send_cols, obs_slots, obs_weights, obs_precision):
    vals, rows, lanes = state.shape
    cell_count = rows * lanes
    steps = vals // GROUP
    sea_float = sea_mask.astype(jnp.float32)
    conduct = diffusivity * jnp.concatenate([sea_float, sea_float], axis=0)
    coef = coefficients(conduct.reshape(steps, GROUP * rows, lanes), rows)
    smooth = diffuse(state, coef)
    rows_of = smooth.reshape(vals, cell_count).T
    send_index = send_cols[0]
    outgoing = select_rows(send_index, rows_of, send_index.shape[0])
    received = to_owners(outgoing)
    equivalent_rows, returned = interpolate(obs_slots, obs_weights, received, obs_precision.T)
    equivalents = equivalent_rows.T
    incoming = to_sources(returned)
    adjoint_rows = place_rows(send_index, incoming, cell_count)
    adjoint_field = adjoint_rows.T.reshape(state.shape)
    product = state + diffuse(adjoint_field, coef)
    return (product, equivalents)


def solution(mesh):
    placed = (
        P(None, "lat", "lon"),
        P(None, "lat", "lon"),
        P(None, "lat", "lon"),
        P(("lon", "lat"), None),
        P(None, ("lon", "lat")),
        P(None, ("lon", "lat")),
        P(None, ("lon", "lat")),
    )
    return jax.shard_map(
        on_device,
        mesh=mesh,
        in_specs=placed,
        out_specs=(P(None, "lat", "lon"), P(None, ("lon", "lat"))),
        check_vma=False,
    )
```

```python
import functools

import jax
import jax.numpy as jnp
from jax import lax
from jax.experimental import pallas as pl
from jax.experimental.pallas import tpu as pltpu
from jax.sharding import PartitionSpec as P

SWEEPS = 2
GROUP = 30
SMEM = pl.BlockSpec(memory_space=pltpu.SMEM)
VMEM = pl.BlockSpec(memory_space=pltpu.VMEM)


def slab_pass(rows, src_ref, conduct_ref, field_halo, coef_halo, scales, dst_ref, edges):
    groups, span, lanes = src_ref.shape
    group = span // rows
    north_ok, south_ok = scales
    row_halo, col_halo = field_halo
    coef_rows, coef_cols = coef_halo

    def body(g, carry):
        lane = lax.broadcasted_iota(jnp.int32, (group, lanes), 1)
        col = lax.broadcasted_iota(jnp.int32, (group, rows), 1)

        def slab(ref, r):
            return ref[g, pl.ds(r, group, stride=rows), :]

        vw = col_halo[0, g]
        ve = col_halo[1, g]
        cw = coef_cols[0, g]
        ce = coef_cols[1, g]
        left = jnp.zeros((group, rows), jnp.float32)
        right = jnp.zeros((group, rows), jnp.float32)
        x_up = row_halo[0, g] * north_ok
        c_up = coef_rows[0, g] * north_ok
        x_mid, c_mid = slab(src_ref, 0), slab(conduct_ref, 0)
        for r in range(rows):
            if r + 1 < rows:
                x_dn, c_dn = slab(src_ref, r + 1), slab(conduct_ref, r + 1)
            else:
                x_dn = row_halo[1, g] * south_ok
                c_dn = coef_rows[1, g] * south_ok
            x_w = jnp.where(lane == 0, vw[:, r : r + 1], pltpu.roll(x_mid, 1, 1))
            x_e = jnp.where(lane == lanes - 1, ve[:, r : r + 1], pltpu.roll(x_mid, lanes - 1, 1))
            c_w = jnp.where(lane == 0, cw[:, r : r + 1], pltpu.roll(c_mid, 1, 1))
            c_e = jnp.where(lane == lanes - 1, ce[:, r : r + 1], pltpu.roll(c_mid, lanes - 1, 1))
            total = jnp.minimum(c_mid, c_up) * (x_up - x_mid)
            total = total + jnp.minimum(c_mid, c_dn) * (x_dn - x_mid)
            total = total + jnp.minimum(c_mid, c_w) * (x_w - x_mid)
            total = total + jnp.minimum(c_mid, c_e) * (x_e - x_mid)
            out = x_mid + total
            dst_ref[g, pl.ds(r, group, stride=rows), :] = out
            if edges is not None:
                if r == 0:
                    edges[0][0, g] = out
                if r == rows - 1:
                    edges[0][1, g] = out
                left = jnp.where(col == r, out[:, 0:1], left)
                right = jnp.where(col == r, out[:, lanes - 1 : lanes], right)
            x_up, c_up = x_mid, c_mid
            x_mid, c_mid = x_dn, c_dn
        if edges is not None:
            edges[1][0, g] = left
            edges[1][1, g] = right
        return carry

    lax.fori_loop(0, groups, body, 0)


def edge_pass(rows, src_ref, row_out, col_out):
    groups, span, lanes = src_ref.shape
    group = span // rows

    def body(g, carry):
        col = lax.broadcasted_iota(jnp.int32, (group, rows), 1)
        left = jnp.zeros((group, rows), jnp.float32)
        right = jnp.zeros((group, rows), jnp.float32)
        for r in range(rows):
            x = src_ref[g, pl.ds(r, group, stride=rows), :]
            if r == 0:
                row_out[0, g] = x
            if r == rows - 1:
                row_out[1, g] = x
            left = jnp.where(col == r, x[:, 0:1], left)
            right = jnp.where(col == r, x[:, lanes - 1 : lanes], right)
        col_out[0, g] = left
        col_out[1, g] = right
        return carry

    lax.fori_loop(0, groups, body, 0)


def diffuse_kernel(rows, v_ref, c_ref, out_ref, mid_ref, row_edge, col_edge, row_halo, col_halo,
                   send_sem, recv_sem):
    lon = lax.axis_index("lon")
    lat = lax.axis_index("lat")
    n_lon = lax.axis_size("lon")
    n_lat = lax.axis_size("lat")
    north = {"lat": (lat + n_lat - 1) % n_lat}
    south = {"lat": (lat + 1) % n_lat}
    west = {"lon": (lon + n_lon - 1) % n_lon}
    east = {"lon": (lon + 1) % n_lon}
    mesh_id = pl.DeviceIdType.MESH

    barrier = pltpu.get_barrier_semaphore()
    for peer in (north, south, west, east):
        pl.semaphore_signal(barrier, inc=1, device_id=peer, device_id_type=mesh_id)
    pl.semaphore_wait(barrier, 4)

    def exchange(rd):
        plan = [
            (row_edge.at[rd, 0], row_halo.at[rd, 1], north, 0),
            (row_edge.at[rd, 1], row_halo.at[rd, 0], south, 1),
            (col_edge.at[rd, 0], col_halo.at[rd, 1], west, 2),
            (col_edge.at[rd, 1], col_halo.at[rd, 0], east, 3),
        ]
        copies = []
        for src, dst, peer, k in plan:
            copy = pltpu.make_async_remote_copy(
                src_ref=src, dst_ref=dst, send_sem=send_sem.at[rd, k], recv_sem=recv_sem.at[rd, k],
                device_id=peer, device_id_type=mesh_id,
            )
            copy.start()
            copies.append(copy)
        return copies

    edge_pass(rows, c_ref, row_edge.at[0], col_edge.at[0])
    edge_pass(rows, v_ref, row_edge.at[1], col_edge.at[1])
    first = exchange(0) + exchange(1)
    for copy in first:
        copy.wait()
    north_ok = jnp.minimum(lat, 1).astype(jnp.float32)
    south_ok = jnp.minimum(n_lat - 1 - lat, 1).astype(jnp.float32)
    scales = (north_ok, south_ok)
    coef_halo = (row_halo.at[0], col_halo.at[0])
    slab_pass(rows, v_ref, c_ref, (row_halo.at[1], col_halo.at[1]), coef_halo, scales, mid_ref,
              (row_edge.at[2], col_edge.at[2]))
    for copy in exchange(2):
        copy.wait()
    slab_pass(rows, mid_ref, c_ref, (row_halo.at[2], col_halo.at[2]), coef_halo, scales, out_ref, None)


def diffuse(field, conduct_blocks):
    vals, rows, lanes = field.shape
    groups = vals // GROUP
    blocks = field.reshape(groups, GROUP * rows, lanes)
    rounds = SWEEPS + 1
    out = pl.pallas_call(
        functools.partial(diffuse_kernel, rows),
        in_specs=[VMEM, VMEM],
        out_specs=VMEM,
        out_shape=jax.ShapeDtypeStruct(blocks.shape, jnp.float32),
        scratch_shapes=[
            pltpu.VMEM(blocks.shape, jnp.float32),
            pltpu.VMEM((rounds, 2, groups, GROUP, lanes), jnp.float32),
            pltpu.VMEM((rounds, 2, groups, GROUP, rows), jnp.float32),
            pltpu.VMEM((rounds, 2, groups, GROUP, lanes), jnp.float32),
            pltpu.VMEM((rounds, 2, groups, GROUP, rows), jnp.float32),
            pltpu.SemaphoreType.DMA((rounds, 4)),
            pltpu.SemaphoreType.DMA((rounds, 4)),
        ],
        compiler_params=pltpu.CompilerParams(collective_id=0, has_side_effects=True),
        cost_estimate=pl.CostEstimate(
            flops=50 * field.size, bytes_accessed=12 * field.size, transcendentals=0
        ),
    )(blocks, conduct_blocks)
    return out.reshape(vals, rows, lanes)


def load_row(ref, index):
    return ref[pl.ds(index, 1), :]


def add_row(ref, index, value):
    spot = pl.ds(index, 1)
    ref[spot, :] = ref[spot, :] + value


def select_kernel(index_ref, rows_ref, out_ref):
    cells = rows_ref.shape[0]
    width = out_ref.shape[1]
    sub = lax.broadcasted_iota(jnp.int32, (8, width), 0)

    def body(t, carry):
        tile = jnp.zeros((8, width), jnp.float32)
        for i in range(8):
            source = index_ref[t * 8 + i]
            row = load_row(rows_ref, jnp.minimum(source, cells - 1))
            tile = jnp.where((sub == i) & (source < cells), jnp.broadcast_to(row, (8, width)), tile)
        out_ref[pl.ds(pl.multiple_of(t * 8, 8), 8), :] = tile
        return carry

    lax.fori_loop(0, out_ref.shape[0] // 8, body, 0, unroll=2)


def place_kernel(index_ref, rows_ref, out_ref, *parts):
    cells = out_ref.shape[0]
    for part in parts:
        part[...] = jnp.zeros_like(part)

    def body(t, carry):
        for i, part in enumerate(parts):
            q = t * len(parts) + i
            target = index_ref[q]
            row = load_row(rows_ref, q)
            add_row(part, jnp.minimum(target, cells - 1), jnp.where(target < cells, row, 0.0))
        return carry

    lax.fori_loop(0, rows_ref.shape[0] // len(parts), body, 0, unroll=2)
    total = parts[0][...]
    for part in parts[1:]:
        total = total + part[...]
    out_ref[...] = total


def interp_kernel(slot_ref, weight_ref, received_ref, precision_ref, equiv_ref, returned_ref, *parts):
    taps, obs_count = slot_ref.shape
    width = equiv_ref.shape[1]
    sub = lax.broadcasted_iota(jnp.int32, (8, width), 0)
    for part in parts:
        part[...] = jnp.zeros_like(part)

    def body(t, carry):
        tile = jnp.zeros((8, width), jnp.float32)
        for i in range(8):
            j = t * 8 + i
            slots = [slot_ref[k, j] for k in range(taps)]
            weights = [weight_ref[k, j] for k in range(taps)]
            total = load_row(received_ref, slots[0]) * weights[0]
            for k in range(1, taps):
                total = total + load_row(received_ref, slots[k]) * weights[k]
            tile = jnp.where(sub == i, jnp.broadcast_to(total, (8, width)), tile)
            weighted = load_row(precision_ref, j) * total
            for k in range(taps):
                add_row(parts[(i % 2) * taps + k], slots[k], weighted * weights[k])
        equiv_ref[pl.ds(pl.multiple_of(t * 8, 8), 8), :] = tile
        return carry

    lax.fori_loop(0, obs_count // 8, body, 0)
    total = parts[0][...]
    for part in parts[1:]:
        total = total + part[...]
    returned_ref[...] = total


def select_rows(index, rows, count):
    return pl.pallas_call(
        select_kernel,
        in_specs=[SMEM, VMEM],
        out_specs=VMEM,
        out_shape=jax.ShapeDtypeStruct((count, rows.shape[1]), jnp.float32),
    )(index, rows)


def place_rows(index, rows, cells):
    return pl.pallas_call(
        place_kernel,
        in_specs=[SMEM, VMEM],
        out_specs=VMEM,
        out_shape=jax.ShapeDtypeStruct((cells, rows.shape[1]), jnp.float32),
        scratch_shapes=[pltpu.VMEM((cells, rows.shape[1]), jnp.float32) for _ in range(4)],
        compiler_params=pltpu.CompilerParams(vmem_limit_bytes=60 * 1024 * 1024),
    )(index, rows)


def interpolate(obs_slots, obs_weights, received, precision_rows):
    obs_count = obs_slots.shape[1]
    return pl.pallas_call(
        interp_kernel,
        in_specs=[SMEM, SMEM, VMEM, VMEM],
        out_specs=[VMEM, VMEM],
        out_shape=[
            jax.ShapeDtypeStruct((obs_count, received.shape[1]), jnp.float32),
            jax.ShapeDtypeStruct(received.shape, jnp.float32),
        ],
        scratch_shapes=[
            pltpu.VMEM(received.shape, jnp.float32) for _ in range(2 * obs_slots.shape[0])
        ],
        compiler_params=pltpu.CompilerParams(vmem_limit_bytes=60 * 1024 * 1024),
    )(obs_slots, obs_weights, received, precision_rows)


def regroup(rows):
    n_lon = lax.axis_size("lon")
    n_lat = lax.axis_size("lat")
    slots, vals = rows.shape
    chunk = slots // (n_lon * n_lat)
    blocks = rows.reshape(n_lon, n_lat, chunk, vals)
    blocks = lax.all_to_all(blocks, "lat", split_axis=1, concat_axis=1, tiled=True)
    blocks = lax.all_to_all(blocks, "lon", split_axis=0, concat_axis=0, tiled=True)
    return blocks.reshape(slots, vals)


def to_owners(outgoing):
    return regroup(outgoing)


def to_sources(returned):
    return regroup(returned)


def on_device(state, diffusivity, sea_mask, send_cols, obs_slots, obs_weights, obs_precision):
    vals, rows, lanes = state.shape
    cell_count = rows * lanes
    steps = vals // GROUP
    sea_float = sea_mask.astype(jnp.float32)
    conduct = diffusivity * jnp.concatenate([sea_float, sea_float], axis=0)
    conduct_blocks = conduct.reshape(steps, GROUP * rows, lanes)
    smooth = diffuse(state, conduct_blocks)
    rows_of = smooth.reshape(vals, cell_count).T
    send_index = send_cols[0]
    outgoing = select_rows(send_index, rows_of, send_index.shape[0])
    received = to_owners(outgoing)
    equivalent_rows, returned = interpolate(obs_slots, obs_weights, received, obs_precision.T)
    equivalents = equivalent_rows.T
    incoming = to_sources(returned)
    adjoint_rows = place_rows(send_index, incoming, cell_count)
    adjoint_field = adjoint_rows.T.reshape(state.shape)
    product = state + diffuse(adjoint_field, conduct_blocks)
    return (product, equivalents)


def solution(mesh):
    placed = (
        P(None, "lat", "lon"),
        P(None, "lat", "lon"),
        P(None, "lat", "lon"),
        P(("lon", "lat"), None),
        P(None, ("lon", "lat")),
        P(None, ("lon", "lat")),
        P(None, ("lon", "lat")),
    )
    return jax.shard_map(
        on_device,
        mesh=mesh,
        in_specs=placed,
        out_specs=(P(None, "lat", "lon"), P(None, ("lon", "lat"))),
        check_vma=False,
    )
```

```python
import functools

import jax
import jax.numpy as jnp
from jax import lax
from jax.experimental import pallas as pl
from jax.experimental.pallas import tpu as pltpu
from jax.sharding import PartitionSpec as P

SWEEPS = 2
GROUP = 30
SMEM = pl.BlockSpec(memory_space=pltpu.SMEM)
VMEM = pl.BlockSpec(memory_space=pltpu.VMEM)


def coef_pass(rows, c_ref, coef_halo, scales, k_ref):
    groups, span, lanes = c_ref.shape
    group = span // rows
    north_ok, south_ok = scales
    coef_rows, coef_cols = coef_halo

    def body(g, carry):
        lane = lax.broadcasted_iota(jnp.int32, (group, lanes), 1)
        cw = coef_cols[0, g]
        ce = coef_cols[1, g]
        c_up = coef_rows[0, g] * north_ok
        c_mid = c_ref[g, pl.ds(0, group, stride=rows), :]
        for r in range(rows):
            if r + 1 < rows:
                c_dn = c_ref[g, pl.ds(r + 1, group, stride=rows), :]
            else:
                c_dn = coef_rows[1, g] * south_ok
            c_w = jnp.where(lane == 0, cw[:, r : r + 1], pltpu.roll(c_mid, 1, 1))
            c_e = jnp.where(lane == lanes - 1, ce[:, r : r + 1], pltpu.roll(c_mid, lanes - 1, 1))
            k_ref[0, g, r] = jnp.minimum(c_mid, c_up)
            k_ref[1, g, r] = jnp.minimum(c_mid, c_dn)
            k_ref[2, g, r] = jnp.minimum(c_mid, c_w)
            k_ref[3, g, r] = jnp.minimum(c_mid, c_e)
            c_up, c_mid = c_mid, c_dn
        return carry

    lax.fori_loop(0, groups, body, 0)


def slab_pass(rows, src_ref, k_ref, field_halo, scales, dst_ref, edges):
    groups, span, lanes = src_ref.shape
    group = span // rows
    north_ok, south_ok = scales
    row_halo, col_halo = field_halo

    def body(g, carry):
        lane = lax.broadcasted_iota(jnp.int32, (group, lanes), 1)
        col = lax.broadcasted_iota(jnp.int32, (group, rows), 1)

        def slab(ref, r):
            return ref[g, pl.ds(r, group, stride=rows), :]

        vw = col_halo[0, g]
        ve = col_halo[1, g]
        left = jnp.zeros((group, rows), jnp.float32)
        right = jnp.zeros((group, rows), jnp.float32)
        x_up = row_halo[0, g] * north_ok
        x_mid = slab(src_ref, 0)
        for r in range(rows):
            if r + 1 < rows:
                x_dn = slab(src_ref, r + 1)
            else:
                x_dn = row_halo[1, g] * south_ok
            x_w = jnp.where(lane == 0, vw[:, r : r + 1], pltpu.roll(x_mid, 1, 1))
            x_e = jnp.where(lane == lanes - 1, ve[:, r : r + 1], pltpu.roll(x_mid, lanes - 1, 1))
            total = k_ref[0, g, r] * (x_up - x_mid)
            total = total + k_ref[1, g, r] * (x_dn - x_mid)
            total = total + k_ref[2, g, r] * (x_w - x_mid)
            total = total + k_ref[3, g, r] * (x_e - x_mid)
            out = x_mid + total
            dst_ref[g, pl.ds(r, group, stride=rows), :] = out
            if edges is not None:
                if r == 0:
                    edges[0][0, g] = out
                if r == rows - 1:
                    edges[0][1, g] = out
                left = jnp.where(col == r, out[:, 0:1], left)
                right = jnp.where(col == r, out[:, lanes - 1 : lanes], right)
            x_up, x_mid = x_mid, x_dn
        if edges is not None:
            edges[1][0, g] = left
            edges[1][1, g] = right
        return carry

    lax.fori_loop(0, groups, body, 0)


def edge_pass(rows, src_ref, row_out, col_out):
    groups, span, lanes = src_ref.shape
    group = span // rows

    def body(g, carry):
        col = lax.broadcasted_iota(jnp.int32, (group, rows), 1)
        left = jnp.zeros((group, rows), jnp.float32)
        right = jnp.zeros((group, rows), jnp.float32)
        for r in range(rows):
            x = src_ref[g, pl.ds(r, group, stride=rows), :]
            if r == 0:
                row_out[0, g] = x
            if r == rows - 1:
                row_out[1, g] = x
            left = jnp.where(col == r, x[:, 0:1], left)
            right = jnp.where(col == r, x[:, lanes - 1 : lanes], right)
        col_out[0, g] = left
        col_out[1, g] = right
        return carry

    lax.fori_loop(0, groups, body, 0)


def diffuse_kernel(rows, v_ref, c_ref, out_ref, mid_ref, k_ref, row_edge, col_edge, row_halo,
                   col_halo, send_sem, recv_sem):
    lon = lax.axis_index("lon")
    lat = lax.axis_index("lat")
    n_lon = lax.axis_size("lon")
    n_lat = lax.axis_size("lat")
    north = {"lat": (lat + n_lat - 1) % n_lat}
    south = {"lat": (lat + 1) % n_lat}
    west = {"lon": (lon + n_lon - 1) % n_lon}
    east = {"lon": (lon + 1) % n_lon}
    mesh_id = pl.DeviceIdType.MESH

    barrier = pltpu.get_barrier_semaphore()
    for peer in (north, south, west, east):
        pl.semaphore_signal(barrier, inc=1, device_id=peer, device_id_type=mesh_id)
    pl.semaphore_wait(barrier, 4)

    def exchange(rd):
        plan = [
            (row_edge.at[rd, 0], row_halo.at[rd, 1], north, 0),
            (row_edge.at[rd, 1], row_halo.at[rd, 0], south, 1),
            (col_edge.at[rd, 0], col_halo.at[rd, 1], west, 2),
            (col_edge.at[rd, 1], col_halo.at[rd, 0], east, 3),
        ]
        copies = []
        for src, dst, peer, k in plan:
            copy = pltpu.make_async_remote_copy(
                src_ref=src, dst_ref=dst, send_sem=send_sem.at[rd, k], recv_sem=recv_sem.at[rd, k],
                device_id=peer, device_id_type=mesh_id,
            )
            copy.start()
            copies.append(copy)
        return copies

    edge_pass(rows, c_ref, row_edge.at[0], col_edge.at[0])
    edge_pass(rows, v_ref, row_edge.at[1], col_edge.at[1])
    first = exchange(0) + exchange(1)
    for copy in first:
        copy.wait()
    north_ok = jnp.minimum(lat, 1).astype(jnp.float32)
    south_ok = jnp.minimum(n_lat - 1 - lat, 1).astype(jnp.float32)
    scales = (north_ok, south_ok)
    coef_pass(rows, c_ref, (row_halo.at[0], col_halo.at[0]), scales, k_ref)
    slab_pass(rows, v_ref, k_ref, (row_halo.at[1], col_halo.at[1]), scales, mid_ref,
              (row_edge.at[2], col_edge.at[2]))
    for copy in exchange(2):
        copy.wait()
    slab_pass(rows, mid_ref, k_ref, (row_halo.at[2], col_halo.at[2]), scales, out_ref, None)


def diffuse(field, conduct_blocks):
    vals, rows, lanes = field.shape
    groups = vals // GROUP
    blocks = field.reshape(groups, GROUP * rows, lanes)
    rounds = SWEEPS + 1
    out = pl.pallas_call(
        functools.partial(diffuse_kernel, rows),
        in_specs=[VMEM, VMEM],
        out_specs=VMEM,
        out_shape=jax.ShapeDtypeStruct(blocks.shape, jnp.float32),
        scratch_shapes=[
            pltpu.VMEM(blocks.shape, jnp.float32),
            pltpu.VMEM((4, groups, rows, GROUP, lanes), jnp.float32),
            pltpu.VMEM((rounds, 2, groups, GROUP, lanes), jnp.float32),
            pltpu.VMEM((rounds, 2, groups, GROUP, rows), jnp.float32),
            pltpu.VMEM((rounds, 2, groups, GROUP, lanes), jnp.float32),
            pltpu.VMEM((rounds, 2, groups, GROUP, rows), jnp.float32),
            pltpu.SemaphoreType.DMA((rounds, 4)),
            pltpu.SemaphoreType.DMA((rounds, 4)),
        ],
        compiler_params=pltpu.CompilerParams(collective_id=0, has_side_effects=True),
        cost_estimate=pl.CostEstimate(
            flops=50 * field.size, bytes_accessed=12 * field.size, transcendentals=0
        ),
    )(blocks, conduct_blocks)
    return out.reshape(vals, rows, lanes)


def load_row(ref, index):
    return ref[pl.ds(index, 1), :]


def add_row(ref, index, value):
    spot = pl.ds(index, 1)
    ref[spot, :] = ref[spot, :] + value


def select_kernel(index_ref, rows_ref, out_ref):
    cells = rows_ref.shape[0]
    width = out_ref.shape[1]
    sub = lax.broadcasted_iota(jnp.int32, (8, width), 0)

    def body(t, carry):
        tile = jnp.zeros((8, width), jnp.float32)
        for i in range(8):
            source = index_ref[t * 8 + i]
            row = load_row(rows_ref, jnp.minimum(source, cells - 1))
            tile = jnp.where((sub == i) & (source < cells), jnp.broadcast_to(row, (8, width)), tile)
        out_ref[pl.ds(pl.multiple_of(t * 8, 8), 8), :] = tile
        return carry

    lax.fori_loop(0, out_ref.shape[0] // 8, body, 0, unroll=2)


def place_kernel(index_ref, rows_ref, out_ref, *parts):
    cells = out_ref.shape[0]
    for part in parts:
        part[...] = jnp.zeros_like(part)

    def body(t, carry):
        for i, part in enumerate(parts):
            q = t * len(parts) + i
            target = index_ref[q]
            row = load_row(rows_ref, q)
            add_row(part, jnp.minimum(target, cells - 1), jnp.where(target < cells, row, 0.0))
        return carry

    lax.fori_loop(0, rows_ref.shape[0] // len(parts), body, 0, unroll=2)
    total = parts[0][...]
    for part in parts[1:]:
        total = total + part[...]
    out_ref[...] = total


def interp_kernel(slot_ref, weight_ref, received_ref, precision_ref, equiv_ref, returned_ref, *parts):
    taps, obs_count = slot_ref.shape
    width = equiv_ref.shape[1]
    sub = lax.broadcasted_iota(jnp.int32, (8, width), 0)
    for part in parts:
        part[...] = jnp.zeros_like(part)

    def body(t, carry):
        tile = jnp.zeros((8, width), jnp.float32)
        for i in range(8):
            j = t * 8 + i
            slots = [slot_ref[k, j] for k in range(taps)]
            weights = [weight_ref[k, j] for k in range(taps)]
            total = load_row(received_ref, slots[0]) * weights[0]
            for k in range(1, taps):
                total = total + load_row(received_ref, slots[k]) * weights[k]
            tile = jnp.where(sub == i, jnp.broadcast_to(total, (8, width)), tile)
            weighted = load_row(precision_ref, j) * total
            for k in range(taps):
                add_row(parts[(i % 2) * taps + k], slots[k], weighted * weights[k])
        equiv_ref[pl.ds(pl.multiple_of(t * 8, 8), 8), :] = tile
        return carry

    lax.fori_loop(0, obs_count // 8, body, 0)
    total = parts[0][...]
    for part in parts[1:]:
        total = total + part[...]
    returned_ref[...] = total


def select_rows(index, rows, count):
    return pl.pallas_call(
        select_kernel,
        in_specs=[SMEM, VMEM],
        out_specs=VMEM,
        out_shape=jax.ShapeDtypeStruct((count, rows.shape[1]), jnp.float32),
    )(index, rows)


def place_rows(index, rows, cells):
    return pl.pallas_call(
        place_kernel,
        in_specs=[SMEM, VMEM],
        out_specs=VMEM,
        out_shape=jax.ShapeDtypeStruct((cells, rows.shape[1]), jnp.float32),
        scratch_shapes=[pltpu.VMEM((cells, rows.shape[1]), jnp.float32) for _ in range(4)],
        compiler_params=pltpu.CompilerParams(vmem_limit_bytes=60 * 1024 * 1024),
    )(index, rows)


def interpolate(obs_slots, obs_weights, received, precision_rows):
    obs_count = obs_slots.shape[1]
    return pl.pallas_call(
        interp_kernel,
        in_specs=[SMEM, SMEM, VMEM, VMEM],
        out_specs=[VMEM, VMEM],
        out_shape=[
            jax.ShapeDtypeStruct((obs_count, received.shape[1]), jnp.float32),
            jax.ShapeDtypeStruct(received.shape, jnp.float32),
        ],
        scratch_shapes=[
            pltpu.VMEM(received.shape, jnp.float32) for _ in range(2 * obs_slots.shape[0])
        ],
        compiler_params=pltpu.CompilerParams(vmem_limit_bytes=60 * 1024 * 1024),
    )(obs_slots, obs_weights, received, precision_rows)


def to_owners(outgoing):
    return lax.all_to_all(outgoing, ("lon", "lat"), split_axis=0, concat_axis=0, tiled=True)


def to_sources(returned):
    return lax.all_to_all(returned, ("lon", "lat"), split_axis=0, concat_axis=0, tiled=True)


def on_device(state, diffusivity, sea_mask, send_cols, obs_slots, obs_weights, obs_precision):
    vals, rows, lanes = state.shape
    cell_count = rows * lanes
    steps = vals // GROUP
    sea_float = sea_mask.astype(jnp.float32)
    conduct = diffusivity * jnp.concatenate([sea_float, sea_float], axis=0)
    conduct_blocks = conduct.reshape(steps, GROUP * rows, lanes)
    smooth = diffuse(state, conduct_blocks)
    rows_of = smooth.reshape(vals, cell_count).T
    send_index = send_cols[0]
    outgoing = select_rows(send_index, rows_of, send_index.shape[0])
    received = to_owners(outgoing)
    equivalent_rows, returned = interpolate(obs_slots, obs_weights, received, obs_precision.T)
    equivalents = equivalent_rows.T
    incoming = to_sources(returned)
    adjoint_rows = place_rows(send_index, incoming, cell_count)
    adjoint_field = adjoint_rows.T.reshape(state.shape)
    product = state + diffuse(adjoint_field, conduct_blocks)
    return (product, equivalents)


def solution(mesh):
    placed = (
        P(None, "lat", "lon"),
        P(None, "lat", "lon"),
        P(None, "lat", "lon"),
        P(("lon", "lat"), None),
        P(None, ("lon", "lat")),
        P(None, ("lon", "lat")),
        P(None, ("lon", "lat")),
    )
    return jax.shard_map(
        on_device,
        mesh=mesh,
        in_specs=placed,
        out_specs=(P(None, "lat", "lon"), P(None, ("lon", "lat"))),
        check_vma=False,
    )
```

```python
import functools

import jax
import jax.numpy as jnp
from jax import lax
from jax.experimental import pallas as pl
from jax.experimental.pallas import tpu as pltpu
from jax.sharding import PartitionSpec as P

SWEEPS = 2
GROUP = 30
SMEM = pl.BlockSpec(memory_space=pltpu.SMEM)
VMEM = pl.BlockSpec(memory_space=pltpu.VMEM)


def coef_pass(rows, c_ref, coef_halo, scales, k_ref):
    groups, span, lanes = c_ref.shape
    group = span // rows
    north_ok, south_ok = scales
    coef_rows, coef_cols = coef_halo

    def body(g, carry):
        lane = lax.broadcasted_iota(jnp.int32, (group, lanes), 1)
        cw = coef_cols[0, g]
        ce = coef_cols[1, g]
        c_up = coef_rows[0, g] * north_ok
        c_mid = c_ref[g, pl.ds(0, group, stride=rows), :]
        for r in range(rows):
            if r + 1 < rows:
                c_dn = c_ref[g, pl.ds(r + 1, group, stride=rows), :]
            else:
                c_dn = coef_rows[1, g] * south_ok
            c_w = jnp.where(lane == 0, cw[:, r : r + 1], pltpu.roll(c_mid, 1, 1))
            c_e = jnp.where(lane == lanes - 1, ce[:, r : r + 1], pltpu.roll(c_mid, lanes - 1, 1))
            k_ref[0, g, r] = jnp.minimum(c_mid, c_up)
            k_ref[1, g, r] = jnp.minimum(c_mid, c_dn)
            k_ref[2, g, r] = jnp.minimum(c_mid, c_w)
            k_ref[3, g, r] = jnp.minimum(c_mid, c_e)
            c_up, c_mid = c_mid, c_dn
        return carry

    lax.fori_loop(0, groups, body, 0)


def slab_pass(rows, src_ref, k_ref, field_halo, scales, dst_ref, edges):
    groups, span, lanes = src_ref.shape
    group = span // rows
    north_ok, south_ok = scales
    row_halo, col_halo = field_halo

    def body(g, carry):
        lane = lax.broadcasted_iota(jnp.int32, (group, lanes), 1)
        col = lax.broadcasted_iota(jnp.int32, (group, rows), 1)

        def slab(ref, r):
            return ref[g, pl.ds(r, group, stride=rows), :]

        vw = col_halo[0, g]
        ve = col_halo[1, g]
        left = jnp.zeros((group, rows), jnp.float32)
        right = jnp.zeros((group, rows), jnp.float32)
        x_up = row_halo[0, g] * north_ok
        x_mid = slab(src_ref, 0)
        for r in range(rows):
            if r + 1 < rows:
                x_dn = slab(src_ref, r + 1)
            else:
                x_dn = row_halo[1, g] * south_ok
            x_w = jnp.where(lane == 0, vw[:, r : r + 1], pltpu.roll(x_mid, 1, 1))
            x_e = jnp.where(lane == lanes - 1, ve[:, r : r + 1], pltpu.roll(x_mid, lanes - 1, 1))
            total = k_ref[0, g, r] * (x_up - x_mid)
            total = total + k_ref[1, g, r] * (x_dn - x_mid)
            total = total + k_ref[2, g, r] * (x_w - x_mid)
            total = total + k_ref[3, g, r] * (x_e - x_mid)
            out = x_mid + total
            dst_ref[g, pl.ds(r, group, stride=rows), :] = out
            if edges is not None:
                if r == 0:
                    edges[0][0, g] = out
                if r == rows - 1:
                    edges[0][1, g] = out
                left = jnp.where(col == r, out[:, 0:1], left)
                right = jnp.where(col == r, out[:, lanes - 1 : lanes], right)
            x_up, x_mid = x_mid, x_dn
        if edges is not None:
            edges[1][0, g] = left
            edges[1][1, g] = right
        return carry

    lax.fori_loop(0, groups, body, 0)


def edge_pass(rows, src_ref, row_out, col_out):
    groups, span, lanes = src_ref.shape
    group = span // rows

    def body(g, carry):
        col = lax.broadcasted_iota(jnp.int32, (group, rows), 1)
        left = jnp.zeros((group, rows), jnp.float32)
        right = jnp.zeros((group, rows), jnp.float32)
        for r in range(rows):
            x = src_ref[g, pl.ds(r, group, stride=rows), :]
            if r == 0:
                row_out[0, g] = x
            if r == rows - 1:
                row_out[1, g] = x
            left = jnp.where(col == r, x[:, 0:1], left)
            right = jnp.where(col == r, x[:, lanes - 1 : lanes], right)
        col_out[0, g] = left
        col_out[1, g] = right
        return carry

    lax.fori_loop(0, groups, body, 0)


def diffuse_kernel(rows, v_ref, c_ref, out_ref, mid_ref, k_ref, row_edge, col_edge, row_halo,
                   col_halo, send_sem, recv_sem):
    lon = lax.axis_index("lon")
    lat = lax.axis_index("lat")
    n_lon = lax.axis_size("lon")
    n_lat = lax.axis_size("lat")
    north = {"lat": (lat + n_lat - 1) % n_lat}
    south = {"lat": (lat + 1) % n_lat}
    west = {"lon": (lon + n_lon - 1) % n_lon}
    east = {"lon": (lon + 1) % n_lon}
    mesh_id = pl.DeviceIdType.MESH

    barrier = pltpu.get_barrier_semaphore()
    for peer in (north, south, west, east):
        pl.semaphore_signal(barrier, inc=1, device_id=peer, device_id_type=mesh_id)
    pl.semaphore_wait(barrier, 4)

    def exchange(rd):
        plan = [
            (row_edge.at[rd, 0], row_halo.at[rd, 1], north, 0),
            (row_edge.at[rd, 1], row_halo.at[rd, 0], south, 1),
            (col_edge.at[rd, 0], col_halo.at[rd, 1], west, 2),
            (col_edge.at[rd, 1], col_halo.at[rd, 0], east, 3),
        ]
        copies = []
        for src, dst, peer, k in plan:
            copy = pltpu.make_async_remote_copy(
                src_ref=src, dst_ref=dst, send_sem=send_sem.at[rd, k], recv_sem=recv_sem.at[rd, k],
                device_id=peer, device_id_type=mesh_id,
            )
            copy.start()
            copies.append(copy)
        return copies

    edge_pass(rows, c_ref, row_edge.at[0], col_edge.at[0])
    edge_pass(rows, v_ref, row_edge.at[1], col_edge.at[1])
    first = exchange(0) + exchange(1)
    for copy in first:
        copy.wait()
    north_ok = jnp.minimum(lat, 1).astype(jnp.float32)
    south_ok = jnp.minimum(n_lat - 1 - lat, 1).astype(jnp.float32)
    scales = (north_ok, south_ok)
    coef_pass(rows, c_ref, (row_halo.at[0], col_halo.at[0]), scales, k_ref)
    slab_pass(rows, v_ref, k_ref, (row_halo.at[1], col_halo.at[1]), scales, mid_ref,
              (row_edge.at[2], col_edge.at[2]))
    for copy in exchange(2):
        copy.wait()
    slab_pass(rows, mid_ref, k_ref, (row_halo.at[2], col_halo.at[2]), scales, out_ref, None)


def diffuse(field, conduct_blocks):
    vals, rows, lanes = field.shape
    groups = vals // GROUP
    blocks = field.reshape(groups, GROUP * rows, lanes)
    rounds = SWEEPS + 1
    out = pl.pallas_call(
        functools.partial(diffuse_kernel, rows),
        in_specs=[VMEM, VMEM],
        out_specs=VMEM,
        out_shape=jax.ShapeDtypeStruct(blocks.shape, jnp.float32),
        scratch_shapes=[
            pltpu.VMEM(blocks.shape, jnp.float32),
            pltpu.VMEM((4, groups, rows, GROUP, lanes), jnp.float32),
            pltpu.VMEM((rounds, 2, groups, GROUP, lanes), jnp.float32),
            pltpu.VMEM((rounds, 2, groups, GROUP, rows), jnp.float32),
            pltpu.VMEM((rounds, 2, groups, GROUP, lanes), jnp.float32),
            pltpu.VMEM((rounds, 2, groups, GROUP, rows), jnp.float32),
            pltpu.SemaphoreType.DMA((rounds, 4)),
            pltpu.SemaphoreType.DMA((rounds, 4)),
        ],
        compiler_params=pltpu.CompilerParams(collective_id=0, has_side_effects=True),
        cost_estimate=pl.CostEstimate(
            flops=50 * field.size, bytes_accessed=12 * field.size, transcendentals=0
        ),
    )(blocks, conduct_blocks)
    return out.reshape(vals, rows, lanes)


def load_row(ref, index):
    return ref[pl.ds(index, 1), :]


def add_row(ref, index, value):
    spot = pl.ds(index, 1)
    ref[spot, :] = ref[spot, :] + value


def select_kernel(index_ref, rows_ref, out_ref):
    cells = rows_ref.shape[0]
    width = out_ref.shape[1]
    sub = lax.broadcasted_iota(jnp.int32, (8, width), 0)

    def body(t, carry):
        tile = jnp.zeros((8, width), jnp.float32)
        for i in range(8):
            source = index_ref[t * 8 + i]
            row = load_row(rows_ref, jnp.minimum(source, cells - 1))
            tile = jnp.where((sub == i) & (source < cells), jnp.broadcast_to(row, (8, width)), tile)
        out_ref[pl.ds(pl.multiple_of(t * 8, 8), 8), :] = tile
        return carry

    lax.fori_loop(0, out_ref.shape[0] // 8, body, 0, unroll=2)


def place_kernel(index_ref, rows_ref, out_ref, *parts):
    cells = out_ref.shape[0]
    for part in parts:
        part[...] = jnp.zeros_like(part)

    def body(t, carry):
        spots, rows = [], []
        for i in range(len(parts)):
            q = t * len(parts) + i
            target = index_ref[q]
            spots.append(pl.ds(jnp.minimum(target, cells - 1), 1))
            rows.append(jnp.where(target < cells, load_row(rows_ref, q), 0.0))
        sums = [part[spot, :] + row for part, spot, row in zip(parts, spots, rows)]
        for part, spot, value in zip(parts, spots, sums):
            part[spot, :] = value
        return carry

    lax.fori_loop(0, rows_ref.shape[0] // len(parts), body, 0)
    total = parts[0][...]
    for part in parts[1:]:
        total = total + part[...]
    out_ref[...] = total


def interp_kernel(slot_ref, weight_ref, received_ref, precision_ref, equiv_ref, returned_ref, *parts):
    taps, obs_count = slot_ref.shape
    width = equiv_ref.shape[1]
    sub = lax.broadcasted_iota(jnp.int32, (8, width), 0)
    pair = len(parts) // taps
    for part in parts:
        part[...] = jnp.zeros_like(part)

    def body(t, carry):
        slots = [[slot_ref[k, t * 8 + i] for k in range(taps)] for i in range(8)]
        weights = [[weight_ref[k, t * 8 + i] for k in range(taps)] for i in range(8)]
        picked = [[load_row(received_ref, slots[i][k]) for k in range(taps)] for i in range(8)]
        precision = [load_row(precision_ref, t * 8 + i) for i in range(8)]
        tile = jnp.zeros((8, width), jnp.float32)
        weighted = []
        for i in range(8):
            total = picked[i][0] * weights[i][0]
            for k in range(1, taps):
                total = total + picked[i][k] * weights[i][k]
            tile = jnp.where(sub == i, jnp.broadcast_to(total, (8, width)), tile)
            weighted.append(precision[i] * total)
        equiv_ref[pl.ds(pl.multiple_of(t * 8, 8), 8), :] = tile
        for first in range(0, 8, pair):
            batch = [(i, k) for i in range(first, first + pair) for k in range(taps)]
            spots = [pl.ds(slots[i][k], 1) for i, k in batch]
            owners = [parts[(i - first) * taps + k] for i, k in batch]
            sums = [
                owner[spot, :] + weighted[i] * weights[i][k]
                for owner, spot, (i, k) in zip(owners, spots, batch)
            ]
            for owner, spot, value in zip(owners, spots, sums):
                owner[spot, :] = value
        return carry

    lax.fori_loop(0, obs_count // 8, body, 0)
    total = parts[0][...]
    for part in parts[1:]:
        total = total + part[...]
    returned_ref[...] = total


def select_rows(index, rows, count):
    return pl.pallas_call(
        select_kernel,
        in_specs=[SMEM, VMEM],
        out_specs=VMEM,
        out_shape=jax.ShapeDtypeStruct((count, rows.shape[1]), jnp.float32),
    )(index, rows)


def place_rows(index, rows, cells):
    return pl.pallas_call(
        place_kernel,
        in_specs=[SMEM, VMEM],
        out_specs=VMEM,
        out_shape=jax.ShapeDtypeStruct((cells, rows.shape[1]), jnp.float32),
        scratch_shapes=[pltpu.VMEM((cells, rows.shape[1]), jnp.float32) for _ in range(8)],
        compiler_params=pltpu.CompilerParams(vmem_limit_bytes=60 * 1024 * 1024),
    )(index, rows)


def interpolate(obs_slots, obs_weights, received, precision_rows):
    obs_count = obs_slots.shape[1]
    return pl.pallas_call(
        interp_kernel,
        in_specs=[SMEM, SMEM, VMEM, VMEM],
        out_specs=[VMEM, VMEM],
        out_shape=[
            jax.ShapeDtypeStruct((obs_count, received.shape[1]), jnp.float32),
            jax.ShapeDtypeStruct(received.shape, jnp.float32),
        ],
        scratch_shapes=[
            pltpu.VMEM(received.shape, jnp.float32) for _ in range(2 * obs_slots.shape[0])
        ],
        compiler_params=pltpu.CompilerParams(vmem_limit_bytes=60 * 1024 * 1024),
    )(obs_slots, obs_weights, received, precision_rows)


def to_owners(outgoing):
    return lax.all_to_all(outgoing, ("lon", "lat"), split_axis=0, concat_axis=0, tiled=True)


def to_sources(returned):
    return lax.all_to_all(returned, ("lon", "lat"), split_axis=0, concat_axis=0, tiled=True)


def on_device(state, diffusivity, sea_mask, send_cols, obs_slots, obs_weights, obs_precision):
    vals, rows, lanes = state.shape
    cell_count = rows * lanes
    steps = vals // GROUP
    sea_float = sea_mask.astype(jnp.float32)
    conduct = diffusivity * jnp.concatenate([sea_float, sea_float], axis=0)
    conduct_blocks = conduct.reshape(steps, GROUP * rows, lanes)
    smooth = diffuse(state, conduct_blocks)
    rows_of = smooth.reshape(vals, cell_count).T
    send_index = send_cols[0]
    outgoing = select_rows(send_index, rows_of, send_index.shape[0])
    received = to_owners(outgoing)
    equivalent_rows, returned = interpolate(obs_slots, obs_weights, received, obs_precision.T)
    equivalents = equivalent_rows.T
    incoming = to_sources(returned)
    adjoint_rows = place_rows(send_index, incoming, cell_count)
    adjoint_field = adjoint_rows.T.reshape(state.shape)
    product = state + diffuse(adjoint_field, conduct_blocks)
    return (product, equivalents)


def solution(mesh):
    placed = (
        P(None, "lat", "lon"),
        P(None, "lat", "lon"),
        P(None, "lat", "lon"),
        P(("lon", "lat"), None),
        P(None, ("lon", "lat")),
        P(None, ("lon", "lat")),
        P(None, ("lon", "lat")),
    )
    return jax.shard_map(
        on_device,
        mesh=mesh,
        in_specs=placed,
        out_specs=(P(None, "lat", "lon"), P(None, ("lon", "lat"))),
        check_vma=False,
    )
```

```python
import functools

import jax
import jax.numpy as jnp
from jax import lax
from jax.experimental import pallas as pl
from jax.experimental.pallas import tpu as pltpu
from jax.sharding import PartitionSpec as P

SWEEPS = 2
GROUP = 30
SMEM = pl.BlockSpec(memory_space=pltpu.SMEM)
VMEM = pl.BlockSpec(memory_space=pltpu.VMEM)


def coef_pass(rows, c_ref, coef_halo, scales, k_ref):
    groups, span, lanes = c_ref.shape
    group = span // rows
    north_ok, south_ok = scales
    coef_rows, coef_cols = coef_halo

    def body(g, carry):
        lane = lax.broadcasted_iota(jnp.int32, (group, lanes), 1)
        cw = coef_cols[0, g]
        ce = coef_cols[1, g]
        c_up = coef_rows[0, g] * north_ok
        c_mid = c_ref[g, pl.ds(0, group, stride=rows), :]
        for r in range(rows):
            if r + 1 < rows:
                c_dn = c_ref[g, pl.ds(r + 1, group, stride=rows), :]
            else:
                c_dn = coef_rows[1, g] * south_ok
            c_w = jnp.where(lane == 0, cw[:, r : r + 1], pltpu.roll(c_mid, 1, 1))
            c_e = jnp.where(lane == lanes - 1, ce[:, r : r + 1], pltpu.roll(c_mid, lanes - 1, 1))
            k_ref[0, g, r] = jnp.minimum(c_mid, c_up)
            k_ref[1, g, r] = jnp.minimum(c_mid, c_dn)
            k_ref[2, g, r] = jnp.minimum(c_mid, c_w)
            k_ref[3, g, r] = jnp.minimum(c_mid, c_e)
            c_up, c_mid = c_mid, c_dn
        return carry

    lax.fori_loop(0, groups, body, 0)


def slab_pass(rows, src_ref, k_ref, field_halo, scales, dst_ref, edges):
    groups, span, lanes = src_ref.shape
    group = span // rows
    north_ok, south_ok = scales
    row_halo, col_halo = field_halo

    def body(g, carry):
        lane = lax.broadcasted_iota(jnp.int32, (group, lanes), 1)
        col = lax.broadcasted_iota(jnp.int32, (group, rows), 1)

        def slab(ref, r):
            return ref[g, pl.ds(r, group, stride=rows), :]

        vw = col_halo[0, g]
        ve = col_halo[1, g]
        left = jnp.zeros((group, rows), jnp.float32)
        right = jnp.zeros((group, rows), jnp.float32)
        x_up = row_halo[0, g] * north_ok
        x_mid = slab(src_ref, 0)
        for r in range(rows):
            if r + 1 < rows:
                x_dn = slab(src_ref, r + 1)
            else:
                x_dn = row_halo[1, g] * south_ok
            x_w = jnp.where(lane == 0, vw[:, r : r + 1], pltpu.roll(x_mid, 1, 1))
            x_e = jnp.where(lane == lanes - 1, ve[:, r : r + 1], pltpu.roll(x_mid, lanes - 1, 1))
            total = k_ref[0, g, r] * (x_up - x_mid)
            total = total + k_ref[1, g, r] * (x_dn - x_mid)
            total = total + k_ref[2, g, r] * (x_w - x_mid)
            total = total + k_ref[3, g, r] * (x_e - x_mid)
            out = x_mid + total
            dst_ref[g, pl.ds(r, group, stride=rows), :] = out
            if edges is not None:
                if r == 0:
                    edges[0][0, g] = out
                if r == rows - 1:
                    edges[0][1, g] = out
                left = jnp.where(col == r, out[:, 0:1], left)
                right = jnp.where(col == r, out[:, lanes - 1 : lanes], right)
            x_up, x_mid = x_mid, x_dn
        if edges is not None:
            edges[1][0, g] = left
            edges[1][1, g] = right
        return carry

    lax.fori_loop(0, groups, body, 0)


def edge_pass(rows, src_ref, row_out, col_out):
    groups, span, lanes = src_ref.shape
    group = span // rows

    def body(g, carry):
        col = lax.broadcasted_iota(jnp.int32, (group, rows), 1)
        left = jnp.zeros((group, rows), jnp.float32)
        right = jnp.zeros((group, rows), jnp.float32)
        for r in range(rows):
            x = src_ref[g, pl.ds(r, group, stride=rows), :]
            if r == 0:
                row_out[0, g] = x
            if r == rows - 1:
                row_out[1, g] = x
            left = jnp.where(col == r, x[:, 0:1], left)
            right = jnp.where(col == r, x[:, lanes - 1 : lanes], right)
        col_out[0, g] = left
        col_out[1, g] = right
        return carry

    lax.fori_loop(0, groups, body, 0)


def diffuse_kernel(rows, v_ref, c_ref, out_ref, mid_ref, k_ref, row_edge, col_edge, row_halo,
                   col_halo, send_sem, recv_sem):
    lon = lax.axis_index("lon")
    lat = lax.axis_index("lat")
    n_lon = lax.axis_size("lon")
    n_lat = lax.axis_size("lat")
    north = {"lat": (lat + n_lat - 1) % n_lat}
    south = {"lat": (lat + 1) % n_lat}
    west = {"lon": (lon + n_lon - 1) % n_lon}
    east = {"lon": (lon + 1) % n_lon}
    mesh_id = pl.DeviceIdType.MESH

    barrier = pltpu.get_barrier_semaphore()
    for peer in (north, south, west, east):
        pl.semaphore_signal(barrier, inc=1, device_id=peer, device_id_type=mesh_id)
    pl.semaphore_wait(barrier, 4)

    def exchange(rd):
        plan = [
            (row_edge.at[rd, 0], row_halo.at[rd, 1], north, 0),
            (row_edge.at[rd, 1], row_halo.at[rd, 0], south, 1),
            (col_edge.at[rd, 0], col_halo.at[rd, 1], west, 2),
            (col_edge.at[rd, 1], col_halo.at[rd, 0], east, 3),
        ]
        copies = []
        for src, dst, peer, k in plan:
            copy = pltpu.make_async_remote_copy(
                src_ref=src, dst_ref=dst, send_sem=send_sem.at[rd, k], recv_sem=recv_sem.at[rd, k],
                device_id=peer, device_id_type=mesh_id,
            )
            copy.start()
            copies.append(copy)
        return copies

    edge_pass(rows, c_ref, row_edge.at[0], col_edge.at[0])
    edge_pass(rows, v_ref, row_edge.at[1], col_edge.at[1])
    first = exchange(0) + exchange(1)
    for copy in first:
        copy.wait()
    north_ok = jnp.minimum(lat, 1).astype(jnp.float32)
    south_ok = jnp.minimum(n_lat - 1 - lat, 1).astype(jnp.float32)
    scales = (north_ok, south_ok)
    coef_pass(rows, c_ref, (row_halo.at[0], col_halo.at[0]), scales, k_ref)
    slab_pass(rows, v_ref, k_ref, (row_halo.at[1], col_halo.at[1]), scales, mid_ref,
              (row_edge.at[2], col_edge.at[2]))
    for copy in exchange(2):
        copy.wait()
    slab_pass(rows, mid_ref, k_ref, (row_halo.at[2], col_halo.at[2]), scales, out_ref, None)


def diffuse(field, conduct_blocks):
    vals, rows, lanes = field.shape
    groups = vals // GROUP
    blocks = field.reshape(groups, GROUP * rows, lanes)
    rounds = SWEEPS + 1
    out = pl.pallas_call(
        functools.partial(diffuse_kernel, rows),
        in_specs=[VMEM, VMEM],
        out_specs=VMEM,
        out_shape=jax.ShapeDtypeStruct(blocks.shape, jnp.float32),
        scratch_shapes=[
            pltpu.VMEM(blocks.shape, jnp.float32),
            pltpu.VMEM((4, groups, rows, GROUP, lanes), jnp.float32),
            pltpu.VMEM((rounds, 2, groups, GROUP, lanes), jnp.float32),
            pltpu.VMEM((rounds, 2, groups, GROUP, rows), jnp.float32),
            pltpu.VMEM((rounds, 2, groups, GROUP, lanes), jnp.float32),
            pltpu.VMEM((rounds, 2, groups, GROUP, rows), jnp.float32),
            pltpu.SemaphoreType.DMA((rounds, 4)),
            pltpu.SemaphoreType.DMA((rounds, 4)),
        ],
        compiler_params=pltpu.CompilerParams(collective_id=0, has_side_effects=True),
        cost_estimate=pl.CostEstimate(
            flops=50 * field.size, bytes_accessed=12 * field.size, transcendentals=0
        ),
    )(blocks, conduct_blocks)
    return out.reshape(vals, rows, lanes)


def load_row(ref, index):
    return ref[pl.ds(index, 1), :]


def add_row(ref, index, value):
    spot = pl.ds(index, 1)
    ref[spot, :] = ref[spot, :] + value


def select_kernel(index_ref, rows_ref, out_ref):
    cells = rows_ref.shape[0]
    width = out_ref.shape[1]
    sub = lax.broadcasted_iota(jnp.int32, (8, width), 0)

    def body(t, carry):
        tile = jnp.zeros((8, width), jnp.float32)
        for i in range(8):
            source = index_ref[t * 8 + i]
            row = load_row(rows_ref, jnp.minimum(source, cells - 1))
            tile = jnp.where((sub == i) & (source < cells), jnp.broadcast_to(row, (8, width)), tile)
        out_ref[pl.ds(pl.multiple_of(t * 8, 8), 8), :] = tile
        return carry

    lax.fori_loop(0, out_ref.shape[0] // 8, body, 0, unroll=2)


def place_kernel(index_ref, rows_ref, out_ref, *parts):
    cells = out_ref.shape[0]
    for part in parts:
        part[...] = jnp.zeros_like(part)

    def body(t, carry):
        for i, part in enumerate(parts):
            q = t * len(parts) + i
            target = index_ref[q]
            row = load_row(rows_ref, q)
            add_row(part, jnp.minimum(target, cells - 1), jnp.where(target < cells, row, 0.0))
        return carry

    lax.fori_loop(0, rows_ref.shape[0] // len(parts), body, 0, unroll=2)
    total = parts[0][...]
    for part in parts[1:]:
        total = total + part[...]
    out_ref[...] = total


def interp_kernel(slot_ref, weight_ref, received_ref, precision_ref, equiv_ref, returned_ref, *parts):
    taps, obs_count = slot_ref.shape
    width = equiv_ref.shape[1]
    sub = lax.broadcasted_iota(jnp.int32, (8, width), 0)
    for part in parts:
        part[...] = jnp.zeros_like(part)

    def body(t, carry):
        tile = jnp.zeros((8, width), jnp.float32)
        for i in range(8):
            j = t * 8 + i
            slots = [slot_ref[k, j] for k in range(taps)]
            weights = [weight_ref[k, j] for k in range(taps)]
            total = load_row(received_ref, slots[0]) * weights[0]
            for k in range(1, taps):
                total = total + load_row(received_ref, slots[k]) * weights[k]
            tile = jnp.where(sub == i, jnp.broadcast_to(total, (8, width)), tile)
            weighted = load_row(precision_ref, j) * total
            for k in range(taps):
                add_row(parts[(i % 2) * taps + k], slots[k], weighted * weights[k])
        equiv_ref[pl.ds(pl.multiple_of(t * 8, 8), 8), :] = tile
        return carry

    lax.fori_loop(0, obs_count // 8, body, 0)
    total = parts[0][...]
    for part in parts[1:]:
        total = total + part[...]
    returned_ref[...] = total


def select_rows(index, rows, count):
    return pl.pallas_call(
        select_kernel,
        in_specs=[SMEM, VMEM],
        out_specs=VMEM,
        out_shape=jax.ShapeDtypeStruct((count, rows.shape[1]), jnp.float32),
    )(index, rows)


def place_rows(index, rows, cells):
    return pl.pallas_call(
        place_kernel,
        in_specs=[SMEM, VMEM],
        out_specs=VMEM,
        out_shape=jax.ShapeDtypeStruct((cells, rows.shape[1]), jnp.float32),
        scratch_shapes=[pltpu.VMEM((cells, rows.shape[1]), jnp.float32) for _ in range(4)],
        compiler_params=pltpu.CompilerParams(vmem_limit_bytes=60 * 1024 * 1024),
    )(index, rows)


def interpolate(obs_slots, obs_weights, received, precision_rows):
    obs_count = obs_slots.shape[1]
    return pl.pallas_call(
        interp_kernel,
        in_specs=[SMEM, SMEM, VMEM, VMEM],
        out_specs=[VMEM, VMEM],
        out_shape=[
            jax.ShapeDtypeStruct((obs_count, received.shape[1]), jnp.float32),
            jax.ShapeDtypeStruct(received.shape, jnp.float32),
        ],
        scratch_shapes=[
            pltpu.VMEM(received.shape, jnp.float32) for _ in range(2 * obs_slots.shape[0])
        ],
        compiler_params=pltpu.CompilerParams(vmem_limit_bytes=60 * 1024 * 1024),
    )(obs_slots, obs_weights, received, precision_rows)


def to_owners(outgoing):
    return lax.all_to_all(outgoing, ("lon", "lat"), split_axis=0, concat_axis=0, tiled=True)


def to_sources(returned):
    return lax.all_to_all(returned, ("lon", "lat"), split_axis=0, concat_axis=0, tiled=True)


def on_device(state, diffusivity, sea_mask, send_cols, obs_slots, obs_weights, obs_precision):
    vals, rows, lanes = state.shape
    cell_count = rows * lanes
    steps = vals // GROUP
    sea_float = sea_mask.astype(jnp.float32)
    conduct = diffusivity * jnp.concatenate([sea_float, sea_float], axis=0)
    conduct_blocks = conduct.reshape(steps, GROUP * rows, lanes)
    smooth = diffuse(state, conduct_blocks)
    rows_of = smooth.transpose(1, 2, 0).reshape(cell_count, vals)
    send_index = send_cols[0]
    outgoing = select_rows(send_index, rows_of, send_index.shape[0])
    received = to_owners(outgoing)
    equivalent_rows, returned = interpolate(obs_slots, obs_weights, received, obs_precision.T)
    equivalents = equivalent_rows.T
    incoming = to_sources(returned)
    adjoint_rows = place_rows(send_index, incoming, cell_count)
    adjoint_field = adjoint_rows.reshape(rows, lanes, vals).transpose(2, 0, 1)
    product = state + diffuse(adjoint_field, conduct_blocks)
    return (product, equivalents)


def solution(mesh):
    placed = (
        P(None, "lat", "lon"),
        P(None, "lat", "lon"),
        P(None, "lat", "lon"),
        P(("lon", "lat"), None),
        P(None, ("lon", "lat")),
        P(None, ("lon", "lat")),
        P(None, ("lon", "lat")),
    )
    return jax.shard_map(
        on_device,
        mesh=mesh,
        in_specs=placed,
        out_specs=(P(None, "lat", "lon"), P(None, ("lon", "lat"))),
        check_vma=False,
    )
```

```python
import functools

import jax
import jax.numpy as jnp
from jax import lax
from jax.experimental import pallas as pl
from jax.experimental.pallas import tpu as pltpu
from jax.sharding import PartitionSpec as P

SWEEPS = 2
GROUP = 30
SMEM = pl.BlockSpec(memory_space=pltpu.SMEM)
VMEM = pl.BlockSpec(memory_space=pltpu.VMEM)


def coef_pass(rows, c_ref, coef_halo, scales, k_ref):
    groups, span, lanes = c_ref.shape
    group = span // rows
    north_ok, south_ok = scales
    coef_rows, coef_cols = coef_halo

    def body(g, carry):
        lane = lax.broadcasted_iota(jnp.int32, (group, lanes), 1)
        cw = coef_cols[0, g]
        ce = coef_cols[1, g]
        c_up = coef_rows[0, g] * north_ok
        c_mid = c_ref[g, pl.ds(0, group, stride=rows), :]
        for r in range(rows):
            if r + 1 < rows:
                c_dn = c_ref[g, pl.ds(r + 1, group, stride=rows), :]
            else:
                c_dn = coef_rows[1, g] * south_ok
            c_w = jnp.where(lane == 0, cw[:, r : r + 1], pltpu.roll(c_mid, 1, 1))
            c_e = jnp.where(lane == lanes - 1, ce[:, r : r + 1], pltpu.roll(c_mid, lanes - 1, 1))
            k_ref[0, g, r] = jnp.minimum(c_mid, c_up)
            k_ref[1, g, r] = jnp.minimum(c_mid, c_dn)
            k_ref[2, g, r] = jnp.minimum(c_mid, c_w)
            k_ref[3, g, r] = jnp.minimum(c_mid, c_e)
            c_up, c_mid = c_mid, c_dn
        return carry

    lax.fori_loop(0, groups, body, 0)


def slab_pass(rows, src_ref, k_ref, field_halo, scales, dst_ref, edges):
    groups, span, lanes = src_ref.shape
    group = span // rows
    north_ok, south_ok = scales
    row_halo, col_halo = field_halo

    def body(g, carry):
        lane = lax.broadcasted_iota(jnp.int32, (group, lanes), 1)
        col = lax.broadcasted_iota(jnp.int32, (group, rows), 1)

        def slab(ref, r):
            return ref[g, pl.ds(r, group, stride=rows), :]

        vw = col_halo[0, g]
        ve = col_halo[1, g]
        left = jnp.zeros((group, rows), jnp.float32)
        right = jnp.zeros((group, rows), jnp.float32)
        x_up = row_halo[0, g] * north_ok
        x_mid = slab(src_ref, 0)
        for r in range(rows):
            if r + 1 < rows:
                x_dn = slab(src_ref, r + 1)
            else:
                x_dn = row_halo[1, g] * south_ok
            x_w = jnp.where(lane == 0, vw[:, r : r + 1], pltpu.roll(x_mid, 1, 1))
            x_e = jnp.where(lane == lanes - 1, ve[:, r : r + 1], pltpu.roll(x_mid, lanes - 1, 1))
            total = k_ref[0, g, r] * (x_up - x_mid)
            total = total + k_ref[1, g, r] * (x_dn - x_mid)
            total = total + k_ref[2, g, r] * (x_w - x_mid)
            total = total + k_ref[3, g, r] * (x_e - x_mid)
            out = x_mid + total
            dst_ref[g, pl.ds(r, group, stride=rows), :] = out
            if edges is not None:
                if r == 0:
                    edges[0][0, g] = out
                if r == rows - 1:
                    edges[0][1, g] = out
                left = jnp.where(col == r, out[:, 0:1], left)
                right = jnp.where(col == r, out[:, lanes - 1 : lanes], right)
            x_up, x_mid = x_mid, x_dn
        if edges is not None:
            edges[1][0, g] = left
            edges[1][1, g] = right
        return carry

    lax.fori_loop(0, groups, body, 0)


def edge_pass(rows, src_ref, row_out, col_out):
    groups, span, lanes = src_ref.shape
    group = span // rows

    def body(g, carry):
        col = lax.broadcasted_iota(jnp.int32, (group, rows), 1)
        left = jnp.zeros((group, rows), jnp.float32)
        right = jnp.zeros((group, rows), jnp.float32)
        for r in range(rows):
            x = src_ref[g, pl.ds(r, group, stride=rows), :]
            if r == 0:
                row_out[0, g] = x
            if r == rows - 1:
                row_out[1, g] = x
            left = jnp.where(col == r, x[:, 0:1], left)
            right = jnp.where(col == r, x[:, lanes - 1 : lanes], right)
        col_out[0, g] = left
        col_out[1, g] = right
        return carry

    lax.fori_loop(0, groups, body, 0)


def exchanger(row_edge, col_edge, row_halo, col_halo, send_sem, recv_sem):
    lon = lax.axis_index("lon")
    lat = lax.axis_index("lat")
    n_lon = lax.axis_size("lon")
    n_lat = lax.axis_size("lat")
    north = {"lat": (lat + n_lat - 1) % n_lat}
    south = {"lat": (lat + 1) % n_lat}
    west = {"lon": (lon + n_lon - 1) % n_lon}
    east = {"lon": (lon + 1) % n_lon}
    mesh_id = pl.DeviceIdType.MESH

    barrier = pltpu.get_barrier_semaphore()
    for peer in (north, south, west, east):
        pl.semaphore_signal(barrier, inc=1, device_id=peer, device_id_type=mesh_id)
    pl.semaphore_wait(barrier, 4)

    def exchange(rd):
        plan = [
            (row_edge.at[rd, 0], row_halo.at[rd, 1], north, 0),
            (row_edge.at[rd, 1], row_halo.at[rd, 0], south, 1),
            (col_edge.at[rd, 0], col_halo.at[rd, 1], west, 2),
            (col_edge.at[rd, 1], col_halo.at[rd, 0], east, 3),
        ]
        copies = []
        for src, dst, peer, k in plan:
            copy = pltpu.make_async_remote_copy(
                src_ref=src, dst_ref=dst, send_sem=send_sem.at[rd, k], recv_sem=recv_sem.at[rd, k],
                device_id=peer, device_id_type=mesh_id,
            )
            copy.start()
            copies.append(copy)
        return copies

    north_ok = jnp.minimum(lat, 1).astype(jnp.float32)
    south_ok = jnp.minimum(n_lat - 1 - lat, 1).astype(jnp.float32)
    return exchange, (north_ok, south_ok)


def diffuse_kernel(rows, v_ref, c_ref, out_ref, mid_ref, k_ref, row_edge, col_edge, row_halo,
                   col_halo, send_sem, recv_sem):
    exchange, scales = exchanger(row_edge, col_edge, row_halo, col_halo, send_sem, recv_sem)
    edge_pass(rows, c_ref, row_edge.at[0], col_edge.at[0])
    edge_pass(rows, v_ref, row_edge.at[1], col_edge.at[1])
    for copy in exchange(0) + exchange(1):
        copy.wait()
    coef_pass(rows, c_ref, (row_halo.at[0], col_halo.at[0]), scales, k_ref)
    sweeps(rows, v_ref, k_ref, out_ref, mid_ref, row_edge, col_edge, row_halo, col_halo, exchange,
           scales)


def sweeps(rows, v_ref, k_ref, out_ref, mid_ref, row_edge, col_edge, row_halo, col_halo, exchange,
           scales):
    slab_pass(rows, v_ref, k_ref, (row_halo.at[1], col_halo.at[1]), scales, mid_ref,
              (row_edge.at[2], col_edge.at[2]))
    for copy in exchange(2):
        copy.wait()
    slab_pass(rows, mid_ref, k_ref, (row_halo.at[2], col_halo.at[2]), scales, out_ref, None)


def sweep_kernel(rows, v_ref, k_ref, out_ref, mid_ref, row_edge, col_edge, row_halo, col_halo,
                 send_sem, recv_sem):
    exchange, scales = exchanger(row_edge, col_edge, row_halo, col_halo, send_sem, recv_sem)
    edge_pass(rows, v_ref, row_edge.at[1], col_edge.at[1])
    for copy in exchange(1):
        copy.wait()
    sweeps(rows, v_ref, k_ref, out_ref, mid_ref, row_edge, col_edge, row_halo, col_halo, exchange,
           scales)


def coef_kernel(rows, c_ref, anchor_ref, k_ref, row_edge, col_edge, row_halo, col_halo, send_sem,
                recv_sem):
    del anchor_ref
    exchange, scales = exchanger(row_edge, col_edge, row_halo, col_halo, send_sem, recv_sem)
    edge_pass(rows, c_ref, row_edge.at[0], col_edge.at[0])
    for copy in exchange(0):
        copy.wait()
    coef_pass(rows, c_ref, (row_halo.at[0], col_halo.at[0]), scales, k_ref)


def halo_scratch(groups, rows, lanes):
    rounds = SWEEPS + 1
    return [
        pltpu.VMEM((rounds, 2, groups, GROUP, lanes), jnp.float32),
        pltpu.VMEM((rounds, 2, groups, GROUP, rows), jnp.float32),
        pltpu.VMEM((rounds, 2, groups, GROUP, lanes), jnp.float32),
        pltpu.VMEM((rounds, 2, groups, GROUP, rows), jnp.float32),
        pltpu.SemaphoreType.DMA((rounds, 4)),
        pltpu.SemaphoreType.DMA((rounds, 4)),
    ]


def diffuse(field, conduct_blocks):
    vals, rows, lanes = field.shape
    groups = vals // GROUP
    blocks = field.reshape(groups, GROUP * rows, lanes)
    out = pl.pallas_call(
        functools.partial(diffuse_kernel, rows),
        in_specs=[VMEM, VMEM],
        out_specs=VMEM,
        out_shape=jax.ShapeDtypeStruct(blocks.shape, jnp.float32),
        scratch_shapes=[
            pltpu.VMEM(blocks.shape, jnp.float32),
            pltpu.VMEM((4, groups, rows, GROUP, lanes), jnp.float32),
        ]
        + halo_scratch(groups, rows, lanes),
        compiler_params=pltpu.CompilerParams(collective_id=0, has_side_effects=True),
        cost_estimate=pl.CostEstimate(
            flops=50 * field.size, bytes_accessed=12 * field.size, transcendentals=0
        ),
    )(blocks, conduct_blocks)
    return out.reshape(vals, rows, lanes)


def coefficients(conduct_blocks, anchor, rows):
    groups, span, lanes = conduct_blocks.shape
    return pl.pallas_call(
        functools.partial(coef_kernel, rows),
        in_specs=[VMEM, VMEM],
        out_specs=VMEM,
        out_shape=jax.ShapeDtypeStruct((4, groups, rows, GROUP, lanes), jnp.float32),
        scratch_shapes=halo_scratch(groups, rows, lanes),
        compiler_params=pltpu.CompilerParams(collective_id=1, has_side_effects=True),
        cost_estimate=pl.CostEstimate(
            flops=10 * conduct_blocks.size, bytes_accessed=20 * conduct_blocks.size,
            transcendentals=0,
        ),
    )(conduct_blocks, anchor)


def diffuse_with(field, coef):
    vals, rows, lanes = field.shape
    groups = vals // GROUP
    blocks = field.reshape(groups, GROUP * rows, lanes)
    out = pl.pallas_call(
        functools.partial(sweep_kernel, rows),
        in_specs=[VMEM, VMEM],
        out_specs=VMEM,
        out_shape=jax.ShapeDtypeStruct(blocks.shape, jnp.float32),
        scratch_shapes=[pltpu.VMEM(blocks.shape, jnp.float32)] + halo_scratch(groups, rows, lanes),
        compiler_params=pltpu.CompilerParams(collective_id=2, has_side_effects=True),
        cost_estimate=pl.CostEstimate(
            flops=40 * field.size, bytes_accessed=24 * field.size, transcendentals=0
        ),
    )(blocks, coef)
    return out.reshape(vals, rows, lanes)


def load_row(ref, index):
    return ref[pl.ds(index, 1), :]


def add_row(ref, index, value):
    spot = pl.ds(index, 1)
    ref[spot, :] = ref[spot, :] + value


def select_kernel(index_ref, rows_ref, out_ref):
    cells = rows_ref.shape[0]
    width = out_ref.shape[1]
    sub = lax.broadcasted_iota(jnp.int32, (8, width), 0)

    def body(t, carry):
        tile = jnp.zeros((8, width), jnp.float32)
        for i in range(8):
            source = index_ref[t * 8 + i]
            row = load_row(rows_ref, jnp.minimum(source, cells - 1))
            tile = jnp.where((sub == i) & (source < cells), jnp.broadcast_to(row, (8, width)), tile)
        out_ref[pl.ds(pl.multiple_of(t * 8, 8), 8), :] = tile
        return carry

    lax.fori_loop(0, out_ref.shape[0] // 8, body, 0, unroll=2)


def place_kernel(index_ref, rows_ref, out_ref, *parts):
    cells = out_ref.shape[0]
    for part in parts:
        part[...] = jnp.zeros_like(part)

    def body(t, carry):
        for i, part in enumerate(parts):
            q = t * len(parts) + i
            target = index_ref[q]
            row = load_row(rows_ref, q)
            add_row(part, jnp.minimum(target, cells - 1), jnp.where(target < cells, row, 0.0))
        return carry

    lax.fori_loop(0, rows_ref.shape[0] // len(parts), body, 0, unroll=2)
    total = parts[0][...]
    for part in parts[1:]:
        total = total + part[...]
    out_ref[...] = total


def interp_kernel(slot_ref, weight_ref, received_ref, precision_ref, equiv_ref, returned_ref, *parts):
    taps, obs_count = slot_ref.shape
    width = equiv_ref.shape[1]
    sub = lax.broadcasted_iota(jnp.int32, (8, width), 0)
    for part in parts:
        part[...] = jnp.zeros_like(part)

    def body(t, carry):
        tile = jnp.zeros((8, width), jnp.float32)
        for i in range(8):
            j = t * 8 + i
            slots = [slot_ref[k, j] for k in range(taps)]
            weights = [weight_ref[k, j] for k in range(taps)]
            total = load_row(received_ref, slots[0]) * weights[0]
            for k in range(1, taps):
                total = total + load_row(received_ref, slots[k]) * weights[k]
            tile = jnp.where(sub == i, jnp.broadcast_to(total, (8, width)), tile)
            weighted = load_row(precision_ref, j) * total
            for k in range(taps):
                add_row(parts[(i % 2) * taps + k], slots[k], weighted * weights[k])
        equiv_ref[pl.ds(pl.multiple_of(t * 8, 8), 8), :] = tile
        return carry

    lax.fori_loop(0, obs_count // 8, body, 0)
    total = parts[0][...]
    for part in parts[1:]:
        total = total + part[...]
    returned_ref[...] = total


def select_rows(index, rows, count):
    return pl.pallas_call(
        select_kernel,
        in_specs=[SMEM, VMEM],
        out_specs=VMEM,
        out_shape=jax.ShapeDtypeStruct((count, rows.shape[1]), jnp.float32),
    )(index, rows)


def place_rows(index, rows, cells):
    return pl.pallas_call(
        place_kernel,
        in_specs=[SMEM, VMEM],
        out_specs=VMEM,
        out_shape=jax.ShapeDtypeStruct((cells, rows.shape[1]), jnp.float32),
        scratch_shapes=[pltpu.VMEM((cells, rows.shape[1]), jnp.float32) for _ in range(4)],
        compiler_params=pltpu.CompilerParams(vmem_limit_bytes=60 * 1024 * 1024),
    )(index, rows)


def interpolate(obs_slots, obs_weights, received, precision_rows):
    obs_count = obs_slots.shape[1]
    return pl.pallas_call(
        interp_kernel,
        in_specs=[SMEM, SMEM, VMEM, VMEM],
        out_specs=[VMEM, VMEM],
        out_shape=[
            jax.ShapeDtypeStruct((obs_count, received.shape[1]), jnp.float32),
            jax.ShapeDtypeStruct(received.shape, jnp.float32),
        ],
        scratch_shapes=[
            pltpu.VMEM(received.shape, jnp.float32) for _ in range(2 * obs_slots.shape[0])
        ],
        compiler_params=pltpu.CompilerParams(vmem_limit_bytes=60 * 1024 * 1024),
    )(obs_slots, obs_weights, received, precision_rows)


def to_owners(outgoing):
    return lax.all_to_all(outgoing, ("lon", "lat"), split_axis=0, concat_axis=0, tiled=True)


def to_sources(returned):
    return lax.all_to_all(returned, ("lon", "lat"), split_axis=0, concat_axis=0, tiled=True)


def on_device(state, diffusivity, sea_mask, send_cols, obs_slots, obs_weights, obs_precision):
    vals, rows, lanes = state.shape
    cell_count = rows * lanes
    steps = vals // GROUP
    sea_float = sea_mask.astype(jnp.float32)
    conduct = diffusivity * jnp.concatenate([sea_float, sea_float], axis=0)
    conduct_blocks = conduct.reshape(steps, GROUP * rows, lanes)
    smooth = diffuse(state, conduct_blocks)
    rows_of = smooth.transpose(1, 2, 0).reshape(cell_count, vals)
    send_index = send_cols[0]
    outgoing = select_rows(send_index, rows_of, send_index.shape[0])
    received = to_owners(outgoing)
    equivalent_rows, returned = interpolate(obs_slots, obs_weights, received, obs_precision.T)
    equivalents = equivalent_rows.T
    coef = coefficients(conduct_blocks, returned[:8, :], rows)
    incoming = to_sources(returned)
    adjoint_rows = place_rows(send_index, incoming, cell_count)
    adjoint_field = adjoint_rows.reshape(rows, lanes, vals).transpose(2, 0, 1)
    product = state + diffuse_with(adjoint_field, coef)
    return (product, equivalents)


def solution(mesh):
    placed = (
        P(None, "lat", "lon"),
        P(None, "lat", "lon"),
        P(None, "lat", "lon"),
        P(("lon", "lat"), None),
        P(None, ("lon", "lat")),
        P(None, ("lon", "lat")),
        P(None, ("lon", "lat")),
    )
    return jax.shard_map(
        on_device,
        mesh=mesh,
        in_specs=placed,
        out_specs=(P(None, "lat", "lon"), P(None, ("lon", "lat"))),
        check_vma=False,
    )
```

```python
import functools

import jax
import jax.numpy as jnp
from jax import lax
from jax.experimental import pallas as pl
from jax.experimental.pallas import tpu as pltpu
from jax.sharding import PartitionSpec as P

SWEEPS = 2
GROUP = 30
SMEM = pl.BlockSpec(memory_space=pltpu.SMEM)
VMEM = pl.BlockSpec(memory_space=pltpu.VMEM)


def coef_pass(rows, c_ref, coef_halo, scales, k_ref):
    groups, span, lanes = c_ref.shape
    group = span // rows
    north_ok, south_ok = scales
    coef_rows, coef_cols = coef_halo

    def body(g, carry):
        lane = lax.broadcasted_iota(jnp.int32, (group, lanes), 1)
        cw = coef_cols[0, g]
        ce = coef_cols[1, g]
        c_up = coef_rows[0, g] * north_ok
        c_mid = c_ref[g, pl.ds(0, group, stride=rows), :]
        for r in range(rows):
            if r + 1 < rows:
                c_dn = c_ref[g, pl.ds(r + 1, group, stride=rows), :]
            else:
                c_dn = coef_rows[1, g] * south_ok
            c_w = jnp.where(lane == 0, cw[:, r : r + 1], pltpu.roll(c_mid, 1, 1))
            c_e = jnp.where(lane == lanes - 1, ce[:, r : r + 1], pltpu.roll(c_mid, lanes - 1, 1))
            k_ref[0, g, r] = jnp.minimum(c_mid, c_up)
            k_ref[1, g, r] = jnp.minimum(c_mid, c_dn)
            k_ref[2, g, r] = jnp.minimum(c_mid, c_w)
            k_ref[3, g, r] = jnp.minimum(c_mid, c_e)
            c_up, c_mid = c_mid, c_dn
        return carry

    lax.fori_loop(0, groups, body, 0)


def slab_pass(rows, src_ref, k_ref, field_halo, scales, dst_ref, edges):
    groups, span, lanes = src_ref.shape
    group = span // rows
    north_ok, south_ok = scales
    row_halo, col_halo = field_halo

    def body(g, carry):
        lane = lax.broadcasted_iota(jnp.int32, (group, lanes), 1)
        col = lax.broadcasted_iota(jnp.int32, (group, rows), 1)

        def slab(ref, r):
            return ref[g, pl.ds(r, group, stride=rows), :]

        vw = col_halo[0, g]
        ve = col_halo[1, g]
        left = jnp.zeros((group, rows), jnp.float32)
        right = jnp.zeros((group, rows), jnp.float32)
        x_up = row_halo[0, g] * north_ok
        x_mid = slab(src_ref, 0)
        for r in range(rows):
            if r + 1 < rows:
                x_dn = slab(src_ref, r + 1)
            else:
                x_dn = row_halo[1, g] * south_ok
            x_w = jnp.where(lane == 0, vw[:, r : r + 1], pltpu.roll(x_mid, 1, 1))
            x_e = jnp.where(lane == lanes - 1, ve[:, r : r + 1], pltpu.roll(x_mid, lanes - 1, 1))
            total = k_ref[0, g, r] * (x_up - x_mid)
            total = total + k_ref[1, g, r] * (x_dn - x_mid)
            total = total + k_ref[2, g, r] * (x_w - x_mid)
            total = total + k_ref[3, g, r] * (x_e - x_mid)
            out = x_mid + total
            dst_ref[g, pl.ds(r, group, stride=rows), :] = out
            if edges is not None:
                if r == 0:
                    edges[0][0, g] = out
                if r == rows - 1:
                    edges[0][1, g] = out
                left = jnp.where(col == r, out[:, 0:1], left)
                right = jnp.where(col == r, out[:, lanes - 1 : lanes], right)
            x_up, x_mid = x_mid, x_dn
        if edges is not None:
            edges[1][0, g] = left
            edges[1][1, g] = right
        return carry

    lax.fori_loop(0, groups, body, 0)


def edge_pass(rows, src_ref, row_out, col_out):
    groups, span, lanes = src_ref.shape
    group = span // rows

    def body(g, carry):
        col = lax.broadcasted_iota(jnp.int32, (group, rows), 1)
        left = jnp.zeros((group, rows), jnp.float32)
        right = jnp.zeros((group, rows), jnp.float32)
        for r in range(rows):
            x = src_ref[g, pl.ds(r, group, stride=rows), :]
            if r == 0:
                row_out[0, g] = x
            if r == rows - 1:
                row_out[1, g] = x
            left = jnp.where(col == r, x[:, 0:1], left)
            right = jnp.where(col == r, x[:, lanes - 1 : lanes], right)
        col_out[0, g] = left
        col_out[1, g] = right
        return carry

    lax.fori_loop(0, groups, body, 0)


def diffuse_kernel(rows, v_ref, c_ref, out_ref, mid_ref, k_ref, row_edge, col_edge, row_halo,
                   col_halo, send_sem, recv_sem):
    lon = lax.axis_index("lon")
    lat = lax.axis_index("lat")
    n_lon = lax.axis_size("lon")
    n_lat = lax.axis_size("lat")
    north = {"lat": (lat + n_lat - 1) % n_lat}
    south = {"lat": (lat + 1) % n_lat}
    west = {"lon": (lon + n_lon - 1) % n_lon}
    east = {"lon": (lon + 1) % n_lon}
    mesh_id = pl.DeviceIdType.MESH

    barrier = pltpu.get_barrier_semaphore()
    for peer in (north, south, west, east):
        pl.semaphore_signal(barrier, inc=1, device_id=peer, device_id_type=mesh_id)
    pl.semaphore_wait(barrier, 4)

    def exchange(rd):
        plan = [
            (row_edge.at[rd, 0], row_halo.at[rd, 1], north, 0),
            (row_edge.at[rd, 1], row_halo.at[rd, 0], south, 1),
            (col_edge.at[rd, 0], col_halo.at[rd, 1], west, 2),
            (col_edge.at[rd, 1], col_halo.at[rd, 0], east, 3),
        ]
        copies = []
        for src, dst, peer, k in plan:
            copy = pltpu.make_async_remote_copy(
                src_ref=src, dst_ref=dst, send_sem=send_sem.at[rd, k], recv_sem=recv_sem.at[rd, k],
                device_id=peer, device_id_type=mesh_id,
            )
            copy.start()
            copies.append(copy)
        return copies

    edge_pass(rows, c_ref, row_edge.at[0], col_edge.at[0])
    edge_pass(rows, v_ref, row_edge.at[1], col_edge.at[1])
    first = exchange(0) + exchange(1)
    for copy in first:
        copy.wait()
    north_ok = jnp.minimum(lat, 1).astype(jnp.float32)
    south_ok = jnp.minimum(n_lat - 1 - lat, 1).astype(jnp.float32)
    scales = (north_ok, south_ok)
    coef_pass(rows, c_ref, (row_halo.at[0], col_halo.at[0]), scales, k_ref)
    slab_pass(rows, v_ref, k_ref, (row_halo.at[1], col_halo.at[1]), scales, mid_ref,
              (row_edge.at[2], col_edge.at[2]))
    for copy in exchange(2):
        copy.wait()
    slab_pass(rows, mid_ref, k_ref, (row_halo.at[2], col_halo.at[2]), scales, out_ref, None)


def diffuse(field, conduct_blocks):
    vals, rows, lanes = field.shape
    groups = vals // GROUP
    blocks = field.reshape(groups, GROUP * rows, lanes)
    rounds = SWEEPS + 1
    out = pl.pallas_call(
        functools.partial(diffuse_kernel, rows),
        in_specs=[VMEM, VMEM],
        out_specs=VMEM,
        out_shape=jax.ShapeDtypeStruct(blocks.shape, jnp.float32),
        scratch_shapes=[
            pltpu.VMEM(blocks.shape, jnp.float32),
            pltpu.VMEM((4, groups, rows, GROUP, lanes), jnp.float32),
            pltpu.VMEM((rounds, 2, groups, GROUP, lanes), jnp.float32),
            pltpu.VMEM((rounds, 2, groups, GROUP, rows), jnp.float32),
            pltpu.VMEM((rounds, 2, groups, GROUP, lanes), jnp.float32),
            pltpu.VMEM((rounds, 2, groups, GROUP, rows), jnp.float32),
            pltpu.SemaphoreType.DMA((rounds, 4)),
            pltpu.SemaphoreType.DMA((rounds, 4)),
        ],
        compiler_params=pltpu.CompilerParams(collective_id=0, has_side_effects=True),
        cost_estimate=pl.CostEstimate(
            flops=50 * field.size, bytes_accessed=12 * field.size, transcendentals=0
        ),
    )(blocks, conduct_blocks)
    return out.reshape(vals, rows, lanes)


def load_row(ref, index):
    return ref[pl.ds(index, 1), :]


def add_row(ref, index, value):
    spot = pl.ds(index, 1)
    ref[spot, :] = ref[spot, :] + value


def select_kernel(index_ref, rows_ref, out_ref):
    cells = rows_ref.shape[0]
    width = out_ref.shape[1]
    sub = lax.broadcasted_iota(jnp.int32, (8, width), 0)

    def body(t, carry):
        tile = jnp.zeros((8, width), jnp.float32)
        for i in range(8):
            source = index_ref[t * 8 + i]
            row = load_row(rows_ref, jnp.minimum(source, cells - 1))
            tile = jnp.where((sub == i) & (source < cells), jnp.broadcast_to(row, (8, width)), tile)
        out_ref[pl.ds(pl.multiple_of(t * 8, 8), 8), :] = tile
        return carry

    lax.fori_loop(0, out_ref.shape[0] // 8, body, 0, unroll=2)


def place_kernel(index_ref, rows_ref, out_ref, *parts):
    cells = out_ref.shape[0]
    for part in parts:
        part[...] = jnp.zeros_like(part)

    def body(t, carry):
        for i, part in enumerate(parts):
            q = t * len(parts) + i
            target = index_ref[q]
            row = load_row(rows_ref, q)
            add_row(part, jnp.minimum(target, cells - 1), jnp.where(target < cells, row, 0.0))
        return carry

    lax.fori_loop(0, rows_ref.shape[0] // len(parts), body, 0, unroll=2)
    total = parts[0][...]
    for part in parts[1:]:
        total = total + part[...]
    out_ref[...] = total


def interp_kernel(slot_ref, weight_ref, received_ref, precision_ref, equiv_ref, returned_ref, *parts):
    taps, obs_count = slot_ref.shape
    width = equiv_ref.shape[1]
    sub = lax.broadcasted_iota(jnp.int32, (8, width), 0)
    for part in parts:
        part[...] = jnp.zeros_like(part)

    def body(t, carry):
        tile = jnp.zeros((8, width), jnp.float32)
        for i in range(8):
            j = t * 8 + i
            slots = [slot_ref[k, j] for k in range(taps)]
            weights = [weight_ref[k, j] for k in range(taps)]
            total = load_row(received_ref, slots[0]) * weights[0]
            for k in range(1, taps):
                total = total + load_row(received_ref, slots[k]) * weights[k]
            tile = jnp.where(sub == i, jnp.broadcast_to(total, (8, width)), tile)
            weighted = load_row(precision_ref, j) * total
            for k in range(taps):
                add_row(parts[k], slots[k], weighted * weights[k])
        equiv_ref[pl.ds(pl.multiple_of(t * 8, 8), 8), :] = tile
        return carry

    lax.fori_loop(0, obs_count // 8, body, 0)
    total = parts[0][...]
    for part in parts[1:]:
        total = total + part[...]
    returned_ref[...] = total


def select_rows(index, rows, count):
    return pl.pallas_call(
        select_kernel,
        in_specs=[SMEM, VMEM],
        out_specs=VMEM,
        out_shape=jax.ShapeDtypeStruct((count, rows.shape[1]), jnp.float32),
    )(index, rows)


def place_rows(index, rows, cells):
    return pl.pallas_call(
        place_kernel,
        in_specs=[SMEM, VMEM],
        out_specs=VMEM,
        out_shape=jax.ShapeDtypeStruct((cells, rows.shape[1]), jnp.float32),
        scratch_shapes=[pltpu.VMEM((cells, rows.shape[1]), jnp.float32) for _ in range(2)],
        compiler_params=pltpu.CompilerParams(vmem_limit_bytes=60 * 1024 * 1024),
    )(index, rows)


def interpolate(obs_slots, obs_weights, received, precision_rows):
    obs_count = obs_slots.shape[1]
    return pl.pallas_call(
        interp_kernel,
        in_specs=[SMEM, SMEM, VMEM, VMEM],
        out_specs=[VMEM, VMEM],
        out_shape=[
            jax.ShapeDtypeStruct((obs_count, received.shape[1]), jnp.float32),
            jax.ShapeDtypeStruct(received.shape, jnp.float32),
        ],
        scratch_shapes=[
            pltpu.VMEM(received.shape, jnp.float32) for _ in range(obs_slots.shape[0])
        ],
        compiler_params=pltpu.CompilerParams(vmem_limit_bytes=60 * 1024 * 1024),
    )(obs_slots, obs_weights, received, precision_rows)


def to_owners(outgoing):
    return lax.all_to_all(outgoing, ("lon", "lat"), split_axis=0, concat_axis=0, tiled=True)


def to_sources(returned):
    return lax.all_to_all(returned, ("lon", "lat"), split_axis=0, concat_axis=0, tiled=True)


def on_device(state, diffusivity, sea_mask, send_cols, obs_slots, obs_weights, obs_precision):
    vals, rows, lanes = state.shape
    cell_count = rows * lanes
    steps = vals // GROUP
    sea_float = sea_mask.astype(jnp.float32)
    conduct = diffusivity * jnp.concatenate([sea_float, sea_float], axis=0)
    conduct_blocks = conduct.reshape(steps, GROUP * rows, lanes)
    smooth = diffuse(state, conduct_blocks)
    rows_of = smooth.transpose(1, 2, 0).reshape(cell_count, vals)
    send_index = send_cols[0]
    outgoing = select_rows(send_index, rows_of, send_index.shape[0])
    received = to_owners(outgoing)
    equivalent_rows, returned = interpolate(obs_slots, obs_weights, received, obs_precision.T)
    equivalents = equivalent_rows.T
    incoming = to_sources(returned)
    adjoint_rows = place_rows(send_index, incoming, cell_count)
    adjoint_field = adjoint_rows.reshape(rows, lanes, vals).transpose(2, 0, 1)
    product = state + diffuse(adjoint_field, conduct_blocks)
    return (product, equivalents)


def solution(mesh):
    placed = (
        P(None, "lat", "lon"),
        P(None, "lat", "lon"),
        P(None, "lat", "lon"),
        P(("lon", "lat"), None),
        P(None, ("lon", "lat")),
        P(None, ("lon", "lat")),
        P(None, ("lon", "lat")),
    )
    return jax.shard_map(
        on_device,
        mesh=mesh,
        in_specs=placed,
        out_specs=(P(None, "lat", "lon"), P(None, ("lon", "lat"))),
        check_vma=False,
    )
```

```python
import functools

import jax
import jax.numpy as jnp
from jax import lax
from jax.experimental import pallas as pl
from jax.experimental.pallas import tpu as pltpu
from jax.sharding import PartitionSpec as P

SWEEPS = 2
GROUP = 30
SMEM = pl.BlockSpec(memory_space=pltpu.SMEM)
VMEM = pl.BlockSpec(memory_space=pltpu.VMEM)


def coef_pass(rows, c_ref, coef_halo, scales, k_ref):
    groups, span, lanes = c_ref.shape
    group = span // rows
    north_ok, south_ok = scales
    coef_rows, coef_cols = coef_halo

    def body(g, carry):
        lane = lax.broadcasted_iota(jnp.int32, (group, lanes), 1)
        cw = coef_cols[0, g]
        ce = coef_cols[1, g]
        c_up = coef_rows[0, g] * north_ok
        c_mid = c_ref[g, pl.ds(0, group, stride=rows), :]
        for r in range(rows):
            if r + 1 < rows:
                c_dn = c_ref[g, pl.ds(r + 1, group, stride=rows), :]
            else:
                c_dn = coef_rows[1, g] * south_ok
            c_w = jnp.where(lane == 0, cw[:, r : r + 1], pltpu.roll(c_mid, 1, 1))
            c_e = jnp.where(lane == lanes - 1, ce[:, r : r + 1], pltpu.roll(c_mid, lanes - 1, 1))
            k_ref[0, g, r] = jnp.minimum(c_mid, c_up)
            k_ref[1, g, r] = jnp.minimum(c_mid, c_dn)
            k_ref[2, g, r] = jnp.minimum(c_mid, c_w)
            k_ref[3, g, r] = jnp.minimum(c_mid, c_e)
            c_up, c_mid = c_mid, c_dn
        return carry

    lax.fori_loop(0, groups, body, 0)


def slab_pass(rows, src_ref, k_ref, field_halo, scales, dst_ref, edges):
    groups, span, lanes = src_ref.shape
    group = span // rows
    north_ok, south_ok = scales
    row_halo, col_halo = field_halo

    def body(g, carry):
        lane = lax.broadcasted_iota(jnp.int32, (group, lanes), 1)
        col = lax.broadcasted_iota(jnp.int32, (group, rows), 1)

        def slab(ref, r):
            return ref[g, pl.ds(r, group, stride=rows), :]

        vw = col_halo[0, g]
        ve = col_halo[1, g]
        left = jnp.zeros((group, rows), jnp.float32)
        right = jnp.zeros((group, rows), jnp.float32)
        x_up = row_halo[0, g] * north_ok
        x_mid = slab(src_ref, 0)
        for r in range(rows):
            if r + 1 < rows:
                x_dn = slab(src_ref, r + 1)
            else:
                x_dn = row_halo[1, g] * south_ok
            x_w = jnp.where(lane == 0, vw[:, r : r + 1], pltpu.roll(x_mid, 1, 1))
            x_e = jnp.where(lane == lanes - 1, ve[:, r : r + 1], pltpu.roll(x_mid, lanes - 1, 1))
            total = k_ref[0, g, r] * (x_up - x_mid)
            total = total + k_ref[1, g, r] * (x_dn - x_mid)
            total = total + k_ref[2, g, r] * (x_w - x_mid)
            total = total + k_ref[3, g, r] * (x_e - x_mid)
            out = x_mid + total
            dst_ref[g, pl.ds(r, group, stride=rows), :] = out
            if edges is not None:
                if r == 0:
                    edges[0][0, g] = out
                if r == rows - 1:
                    edges[0][1, g] = out
                left = jnp.where(col == r, out[:, 0:1], left)
                right = jnp.where(col == r, out[:, lanes - 1 : lanes], right)
            x_up, x_mid = x_mid, x_dn
        if edges is not None:
            edges[1][0, g] = left
            edges[1][1, g] = right
        return carry

    lax.fori_loop(0, groups, body, 0)


def edge_pass(rows, src_ref, row_out, col_out):
    groups, span, lanes = src_ref.shape
    group = span // rows

    def body(g, carry):
        col = lax.broadcasted_iota(jnp.int32, (group, rows), 1)
        left = jnp.zeros((group, rows), jnp.float32)
        right = jnp.zeros((group, rows), jnp.float32)
        for r in range(rows):
            x = src_ref[g, pl.ds(r, group, stride=rows), :]
            if r == 0:
                row_out[0, g] = x
            if r == rows - 1:
                row_out[1, g] = x
            left = jnp.where(col == r, x[:, 0:1], left)
            right = jnp.where(col == r, x[:, lanes - 1 : lanes], right)
        col_out[0, g] = left
        col_out[1, g] = right
        return carry

    lax.fori_loop(0, groups, body, 0)


def diffuse_kernel(rows, v_ref, c_ref, out_ref, mid_ref, k_ref, row_edge, col_edge, row_halo,
                   col_halo, send_sem, recv_sem):
    lon = lax.axis_index("lon")
    lat = lax.axis_index("lat")
    n_lon = lax.axis_size("lon")
    n_lat = lax.axis_size("lat")
    north = {"lat": (lat + n_lat - 1) % n_lat}
    south = {"lat": (lat + 1) % n_lat}
    west = {"lon": (lon + n_lon - 1) % n_lon}
    east = {"lon": (lon + 1) % n_lon}
    mesh_id = pl.DeviceIdType.MESH

    barrier = pltpu.get_barrier_semaphore()
    for peer in (north, south, west, east):
        pl.semaphore_signal(barrier, inc=1, device_id=peer, device_id_type=mesh_id)
    pl.semaphore_wait(barrier, 4)

    def exchange(rd):
        plan = [
            (row_edge.at[rd, 0], row_halo.at[rd, 1], north, 0),
            (row_edge.at[rd, 1], row_halo.at[rd, 0], south, 1),
            (col_edge.at[rd, 0], col_halo.at[rd, 1], west, 2),
            (col_edge.at[rd, 1], col_halo.at[rd, 0], east, 3),
        ]
        copies = []
        for src, dst, peer, k in plan:
            copy = pltpu.make_async_remote_copy(
                src_ref=src, dst_ref=dst, send_sem=send_sem.at[rd, k], recv_sem=recv_sem.at[rd, k],
                device_id=peer, device_id_type=mesh_id,
            )
            copy.start()
            copies.append(copy)
        return copies

    edge_pass(rows, c_ref, row_edge.at[0], col_edge.at[0])
    edge_pass(rows, v_ref, row_edge.at[1], col_edge.at[1])
    first = exchange(0) + exchange(1)
    for copy in first:
        copy.wait()
    north_ok = jnp.minimum(lat, 1).astype(jnp.float32)
    south_ok = jnp.minimum(n_lat - 1 - lat, 1).astype(jnp.float32)
    scales = (north_ok, south_ok)
    coef_pass(rows, c_ref, (row_halo.at[0], col_halo.at[0]), scales, k_ref)
    slab_pass(rows, v_ref, k_ref, (row_halo.at[1], col_halo.at[1]), scales, mid_ref,
              (row_edge.at[2], col_edge.at[2]))
    for copy in exchange(2):
        copy.wait()
    slab_pass(rows, mid_ref, k_ref, (row_halo.at[2], col_halo.at[2]), scales, out_ref, None)


def diffuse(field, conduct_blocks):
    vals, rows, lanes = field.shape
    groups = vals // GROUP
    blocks = field.reshape(groups, GROUP * rows, lanes)
    rounds = SWEEPS + 1
    out = pl.pallas_call(
        functools.partial(diffuse_kernel, rows),
        in_specs=[VMEM, VMEM],
        out_specs=VMEM,
        out_shape=jax.ShapeDtypeStruct(blocks.shape, jnp.float32),
        scratch_shapes=[
            pltpu.VMEM(blocks.shape, jnp.float32),
            pltpu.VMEM((4, groups, rows, GROUP, lanes), jnp.float32),
            pltpu.VMEM((rounds, 2, groups, GROUP, lanes), jnp.float32),
            pltpu.VMEM((rounds, 2, groups, GROUP, rows), jnp.float32),
            pltpu.VMEM((rounds, 2, groups, GROUP, lanes), jnp.float32),
            pltpu.VMEM((rounds, 2, groups, GROUP, rows), jnp.float32),
            pltpu.SemaphoreType.DMA((rounds, 4)),
            pltpu.SemaphoreType.DMA((rounds, 4)),
        ],
        compiler_params=pltpu.CompilerParams(collective_id=0, has_side_effects=True),
        cost_estimate=pl.CostEstimate(
            flops=50 * field.size, bytes_accessed=12 * field.size, transcendentals=0
        ),
    )(blocks, conduct_blocks)
    return out.reshape(vals, rows, lanes)


def load_row(ref, index):
    return ref[pl.ds(index, 1), :]


def add_row(ref, index, value):
    spot = pl.ds(index, 1)
    ref[spot, :] = ref[spot, :] + value


def select_kernel(index_ref, rows_ref, out_ref):
    cells = rows_ref.shape[0]
    width = out_ref.shape[1]
    sub = lax.broadcasted_iota(jnp.int32, (8, width), 0)

    def body(t, carry):
        tile = jnp.zeros((8, width), jnp.float32)
        for i in range(8):
            source = index_ref[t * 8 + i]
            row = load_row(rows_ref, jnp.minimum(source, cells - 1))
            tile = jnp.where((sub == i) & (source < cells), jnp.broadcast_to(row, (8, width)), tile)
        out_ref[pl.ds(pl.multiple_of(t * 8, 8), 8), :] = tile
        return carry

    lax.fori_loop(0, out_ref.shape[0] // 8, body, 0, unroll=2)


def place_kernel(index_ref, rows_ref, out_ref, *parts):
    cells = out_ref.shape[0]
    for part in parts:
        part[...] = jnp.zeros_like(part)

    def body(t, carry):
        for i, part in enumerate(parts):
            q = t * len(parts) + i
            target = index_ref[q]
            row = load_row(rows_ref, q)
            add_row(part, jnp.minimum(target, cells - 1), jnp.where(target < cells, row, 0.0))
        return carry

    lax.fori_loop(0, rows_ref.shape[0] // len(parts), body, 0, unroll=2)
    total = parts[0][...]
    for part in parts[1:]:
        total = total + part[...]
    out_ref[...] = total


def interp_kernel(slot_ref, weight_ref, received_ref, precision_ref, equiv_ref, returned_ref, *parts):
    taps, obs_count = slot_ref.shape
    width = equiv_ref.shape[1]
    sub = lax.broadcasted_iota(jnp.int32, (8, width), 0)
    for part in parts:
        part[...] = jnp.zeros_like(part)

    def body(t, carry):
        tile = jnp.zeros((8, width), jnp.float32)
        for i in range(8):
            j = t * 8 + i
            slots = [slot_ref[k, j] for k in range(taps)]
            weights = [weight_ref[k, j] for k in range(taps)]
            total = load_row(received_ref, slots[0]) * weights[0]
            for k in range(1, taps):
                total = total + load_row(received_ref, slots[k]) * weights[k]
            tile = jnp.where(sub == i, jnp.broadcast_to(total, (8, width)), tile)
            weighted = load_row(precision_ref, j) * total
            for k in range(taps):
                add_row(parts[k], slots[k], weighted * weights[k])
        equiv_ref[pl.ds(pl.multiple_of(t * 8, 8), 8), :] = tile
        return carry

    lax.fori_loop(0, obs_count // 8, body, 0)
    total = parts[0][...]
    for part in parts[1:]:
        total = total + part[...]
    returned_ref[...] = total


def select_rows(index, rows, count):
    return pl.pallas_call(
        select_kernel,
        in_specs=[SMEM, VMEM],
        out_specs=VMEM,
        out_shape=jax.ShapeDtypeStruct((count, rows.shape[1]), jnp.float32),
    )(index, rows)


def place_rows(index, rows, cells):
    return pl.pallas_call(
        place_kernel,
        in_specs=[SMEM, VMEM],
        out_specs=VMEM,
        out_shape=jax.ShapeDtypeStruct((cells, rows.shape[1]), jnp.float32),
        scratch_shapes=[pltpu.VMEM((cells, rows.shape[1]), jnp.float32) for _ in range(4)],
        compiler_params=pltpu.CompilerParams(vmem_limit_bytes=60 * 1024 * 1024),
    )(index, rows)


def interpolate(obs_slots, obs_weights, received, precision_rows):
    obs_count = obs_slots.shape[1]
    return pl.pallas_call(
        interp_kernel,
        in_specs=[SMEM, SMEM, VMEM, VMEM],
        out_specs=[VMEM, VMEM],
        out_shape=[
            jax.ShapeDtypeStruct((obs_count, received.shape[1]), jnp.float32),
            jax.ShapeDtypeStruct(received.shape, jnp.float32),
        ],
        scratch_shapes=[
            pltpu.VMEM(received.shape, jnp.float32) for _ in range(obs_slots.shape[0])
        ],
        compiler_params=pltpu.CompilerParams(vmem_limit_bytes=60 * 1024 * 1024),
    )(obs_slots, obs_weights, received, precision_rows)


def to_owners(outgoing):
    return lax.all_to_all(outgoing, ("lon", "lat"), split_axis=0, concat_axis=0, tiled=True)


def to_sources(returned):
    return lax.all_to_all(returned, ("lon", "lat"), split_axis=0, concat_axis=0, tiled=True)


def on_device(state, diffusivity, sea_mask, send_cols, obs_slots, obs_weights, obs_precision):
    vals, rows, lanes = state.shape
    cell_count = rows * lanes
    steps = vals // GROUP
    sea_float = sea_mask.astype(jnp.float32)
    conduct = diffusivity * jnp.concatenate([sea_float, sea_float], axis=0)
    conduct_blocks = conduct.reshape(steps, GROUP * rows, lanes)
    smooth = diffuse(state, conduct_blocks)
    rows_of = smooth.transpose(1, 2, 0).reshape(cell_count, vals)
    send_index = send_cols[0]
    outgoing = select_rows(send_index, rows_of, send_index.shape[0])
    received = to_owners(outgoing)
    equivalent_rows, returned = interpolate(obs_slots, obs_weights, received, obs_precision.T)
    equivalents = equivalent_rows.T
    incoming = to_sources(returned)
    adjoint_rows = place_rows(send_index, incoming, cell_count)
    adjoint_field = adjoint_rows.reshape(rows, lanes, vals).transpose(2, 0, 1)
    product = state + diffuse(adjoint_field, conduct_blocks)
    return (product, equivalents)


def solution(mesh):
    placed = (
        P(None, "lat", "lon"),
        P(None, "lat", "lon"),
        P(None, "lat", "lon"),
        P(("lon", "lat"), None),
        P(None, ("lon", "lat")),
        P(None, ("lon", "lat")),
        P(None, ("lon", "lat")),
    )
    return jax.shard_map(
        on_device,
        mesh=mesh,
        in_specs=placed,
        out_specs=(P(None, "lat", "lon"), P(None, ("lon", "lat"))),
        check_vma=False,
    )
```

```python
import functools

import jax
import jax.numpy as jnp
from jax import lax
from jax.experimental import pallas as pl
from jax.experimental.pallas import tpu as pltpu
from jax.sharding import PartitionSpec as P

SWEEPS = 2
GROUP = 30
SMEM = pl.BlockSpec(memory_space=pltpu.SMEM)
VMEM = pl.BlockSpec(memory_space=pltpu.VMEM)


def coef_pass(rows, c_ref, coef_halo, scales, k_ref):
    groups, span, lanes = c_ref.shape
    group = span // rows
    north_ok, south_ok = scales
    coef_rows, coef_cols = coef_halo

    def body(g, carry):
        lane = lax.broadcasted_iota(jnp.int32, (group, lanes), 1)
        cw = coef_cols[0, g]
        ce = coef_cols[1, g]
        c_up = coef_rows[0, g] * north_ok
        c_mid = c_ref[g, pl.ds(0, group, stride=rows), :]
        for r in range(rows):
            if r + 1 < rows:
                c_dn = c_ref[g, pl.ds(r + 1, group, stride=rows), :]
            else:
                c_dn = coef_rows[1, g] * south_ok
            c_w = jnp.where(lane == 0, cw[:, r : r + 1], pltpu.roll(c_mid, 1, 1))
            c_e = jnp.where(lane == lanes - 1, ce[:, r : r + 1], pltpu.roll(c_mid, lanes - 1, 1))
            k_ref[0, g, r] = jnp.minimum(c_mid, c_up)
            k_ref[1, g, r] = jnp.minimum(c_mid, c_dn)
            k_ref[2, g, r] = jnp.minimum(c_mid, c_w)
            k_ref[3, g, r] = jnp.minimum(c_mid, c_e)
            c_up, c_mid = c_mid, c_dn
        return carry

    lax.fori_loop(0, groups, body, 0)


def slab_pass(rows, src_ref, k_ref, field_halo, scales, dst_ref, edges):
    groups, span, lanes = src_ref.shape
    group = span // rows
    north_ok, south_ok = scales
    row_halo, col_halo = field_halo

    def body(g, carry):
        lane = lax.broadcasted_iota(jnp.int32, (group, lanes), 1)
        col = lax.broadcasted_iota(jnp.int32, (group, rows), 1)

        def slab(ref, r):
            return ref[g, pl.ds(r, group, stride=rows), :]

        vw = col_halo[0, g]
        ve = col_halo[1, g]
        left = jnp.zeros((group, rows), jnp.float32)
        right = jnp.zeros((group, rows), jnp.float32)
        x_up = row_halo[0, g] * north_ok
        x_mid = slab(src_ref, 0)
        for r in range(rows):
            if r + 1 < rows:
                x_dn = slab(src_ref, r + 1)
            else:
                x_dn = row_halo[1, g] * south_ok
            x_w = jnp.where(lane == 0, vw[:, r : r + 1], pltpu.roll(x_mid, 1, 1))
            x_e = jnp.where(lane == lanes - 1, ve[:, r : r + 1], pltpu.roll(x_mid, lanes - 1, 1))
            total = k_ref[0, g, r] * (x_up - x_mid)
            total = total + k_ref[1, g, r] * (x_dn - x_mid)
            total = total + k_ref[2, g, r] * (x_w - x_mid)
            total = total + k_ref[3, g, r] * (x_e - x_mid)
            out = x_mid + total
            dst_ref[g, pl.ds(r, group, stride=rows), :] = out
            if edges is not None:
                if r == 0:
                    edges[0][0, g] = out
                if r == rows - 1:
                    edges[0][1, g] = out
                left = jnp.where(col == r, out[:, 0:1], left)
                right = jnp.where(col == r, out[:, lanes - 1 : lanes], right)
            x_up, x_mid = x_mid, x_dn
        if edges is not None:
            edges[1][0, g] = left
            edges[1][1, g] = right
        return carry

    lax.fori_loop(0, groups, body, 0)


def edge_pass(rows, src_ref, row_out, col_out):
    groups, span, lanes = src_ref.shape
    group = span // rows

    def body(g, carry):
        col = lax.broadcasted_iota(jnp.int32, (group, rows), 1)
        left = jnp.zeros((group, rows), jnp.float32)
        right = jnp.zeros((group, rows), jnp.float32)
        for r in range(rows):
            x = src_ref[g, pl.ds(r, group, stride=rows), :]
            if r == 0:
                row_out[0, g] = x
            if r == rows - 1:
                row_out[1, g] = x
            left = jnp.where(col == r, x[:, 0:1], left)
            right = jnp.where(col == r, x[:, lanes - 1 : lanes], right)
        col_out[0, g] = left
        col_out[1, g] = right
        return carry

    lax.fori_loop(0, groups, body, 0)


def diffuse_kernel(rows, v_ref, c_ref, out_ref, mid_ref, k_ref, row_edge, col_edge, row_halo,
                   col_halo, send_sem, recv_sem):
    lon = lax.axis_index("lon")
    lat = lax.axis_index("lat")
    n_lon = lax.axis_size("lon")
    n_lat = lax.axis_size("lat")
    north = {"lat": (lat + n_lat - 1) % n_lat}
    south = {"lat": (lat + 1) % n_lat}
    west = {"lon": (lon + n_lon - 1) % n_lon}
    east = {"lon": (lon + 1) % n_lon}
    mesh_id = pl.DeviceIdType.MESH

    barrier = pltpu.get_barrier_semaphore()
    for peer in (north, south, west, east):
        pl.semaphore_signal(barrier, inc=1, device_id=peer, device_id_type=mesh_id)
    pl.semaphore_wait(barrier, 4)

    def exchange(rd):
        plan = [
            (row_edge.at[rd, 0], row_halo.at[rd, 1], north, 0),
            (row_edge.at[rd, 1], row_halo.at[rd, 0], south, 1),
            (col_edge.at[rd, 0], col_halo.at[rd, 1], west, 2),
            (col_edge.at[rd, 1], col_halo.at[rd, 0], east, 3),
        ]
        copies = []
        for src, dst, peer, k in plan:
            copy = pltpu.make_async_remote_copy(
                src_ref=src, dst_ref=dst, send_sem=send_sem.at[rd, k], recv_sem=recv_sem.at[rd, k],
                device_id=peer, device_id_type=mesh_id,
            )
            copy.start()
            copies.append(copy)
        return copies

    edge_pass(rows, c_ref, row_edge.at[0], col_edge.at[0])
    edge_pass(rows, v_ref, row_edge.at[1], col_edge.at[1])
    first = exchange(0) + exchange(1)
    for copy in first:
        copy.wait()
    north_ok = jnp.minimum(lat, 1).astype(jnp.float32)
    south_ok = jnp.minimum(n_lat - 1 - lat, 1).astype(jnp.float32)
    scales = (north_ok, south_ok)
    coef_pass(rows, c_ref, (row_halo.at[0], col_halo.at[0]), scales, k_ref)
    slab_pass(rows, v_ref, k_ref, (row_halo.at[1], col_halo.at[1]), scales, mid_ref,
              (row_edge.at[2], col_edge.at[2]))
    for copy in exchange(2):
        copy.wait()
    slab_pass(rows, mid_ref, k_ref, (row_halo.at[2], col_halo.at[2]), scales, out_ref, None)


def diffuse(field, conduct_blocks):
    vals, rows, lanes = field.shape
    groups = vals // GROUP
    blocks = field.reshape(groups, GROUP * rows, lanes)
    rounds = SWEEPS + 1
    out = pl.pallas_call(
        functools.partial(diffuse_kernel, rows),
        in_specs=[VMEM, VMEM],
        out_specs=VMEM,
        out_shape=jax.ShapeDtypeStruct(blocks.shape, jnp.float32),
        scratch_shapes=[
            pltpu.VMEM(blocks.shape, jnp.float32),
            pltpu.VMEM((4, groups, rows, GROUP, lanes), jnp.float32),
            pltpu.VMEM((rounds, 2, groups, GROUP, lanes), jnp.float32),
            pltpu.VMEM((rounds, 2, groups, GROUP, rows), jnp.float32),
            pltpu.VMEM((rounds, 2, groups, GROUP, lanes), jnp.float32),
            pltpu.VMEM((rounds, 2, groups, GROUP, rows), jnp.float32),
            pltpu.SemaphoreType.DMA((rounds, 4)),
            pltpu.SemaphoreType.DMA((rounds, 4)),
        ],
        compiler_params=pltpu.CompilerParams(collective_id=0, has_side_effects=True),
        cost_estimate=pl.CostEstimate(
            flops=50 * field.size, bytes_accessed=12 * field.size, transcendentals=0
        ),
    )(blocks, conduct_blocks)
    return out.reshape(vals, rows, lanes)


def load_row(ref, index):
    return ref[pl.ds(index, 1), :]


def add_row(ref, index, value):
    spot = pl.ds(index, 1)
    ref[spot, :] = ref[spot, :] + value


def select_kernel(index_ref, rows_ref, out_ref):
    cells = rows_ref.shape[0]
    width = out_ref.shape[1]
    sub = lax.broadcasted_iota(jnp.int32, (8, width), 0)

    def body(t, carry):
        tile = jnp.zeros((8, width), jnp.float32)
        for i in range(8):
            source = index_ref[t * 8 + i]
            row = load_row(rows_ref, jnp.minimum(source, cells - 1))
            tile = jnp.where((sub == i) & (source < cells), jnp.broadcast_to(row, (8, width)), tile)
        out_ref[pl.ds(pl.multiple_of(t * 8, 8), 8), :] = tile
        return carry

    lax.fori_loop(0, out_ref.shape[0] // 8, body, 0, unroll=2)


def place_kernel(index_ref, rows_ref, out_ref, *parts):
    cells = out_ref.shape[0]
    for part in parts:
        part[...] = jnp.zeros_like(part)

    def body(t, carry):
        for i, part in enumerate(parts):
            q = t * len(parts) + i
            target = index_ref[q]
            row = load_row(rows_ref, q)
            add_row(part, jnp.minimum(target, cells - 1), jnp.where(target < cells, row, 0.0))
        return carry

    lax.fori_loop(0, rows_ref.shape[0] // len(parts), body, 0, unroll=2)
    total = parts[0][...]
    for part in parts[1:]:
        total = total + part[...]
    out_ref[...] = total


def interp_kernel(slot_ref, weight_ref, received_ref, precision_ref, equiv_ref, returned_ref, *parts):
    taps, obs_count = slot_ref.shape
    width = equiv_ref.shape[1]
    sub = lax.broadcasted_iota(jnp.int32, (8, width), 0)
    for part in parts:
        part[...] = jnp.zeros_like(part)

    def body(t, carry):
        tile = jnp.zeros((8, width), jnp.float32)
        for i in range(8):
            j = t * 8 + i
            slots = [slot_ref[k, j] for k in range(taps)]
            weights = [weight_ref[k, j] for k in range(taps)]
            total = load_row(received_ref, slots[0]) * weights[0]
            for k in range(1, taps):
                total = total + load_row(received_ref, slots[k]) * weights[k]
            tile = jnp.where(sub == i, jnp.broadcast_to(total, (8, width)), tile)
            weighted = load_row(precision_ref, j) * total
            for k in range(taps):
                add_row(parts[k], slots[k], weighted * weights[k])
        equiv_ref[pl.ds(pl.multiple_of(t * 8, 8), 8), :] = tile
        return carry

    lax.fori_loop(0, obs_count // 8, body, 0, unroll=2)
    total = parts[0][...]
    for part in parts[1:]:
        total = total + part[...]
    returned_ref[...] = total


def select_rows(index, rows, count):
    return pl.pallas_call(
        select_kernel,
        in_specs=[SMEM, VMEM],
        out_specs=VMEM,
        out_shape=jax.ShapeDtypeStruct((count, rows.shape[1]), jnp.float32),
    )(index, rows)


def place_rows(index, rows, cells):
    return pl.pallas_call(
        place_kernel,
        in_specs=[SMEM, VMEM],
        out_specs=VMEM,
        out_shape=jax.ShapeDtypeStruct((cells, rows.shape[1]), jnp.float32),
        scratch_shapes=[pltpu.VMEM((cells, rows.shape[1]), jnp.float32) for _ in range(4)],
        compiler_params=pltpu.CompilerParams(vmem_limit_bytes=60 * 1024 * 1024),
    )(index, rows)


def interpolate(obs_slots, obs_weights, received, precision_rows):
    obs_count = obs_slots.shape[1]
    return pl.pallas_call(
        interp_kernel,
        in_specs=[SMEM, SMEM, VMEM, VMEM],
        out_specs=[VMEM, VMEM],
        out_shape=[
            jax.ShapeDtypeStruct((obs_count, received.shape[1]), jnp.float32),
            jax.ShapeDtypeStruct(received.shape, jnp.float32),
        ],
        scratch_shapes=[
            pltpu.VMEM(received.shape, jnp.float32) for _ in range(obs_slots.shape[0])
        ],
        compiler_params=pltpu.CompilerParams(vmem_limit_bytes=60 * 1024 * 1024),
    )(obs_slots, obs_weights, received, precision_rows)


def to_owners(outgoing):
    return lax.all_to_all(outgoing, ("lon", "lat"), split_axis=0, concat_axis=0, tiled=True)


def to_sources(returned):
    return lax.all_to_all(returned, ("lon", "lat"), split_axis=0, concat_axis=0, tiled=True)


def on_device(state, diffusivity, sea_mask, send_cols, obs_slots, obs_weights, obs_precision):
    vals, rows, lanes = state.shape
    cell_count = rows * lanes
    steps = vals // GROUP
    sea_float = sea_mask.astype(jnp.float32)
    conduct = diffusivity * jnp.concatenate([sea_float, sea_float], axis=0)
    conduct_blocks = conduct.reshape(steps, GROUP * rows, lanes)
    smooth = diffuse(state, conduct_blocks)
    rows_of = smooth.transpose(1, 2, 0).reshape(cell_count, vals)
    send_index = send_cols[0]
    outgoing = select_rows(send_index, rows_of, send_index.shape[0])
    received = to_owners(outgoing)
    equivalent_rows, returned = interpolate(obs_slots, obs_weights, received, obs_precision.T)
    equivalents = equivalent_rows.T
    incoming = to_sources(returned)
    adjoint_rows = place_rows(send_index, incoming, cell_count)
    adjoint_field = adjoint_rows.reshape(rows, lanes, vals).transpose(2, 0, 1)
    product = state + diffuse(adjoint_field, conduct_blocks)
    return (product, equivalents)


def solution(mesh):
    placed = (
        P(None, "lat", "lon"),
        P(None, "lat", "lon"),
        P(None, "lat", "lon"),
        P(("lon", "lat"), None),
        P(None, ("lon", "lat")),
        P(None, ("lon", "lat")),
        P(None, ("lon", "lat")),
    )
    return jax.shard_map(
        on_device,
        mesh=mesh,
        in_specs=placed,
        out_specs=(P(None, "lat", "lon"), P(None, ("lon", "lat"))),
        check_vma=False,
    )
```

```python
import functools

import jax
import jax.numpy as jnp
from jax import lax
from jax.experimental import pallas as pl
from jax.experimental.pallas import tpu as pltpu
from jax.sharding import PartitionSpec as P

SWEEPS = 2
GROUP = 15
SMEM = pl.BlockSpec(memory_space=pltpu.SMEM)
VMEM = pl.BlockSpec(memory_space=pltpu.VMEM)


def conduct_slabs(d_ref, m_ref, rows):
    mask_groups = m_ref.shape[0]
    group = d_ref.shape[1] // rows

    def slab(g, r):
        spot = pl.ds(r, group, stride=rows)
        return d_ref[g, spot, :] * m_ref[g % mask_groups, spot, :].astype(jnp.float32)

    return slab


def coef_pass(rows, d_ref, m_ref, coef_halo, scales, k_ref):
    c_slab = conduct_slabs(d_ref, m_ref, rows)
    groups, span, lanes = d_ref.shape
    group = span // rows
    north_ok, south_ok = scales
    coef_rows, coef_cols = coef_halo

    def body(g, carry):
        lane = lax.broadcasted_iota(jnp.int32, (group, lanes), 1)
        cw = coef_cols[0, g]
        ce = coef_cols[1, g]
        c_up = coef_rows[0, g] * north_ok
        c_mid = c_slab(g, 0)
        for r in range(rows):
            if r + 1 < rows:
                c_dn = c_slab(g, r + 1)
            else:
                c_dn = coef_rows[1, g] * south_ok
            c_w = jnp.where(lane == 0, cw[:, r : r + 1], pltpu.roll(c_mid, 1, 1))
            c_e = jnp.where(lane == lanes - 1, ce[:, r : r + 1], pltpu.roll(c_mid, lanes - 1, 1))
            k_ref[0, g, r] = jnp.minimum(c_mid, c_up)
            k_ref[1, g, r] = jnp.minimum(c_mid, c_dn)
            k_ref[2, g, r] = jnp.minimum(c_mid, c_w)
            k_ref[3, g, r] = jnp.minimum(c_mid, c_e)
            c_up, c_mid = c_mid, c_dn
        return carry

    lax.fori_loop(0, groups, body, 0)


def slab_pass(rows, src_ref, k_ref, field_halo, scales, dst_ref, edges):
    groups, span, lanes = src_ref.shape
    group = span // rows
    north_ok, south_ok = scales
    row_halo, col_halo = field_halo

    def body(g, carry):
        lane = lax.broadcasted_iota(jnp.int32, (group, lanes), 1)
        col = lax.broadcasted_iota(jnp.int32, (group, rows), 1)

        def slab(ref, r):
            return ref[g, pl.ds(r, group, stride=rows), :]

        vw = col_halo[0, g]
        ve = col_halo[1, g]
        left = jnp.zeros((group, rows), jnp.float32)
        right = jnp.zeros((group, rows), jnp.float32)
        x_up = row_halo[0, g] * north_ok
        x_mid = slab(src_ref, 0)
        for r in range(rows):
            if r + 1 < rows:
                x_dn = slab(src_ref, r + 1)
            else:
                x_dn = row_halo[1, g] * south_ok
            x_w = jnp.where(lane == 0, vw[:, r : r + 1], pltpu.roll(x_mid, 1, 1))
            x_e = jnp.where(lane == lanes - 1, ve[:, r : r + 1], pltpu.roll(x_mid, lanes - 1, 1))
            total = k_ref[0, g, r] * (x_up - x_mid)
            total = total + k_ref[1, g, r] * (x_dn - x_mid)
            total = total + k_ref[2, g, r] * (x_w - x_mid)
            total = total + k_ref[3, g, r] * (x_e - x_mid)
            out = x_mid + total
            dst_ref[g, pl.ds(r, group, stride=rows), :] = out
            if edges is not None:
                if r == 0:
                    edges[0][0, g] = out
                if r == rows - 1:
                    edges[0][1, g] = out
                left = jnp.where(col == r, out[:, 0:1], left)
                right = jnp.where(col == r, out[:, lanes - 1 : lanes], right)
            x_up, x_mid = x_mid, x_dn
        if edges is not None:
            edges[1][0, g] = left
            edges[1][1, g] = right
        return carry

    lax.fori_loop(0, groups, body, 0)


def edge_pass(rows, src_ref, row_out, col_out, read=None):
    groups, span, lanes = src_ref.shape
    group = span // rows
    if read is None:
        read = lambda g, r: src_ref[g, pl.ds(r, group, stride=rows), :]

    def body(g, carry):
        col = lax.broadcasted_iota(jnp.int32, (group, rows), 1)
        left = jnp.zeros((group, rows), jnp.float32)
        right = jnp.zeros((group, rows), jnp.float32)
        for r in range(rows):
            x = read(g, r)
            if r == 0:
                row_out[0, g] = x
            if r == rows - 1:
                row_out[1, g] = x
            left = jnp.where(col == r, x[:, 0:1], left)
            right = jnp.where(col == r, x[:, lanes - 1 : lanes], right)
        col_out[0, g] = left
        col_out[1, g] = right
        return carry

    lax.fori_loop(0, groups, body, 0)


def diffuse_kernel(rows, v_ref, d_ref, m_ref, out_ref, mid_ref, k_ref, row_edge, col_edge, row_halo,
                   col_halo, send_sem, recv_sem):
    lon = lax.axis_index("lon")
    lat = lax.axis_index("lat")
    n_lon = lax.axis_size("lon")
    n_lat = lax.axis_size("lat")
    north = {"lat": (lat + n_lat - 1) % n_lat}
    south = {"lat": (lat + 1) % n_lat}
    west = {"lon": (lon + n_lon - 1) % n_lon}
    east = {"lon": (lon + 1) % n_lon}
    mesh_id = pl.DeviceIdType.MESH

    barrier = pltpu.get_barrier_semaphore()
    for peer in (north, south, west, east):
        pl.semaphore_signal(barrier, inc=1, device_id=peer, device_id_type=mesh_id)
    pl.semaphore_wait(barrier, 4)

    def exchange(rd):
        plan = [
            (row_edge.at[rd, 0], row_halo.at[rd, 1], north, 0),
            (row_edge.at[rd, 1], row_halo.at[rd, 0], south, 1),
            (col_edge.at[rd, 0], col_halo.at[rd, 1], west, 2),
            (col_edge.at[rd, 1], col_halo.at[rd, 0], east, 3),
        ]
        copies = []
        for src, dst, peer, k in plan:
            copy = pltpu.make_async_remote_copy(
                src_ref=src, dst_ref=dst, send_sem=send_sem.at[rd, k], recv_sem=recv_sem.at[rd, k],
                device_id=peer, device_id_type=mesh_id,
            )
            copy.start()
            copies.append(copy)
        return copies

    edge_pass(rows, d_ref, row_edge.at[0], col_edge.at[0], conduct_slabs(d_ref, m_ref, rows))
    edge_pass(rows, v_ref, row_edge.at[1], col_edge.at[1])
    first = exchange(0) + exchange(1)
    for copy in first:
        copy.wait()
    north_ok = jnp.minimum(lat, 1).astype(jnp.float32)
    south_ok = jnp.minimum(n_lat - 1 - lat, 1).astype(jnp.float32)
    scales = (north_ok, south_ok)
    coef_pass(rows, d_ref, m_ref, (row_halo.at[0], col_halo.at[0]), scales, k_ref)
    slab_pass(rows, v_ref, k_ref, (row_halo.at[1], col_halo.at[1]), scales, mid_ref,
              (row_edge.at[2], col_edge.at[2]))
    for copy in exchange(2):
        copy.wait()
    slab_pass(rows, mid_ref, k_ref, (row_halo.at[2], col_halo.at[2]), scales, out_ref, None)


def diffuse(field, diffusivity_blocks, mask_blocks):
    vals, rows, lanes = field.shape
    groups = vals // GROUP
    blocks = field.reshape(groups, GROUP * rows, lanes)
    rounds = SWEEPS + 1
    out = pl.pallas_call(
        functools.partial(diffuse_kernel, rows),
        in_specs=[VMEM, VMEM, VMEM],
        out_specs=VMEM,
        out_shape=jax.ShapeDtypeStruct(blocks.shape, jnp.float32),
        scratch_shapes=[
            pltpu.VMEM(blocks.shape, jnp.float32),
            pltpu.VMEM((4, groups, rows, GROUP, lanes), jnp.float32),
            pltpu.VMEM((rounds, 2, groups, GROUP, lanes), jnp.float32),
            pltpu.VMEM((rounds, 2, groups, GROUP, rows), jnp.float32),
            pltpu.VMEM((rounds, 2, groups, GROUP, lanes), jnp.float32),
            pltpu.VMEM((rounds, 2, groups, GROUP, rows), jnp.float32),
            pltpu.SemaphoreType.DMA((rounds, 4)),
            pltpu.SemaphoreType.DMA((rounds, 4)),
        ],
        compiler_params=pltpu.CompilerParams(collective_id=0, has_side_effects=True),
        cost_estimate=pl.CostEstimate(
            flops=50 * field.size, bytes_accessed=12 * field.size, transcendentals=0
        ),
    )(blocks, diffusivity_blocks, mask_blocks)
    return out.reshape(vals, rows, lanes)


def load_row(ref, index):
    return ref[pl.ds(index, 1), :]


def add_row(ref, index, value):
    spot = pl.ds(index, 1)
    ref[spot, :] = ref[spot, :] + value


def select_kernel(index_ref, rows_ref, out_ref):
    cells = rows_ref.shape[0]
    width = out_ref.shape[1]
    sub = lax.broadcasted_iota(jnp.int32, (8, width), 0)

    def body(t, carry):
        tile = jnp.zeros((8, width), jnp.float32)
        for i in range(8):
            source = index_ref[t * 8 + i]
            row = load_row(rows_ref, jnp.minimum(source, cells - 1))
            tile = jnp.where((sub == i) & (source < cells), jnp.broadcast_to(row, (8, width)), tile)
        out_ref[pl.ds(pl.multiple_of(t * 8, 8), 8), :] = tile
        return carry

    lax.fori_loop(0, out_ref.shape[0] // 8, body, 0, unroll=2)


def place_kernel(index_ref, rows_ref, out_ref, *parts):
    cells = out_ref.shape[0]
    for part in parts:
        part[...] = jnp.zeros_like(part)

    def body(t, carry):
        for i, part in enumerate(parts):
            q = t * len(parts) + i
            target = index_ref[q]
            row = load_row(rows_ref, q)
            add_row(part, jnp.minimum(target, cells - 1), jnp.where(target < cells, row, 0.0))
        return carry

    lax.fori_loop(0, rows_ref.shape[0] // len(parts), body, 0, unroll=2)
    total = parts[0][...]
    for part in parts[1:]:
        total = total + part[...]
    out_ref[...] = total


def interp_kernel(slot_ref, weight_ref, received_ref, precision_ref, equiv_ref, returned_ref, *parts):
    taps, obs_count = slot_ref.shape
    width = equiv_ref.shape[1]
    sub = lax.broadcasted_iota(jnp.int32, (8, width), 0)
    for part in parts:
        part[...] = jnp.zeros_like(part)

    def body(t, carry):
        tile = jnp.zeros((8, width), jnp.float32)
        for i in range(8):
            j = t * 8 + i
            slots = [slot_ref[k, j] for k in range(taps)]
            weights = [weight_ref[k, j] for k in range(taps)]
            total = load_row(received_ref, slots[0]) * weights[0]
            for k in range(1, taps):
                total = total + load_row(received_ref, slots[k]) * weights[k]
            tile = jnp.where(sub == i, jnp.broadcast_to(total, (8, width)), tile)
            weighted = load_row(precision_ref, j) * total
            for k in range(taps):
                add_row(parts[k], slots[k], weighted * weights[k])
        equiv_ref[pl.ds(pl.multiple_of(t * 8, 8), 8), :] = tile
        return carry

    lax.fori_loop(0, obs_count // 8, body, 0, unroll=2)
    total = parts[0][...]
    for part in parts[1:]:
        total = total + part[...]
    returned_ref[...] = total


def select_rows(index, rows, count):
    return pl.pallas_call(
        select_kernel,
        in_specs=[SMEM, VMEM],
        out_specs=VMEM,
        out_shape=jax.ShapeDtypeStruct((count, rows.shape[1]), jnp.float32),
    )(index, rows)


def place_rows(index, rows, cells):
    return pl.pallas_call(
        place_kernel,
        in_specs=[SMEM, VMEM],
        out_specs=VMEM,
        out_shape=jax.ShapeDtypeStruct((cells, rows.shape[1]), jnp.float32),
        scratch_shapes=[pltpu.VMEM((cells, rows.shape[1]), jnp.float32) for _ in range(4)],
        compiler_params=pltpu.CompilerParams(vmem_limit_bytes=60 * 1024 * 1024),
    )(index, rows)


def interpolate(obs_slots, obs_weights, received, precision_rows):
    obs_count = obs_slots.shape[1]
    return pl.pallas_call(
        interp_kernel,
        in_specs=[SMEM, SMEM, VMEM, VMEM],
        out_specs=[VMEM, VMEM],
        out_shape=[
            jax.ShapeDtypeStruct((obs_count, received.shape[1]), jnp.float32),
            jax.ShapeDtypeStruct(received.shape, jnp.float32),
        ],
        scratch_shapes=[
            pltpu.VMEM(received.shape, jnp.float32) for _ in range(obs_slots.shape[0])
        ],
        compiler_params=pltpu.CompilerParams(vmem_limit_bytes=60 * 1024 * 1024),
    )(obs_slots, obs_weights, received, precision_rows)


def to_owners(outgoing):
    return lax.all_to_all(outgoing, ("lon", "lat"), split_axis=0, concat_axis=0, tiled=True)


def to_sources(returned):
    return lax.all_to_all(returned, ("lon", "lat"), split_axis=0, concat_axis=0, tiled=True)


def on_device(state, diffusivity, sea_mask, send_cols, obs_slots, obs_weights, obs_precision):
    vals, rows, lanes = state.shape
    cell_count = rows * lanes
    steps = vals // GROUP
    diffusivity_blocks = diffusivity.reshape(steps, GROUP * rows, lanes)
    mask_blocks = sea_mask.reshape(sea_mask.shape[0] // GROUP, GROUP * rows, lanes)
    smooth = diffuse(state, diffusivity_blocks, mask_blocks)
    rows_of = smooth.transpose(1, 2, 0).reshape(cell_count, vals)
    send_index = send_cols[0]
    outgoing = select_rows(send_index, rows_of, send_index.shape[0])
    received = to_owners(outgoing)
    equivalent_rows, returned = interpolate(obs_slots, obs_weights, received, obs_precision.T)
    equivalents = equivalent_rows.T
    incoming = to_sources(returned)
    adjoint_rows = place_rows(send_index, incoming, cell_count)
    adjoint_field = adjoint_rows.reshape(rows, lanes, vals).transpose(2, 0, 1)
    product = state + diffuse(adjoint_field, diffusivity_blocks, mask_blocks)
    return (product, equivalents)


def solution(mesh):
    placed = (
        P(None, "lat", "lon"),
        P(None, "lat", "lon"),
        P(None, "lat", "lon"),
        P(("lon", "lat"), None),
        P(None, ("lon", "lat")),
        P(None, ("lon", "lat")),
        P(None, ("lon", "lat")),
    )
    return jax.shard_map(
        on_device,
        mesh=mesh,
        in_specs=placed,
        out_specs=(P(None, "lat", "lon"), P(None, ("lon", "lat"))),
        check_vma=False,
    )
```

```python
import functools

import jax
import jax.numpy as jnp
from jax import lax
from jax.experimental import pallas as pl
from jax.experimental.pallas import tpu as pltpu
from jax.sharding import PartitionSpec as P

SWEEPS = 2
GROUP = 30
SMEM = pl.BlockSpec(memory_space=pltpu.SMEM)
VMEM = pl.BlockSpec(memory_space=pltpu.VMEM)


def coef_pass(rows, c_ref, coef_halo, scales, k_ref):
    groups, span, lanes = c_ref.shape
    group = span // rows
    north_ok, south_ok = scales
    coef_rows, coef_cols = coef_halo

    def body(g, carry):
        lane = lax.broadcasted_iota(jnp.int32, (group, lanes), 1)
        cw = coef_cols[0, g]
        ce = coef_cols[1, g]
        c_up = coef_rows[0, g] * north_ok
        c_mid = c_ref[g, pl.ds(0, group, stride=rows), :]
        for r in range(rows):
            if r + 1 < rows:
                c_dn = c_ref[g, pl.ds(r + 1, group, stride=rows), :]
            else:
                c_dn = coef_rows[1, g] * south_ok
            c_w = jnp.where(lane == 0, cw[:, r : r + 1], pltpu.roll(c_mid, 1, 1))
            c_e = jnp.where(lane == lanes - 1, ce[:, r : r + 1], pltpu.roll(c_mid, lanes - 1, 1))
            k_ref[0, g, r] = jnp.minimum(c_mid, c_up)
            k_ref[1, g, r] = jnp.minimum(c_mid, c_dn)
            k_ref[2, g, r] = jnp.minimum(c_mid, c_w)
            k_ref[3, g, r] = jnp.minimum(c_mid, c_e)
            c_up, c_mid = c_mid, c_dn
        return carry

    lax.fori_loop(0, groups, body, 0)


def slab_pass(rows, src_ref, k_ref, field_halo, scales, dst_ref, edges, base_ref=None):
    groups, span, lanes = src_ref.shape
    group = span // rows
    north_ok, south_ok = scales
    row_halo, col_halo = field_halo

    def body(g, carry):
        lane = lax.broadcasted_iota(jnp.int32, (group, lanes), 1)
        col = lax.broadcasted_iota(jnp.int32, (group, rows), 1)

        def slab(ref, r):
            return ref[g, pl.ds(r, group, stride=rows), :]

        vw = col_halo[0, g]
        ve = col_halo[1, g]
        left = jnp.zeros((group, rows), jnp.float32)
        right = jnp.zeros((group, rows), jnp.float32)
        x_up = row_halo[0, g] * north_ok
        x_mid = slab(src_ref, 0)
        for r in range(rows):
            if r + 1 < rows:
                x_dn = slab(src_ref, r + 1)
            else:
                x_dn = row_halo[1, g] * south_ok
            x_w = jnp.where(lane == 0, vw[:, r : r + 1], pltpu.roll(x_mid, 1, 1))
            x_e = jnp.where(lane == lanes - 1, ve[:, r : r + 1], pltpu.roll(x_mid, lanes - 1, 1))
            total = k_ref[0, g, r] * (x_up - x_mid)
            total = total + k_ref[1, g, r] * (x_dn - x_mid)
            total = total + k_ref[2, g, r] * (x_w - x_mid)
            total = total + k_ref[3, g, r] * (x_e - x_mid)
            out = x_mid + total
            if base_ref is None:
                dst_ref[g, pl.ds(r, group, stride=rows), :] = out
            else:
                dst_ref[g, pl.ds(r, group, stride=rows), :] = slab(base_ref, r) + out
            if edges is not None:
                if r == 0:
                    edges[0][0, g] = out
                if r == rows - 1:
                    edges[0][1, g] = out
                left = jnp.where(col == r, out[:, 0:1], left)
                right = jnp.where(col == r, out[:, lanes - 1 : lanes], right)
            x_up, x_mid = x_mid, x_dn
        if edges is not None:
            edges[1][0, g] = left
            edges[1][1, g] = right
        return carry

    lax.fori_loop(0, groups, body, 0)


def edge_pass(rows, src_ref, row_out, col_out):
    groups, span, lanes = src_ref.shape
    group = span // rows

    def body(g, carry):
        col = lax.broadcasted_iota(jnp.int32, (group, rows), 1)
        left = jnp.zeros((group, rows), jnp.float32)
        right = jnp.zeros((group, rows), jnp.float32)
        for r in range(rows):
            x = src_ref[g, pl.ds(r, group, stride=rows), :]
            if r == 0:
                row_out[0, g] = x
            if r == rows - 1:
                row_out[1, g] = x
            left = jnp.where(col == r, x[:, 0:1], left)
            right = jnp.where(col == r, x[:, lanes - 1 : lanes], right)
        col_out[0, g] = left
        col_out[1, g] = right
        return carry

    lax.fori_loop(0, groups, body, 0)


def diffuse_kernel(rows, v_ref, c_ref, *refs):
    if len(refs) == 10:
        base_ref, refs = refs[0], refs[1:]
    else:
        base_ref = None
    out_ref, mid_ref, k_ref, row_edge, col_edge, row_halo, col_halo, send_sem, recv_sem = refs
    lon = lax.axis_index("lon")
    lat = lax.axis_index("lat")
    n_lon = lax.axis_size("lon")
    n_lat = lax.axis_size("lat")
    north = {"lat": (lat + n_lat - 1) % n_lat}
    south = {"lat": (lat + 1) % n_lat}
    west = {"lon": (lon + n_lon - 1) % n_lon}
    east = {"lon": (lon + 1) % n_lon}
    mesh_id = pl.DeviceIdType.MESH

    barrier = pltpu.get_barrier_semaphore()
    for peer in (north, south, west, east):
        pl.semaphore_signal(barrier, inc=1, device_id=peer, device_id_type=mesh_id)
    pl.semaphore_wait(barrier, 4)

    def exchange(rd):
        plan = [
            (row_edge.at[rd, 0], row_halo.at[rd, 1], north, 0),
            (row_edge.at[rd, 1], row_halo.at[rd, 0], south, 1),
            (col_edge.at[rd, 0], col_halo.at[rd, 1], west, 2),
            (col_edge.at[rd, 1], col_halo.at[rd, 0], east, 3),
        ]
        copies = []
        for src, dst, peer, k in plan:
            copy = pltpu.make_async_remote_copy(
                src_ref=src, dst_ref=dst, send_sem=send_sem.at[rd, k], recv_sem=recv_sem.at[rd, k],
                device_id=peer, device_id_type=mesh_id,
            )
            copy.start()
            copies.append(copy)
        return copies

    edge_pass(rows, c_ref, row_edge.at[0], col_edge.at[0])
    edge_pass(rows, v_ref, row_edge.at[1], col_edge.at[1])
    first = exchange(0) + exchange(1)
    for copy in first:
        copy.wait()
    north_ok = jnp.minimum(lat, 1).astype(jnp.float32)
    south_ok = jnp.minimum(n_lat - 1 - lat, 1).astype(jnp.float32)
    scales = (north_ok, south_ok)
    coef_pass(rows, c_ref, (row_halo.at[0], col_halo.at[0]), scales, k_ref)
    slab_pass(rows, v_ref, k_ref, (row_halo.at[1], col_halo.at[1]), scales, mid_ref,
              (row_edge.at[2], col_edge.at[2]))
    for copy in exchange(2):
        copy.wait()
    slab_pass(rows, mid_ref, k_ref, (row_halo.at[2], col_halo.at[2]), scales, out_ref, None, base_ref)


def diffuse(field, conduct_blocks, base=None):
    vals, rows, lanes = field.shape
    groups = vals // GROUP
    blocks = field.reshape(groups, GROUP * rows, lanes)
    rounds = SWEEPS + 1
    operands = [blocks, conduct_blocks]
    if base is not None:
        operands.append(base.reshape(blocks.shape))
    out = pl.pallas_call(
        functools.partial(diffuse_kernel, rows),
        in_specs=[VMEM] * len(operands),
        out_specs=VMEM,
        out_shape=jax.ShapeDtypeStruct(blocks.shape, jnp.float32),
        scratch_shapes=[
            pltpu.VMEM(blocks.shape, jnp.float32),
            pltpu.VMEM((4, groups, rows, GROUP, lanes), jnp.float32),
            pltpu.VMEM((rounds, 2, groups, GROUP, lanes), jnp.float32),
            pltpu.VMEM((rounds, 2, groups, GROUP, rows), jnp.float32),
            pltpu.VMEM((rounds, 2, groups, GROUP, lanes), jnp.float32),
            pltpu.VMEM((rounds, 2, groups, GROUP, rows), jnp.float32),
            pltpu.SemaphoreType.DMA((rounds, 4)),
            pltpu.SemaphoreType.DMA((rounds, 4)),
        ],
        compiler_params=pltpu.CompilerParams(
            collective_id=0 if base is None else 1, has_side_effects=True
        ),
        cost_estimate=pl.CostEstimate(
            flops=50 * field.size, bytes_accessed=12 * field.size, transcendentals=0
        ),
    )(*operands)
    return out.reshape(vals, rows, lanes)


def load_row(ref, index):
    return ref[pl.ds(index, 1), :]


def add_row(ref, index, value):
    spot = pl.ds(index, 1)
    ref[spot, :] = ref[spot, :] + value


def select_kernel(index_ref, rows_ref, out_ref):
    cells = rows_ref.shape[0]
    width = out_ref.shape[1]
    sub = lax.broadcasted_iota(jnp.int32, (8, width), 0)

    def body(t, carry):
        tile = jnp.zeros((8, width), jnp.float32)
        for i in range(8):
            source = index_ref[t * 8 + i]
            row = load_row(rows_ref, jnp.minimum(source, cells - 1))
            tile = jnp.where((sub == i) & (source < cells), jnp.broadcast_to(row, (8, width)), tile)
        out_ref[pl.ds(pl.multiple_of(t * 8, 8), 8), :] = tile
        return carry

    lax.fori_loop(0, out_ref.shape[0] // 8, body, 0, unroll=2)


def place_kernel(index_ref, rows_ref, out_ref, *parts):
    cells = out_ref.shape[0]
    for part in parts:
        part[...] = jnp.zeros_like(part)

    def body(t, carry):
        for i, part in enumerate(parts):
            q = t * len(parts) + i
            target = index_ref[q]
            row = load_row(rows_ref, q)
            add_row(part, jnp.minimum(target, cells - 1), jnp.where(target < cells, row, 0.0))
        return carry

    lax.fori_loop(0, rows_ref.shape[0] // len(parts), body, 0, unroll=2)
    total = parts[0][...]
    for part in parts[1:]:
        total = total + part[...]
    out_ref[...] = total


def interp_kernel(slot_ref, weight_ref, received_ref, precision_ref, equiv_ref, returned_ref, *parts):
    taps, obs_count = slot_ref.shape
    width = equiv_ref.shape[1]
    sub = lax.broadcasted_iota(jnp.int32, (8, width), 0)
    for part in parts:
        part[...] = jnp.zeros_like(part)

    def body(t, carry):
        tile = jnp.zeros((8, width), jnp.float32)
        for i in range(8):
            j = t * 8 + i
            slots = [slot_ref[k, j] for k in range(taps)]
            weights = [weight_ref[k, j] for k in range(taps)]
            total = load_row(received_ref, slots[0]) * weights[0]
            for k in range(1, taps):
                total = total + load_row(received_ref, slots[k]) * weights[k]
            tile = jnp.where(sub == i, jnp.broadcast_to(total, (8, width)), tile)
            weighted = load_row(precision_ref, j) * total
            for k in range(taps):
                add_row(parts[k], slots[k], weighted * weights[k])
        equiv_ref[pl.ds(pl.multiple_of(t * 8, 8), 8), :] = tile
        return carry

    lax.fori_loop(0, obs_count // 8, body, 0, unroll=2)
    total = parts[0][...]
    for part in parts[1:]:
        total = total + part[...]
    returned_ref[...] = total


def select_rows(index, rows, count):
    return pl.pallas_call(
        select_kernel,
        in_specs=[SMEM, VMEM],
        out_specs=VMEM,
        out_shape=jax.ShapeDtypeStruct((count, rows.shape[1]), jnp.float32),
    )(index, rows)


def place_rows(index, rows, cells):
    return pl.pallas_call(
        place_kernel,
        in_specs=[SMEM, VMEM],
        out_specs=VMEM,
        out_shape=jax.ShapeDtypeStruct((cells, rows.shape[1]), jnp.float32),
        scratch_shapes=[pltpu.VMEM((cells, rows.shape[1]), jnp.float32) for _ in range(4)],
        compiler_params=pltpu.CompilerParams(vmem_limit_bytes=60 * 1024 * 1024),
    )(index, rows)


def interpolate(obs_slots, obs_weights, received, precision_rows):
    obs_count = obs_slots.shape[1]
    return pl.pallas_call(
        interp_kernel,
        in_specs=[SMEM, SMEM, VMEM, VMEM],
        out_specs=[VMEM, VMEM],
        out_shape=[
            jax.ShapeDtypeStruct((obs_count, received.shape[1]), jnp.float32),
            jax.ShapeDtypeStruct(received.shape, jnp.float32),
        ],
        scratch_shapes=[
            pltpu.VMEM(received.shape, jnp.float32) for _ in range(obs_slots.shape[0])
        ],
        compiler_params=pltpu.CompilerParams(vmem_limit_bytes=60 * 1024 * 1024),
    )(obs_slots, obs_weights, received, precision_rows)


def to_owners(outgoing):
    return lax.all_to_all(outgoing, ("lon", "lat"), split_axis=0, concat_axis=0, tiled=True)


def to_sources(returned):
    return lax.all_to_all(returned, ("lon", "lat"), split_axis=0, concat_axis=0, tiled=True)


def on_device(state, diffusivity, sea_mask, send_cols, obs_slots, obs_weights, obs_precision):
    vals, rows, lanes = state.shape
    cell_count = rows * lanes
    steps = vals // GROUP
    sea_float = sea_mask.astype(jnp.float32)
    conduct = diffusivity * jnp.concatenate([sea_float, sea_float], axis=0)
    conduct_blocks = conduct.reshape(steps, GROUP * rows, lanes)
    smooth = diffuse(state, conduct_blocks)
    rows_of = smooth.transpose(1, 2, 0).reshape(cell_count, vals)
    send_index = send_cols[0]
    outgoing = select_rows(send_index, rows_of, send_index.shape[0])
    received = to_owners(outgoing)
    equivalent_rows, returned = interpolate(obs_slots, obs_weights, received, obs_precision.T)
    equivalents = equivalent_rows.T
    incoming = to_sources(returned)
    adjoint_rows = place_rows(send_index, incoming, cell_count)
    adjoint_field = adjoint_rows.reshape(rows, lanes, vals).transpose(2, 0, 1)
    product = diffuse(adjoint_field, conduct_blocks, state)
    return (product, equivalents)


def solution(mesh):
    placed = (
        P(None, "lat", "lon"),
        P(None, "lat", "lon"),
        P(None, "lat", "lon"),
        P(("lon", "lat"), None),
        P(None, ("lon", "lat")),
        P(None, ("lon", "lat")),
        P(None, ("lon", "lat")),
    )
    return jax.shard_map(
        on_device,
        mesh=mesh,
        in_specs=placed,
        out_specs=(P(None, "lat", "lon"), P(None, ("lon", "lat"))),
        check_vma=False,
    )
```

```python
import functools

import jax
import jax.numpy as jnp
from jax import lax
from jax.experimental import pallas as pl
from jax.experimental.pallas import tpu as pltpu
from jax.sharding import PartitionSpec as P

SWEEPS = 2
GROUP = 30
SMEM = pl.BlockSpec(memory_space=pltpu.SMEM)
VMEM = pl.BlockSpec(memory_space=pltpu.VMEM)


def coef_pass(rows, c_ref, coef_halo, scales, k_ref):
    groups, span, lanes = c_ref.shape
    group = span // rows
    north_ok, south_ok = scales
    coef_rows, coef_cols = coef_halo

    def body(g, carry):
        lane = lax.broadcasted_iota(jnp.int32, (group, lanes), 1)
        cw = coef_cols[0, g]
        ce = coef_cols[1, g]
        c_up = coef_rows[0, g] * north_ok
        c_mid = c_ref[g, pl.ds(0, group, stride=rows), :]
        for r in range(rows):
            if r + 1 < rows:
                c_dn = c_ref[g, pl.ds(r + 1, group, stride=rows), :]
            else:
                c_dn = coef_rows[1, g] * south_ok
            c_w = jnp.where(lane == 0, cw[:, r : r + 1], pltpu.roll(c_mid, 1, 1))
            c_e = jnp.where(lane == lanes - 1, ce[:, r : r + 1], pltpu.roll(c_mid, lanes - 1, 1))
            k_ref[0, g, r] = jnp.minimum(c_mid, c_up)
            k_ref[1, g, r] = jnp.minimum(c_mid, c_dn)
            k_ref[2, g, r] = jnp.minimum(c_mid, c_w)
            k_ref[3, g, r] = jnp.minimum(c_mid, c_e)
            c_up, c_mid = c_mid, c_dn
        return carry

    lax.fori_loop(0, groups, body, 0)


def slab_pass(rows, src_ref, k_ref, field_halo, scales, dst_ref, edges):
    groups, span, lanes = src_ref.shape
    group = span // rows
    north_ok, south_ok = scales
    row_halo, col_halo = field_halo

    def body(g, carry):
        lane = lax.broadcasted_iota(jnp.int32, (group, lanes), 1)
        col = lax.broadcasted_iota(jnp.int32, (group, rows), 1)

        def slab(ref, r):
            return ref[g, pl.ds(r, group, stride=rows), :]

        vw = col_halo[0, g]
        ve = col_halo[1, g]
        left = jnp.zeros((group, rows), jnp.float32)
        right = jnp.zeros((group, rows), jnp.float32)
        x_up = row_halo[0, g] * north_ok
        x_mid = slab(src_ref, 0)
        for r in range(rows):
            if r + 1 < rows:
                x_dn = slab(src_ref, r + 1)
            else:
                x_dn = row_halo[1, g] * south_ok
            x_w = jnp.where(lane == 0, vw[:, r : r + 1], pltpu.roll(x_mid, 1, 1))
            x_e = jnp.where(lane == lanes - 1, ve[:, r : r + 1], pltpu.roll(x_mid, lanes - 1, 1))
            total = k_ref[0, g, r] * (x_up - x_mid)
            total = total + k_ref[1, g, r] * (x_dn - x_mid)
            total = total + k_ref[2, g, r] * (x_w - x_mid)
            total = total + k_ref[3, g, r] * (x_e - x_mid)
            out = x_mid + total
            dst_ref[g, pl.ds(r, group, stride=rows), :] = out
            if edges is not None:
                if r == 0:
                    edges[0][0, g] = out
                if r == rows - 1:
                    edges[0][1, g] = out
                left = jnp.where(col == r, out[:, 0:1], left)
                right = jnp.where(col == r, out[:, lanes - 1 : lanes], right)
            x_up, x_mid = x_mid, x_dn
        if edges is not None:
            edges[1][0, g] = left
            edges[1][1, g] = right
        return carry

    lax.fori_loop(0, groups, body, 0)


def edge_pass(rows, src_ref, row_out, col_out):
    groups, span, lanes = src_ref.shape
    group = span // rows

    def body(g, carry):
        col = lax.broadcasted_iota(jnp.int32, (group, rows), 1)
        left = jnp.zeros((group, rows), jnp.float32)
        right = jnp.zeros((group, rows), jnp.float32)
        for r in range(rows):
            x = src_ref[g, pl.ds(r, group, stride=rows), :]
            if r == 0:
                row_out[0, g] = x
            if r == rows - 1:
                row_out[1, g] = x
            left = jnp.where(col == r, x[:, 0:1], left)
            right = jnp.where(col == r, x[:, lanes - 1 : lanes], right)
        col_out[0, g] = left
        col_out[1, g] = right
        return carry

    lax.fori_loop(0, groups, body, 0)


def diffuse_kernel(rows, v_ref, c_ref, out_ref, mid_ref, k_ref, row_edge, col_edge, row_halo,
                   col_halo, send_sem, recv_sem):
    lon = lax.axis_index("lon")
    lat = lax.axis_index("lat")
    n_lon = lax.axis_size("lon")
    n_lat = lax.axis_size("lat")
    north = {"lat": (lat + n_lat - 1) % n_lat}
    south = {"lat": (lat + 1) % n_lat}
    west = {"lon": (lon + n_lon - 1) % n_lon}
    east = {"lon": (lon + 1) % n_lon}
    mesh_id = pl.DeviceIdType.MESH

    barrier = pltpu.get_barrier_semaphore()
    for peer in (north, south, west, east):
        pl.semaphore_signal(barrier, inc=1, device_id=peer, device_id_type=mesh_id)
    pl.semaphore_wait(barrier, 4)

    def exchange(rd):
        plan = [
            (row_edge.at[rd, 0], row_halo.at[rd, 1], north, 0),
            (row_edge.at[rd, 1], row_halo.at[rd, 0], south, 1),
            (col_edge.at[rd, 0], col_halo.at[rd, 1], west, 2),
            (col_edge.at[rd, 1], col_halo.at[rd, 0], east, 3),
        ]
        copies = []
        for src, dst, peer, k in plan:
            copy = pltpu.make_async_remote_copy(
                src_ref=src, dst_ref=dst, send_sem=send_sem.at[rd, k], recv_sem=recv_sem.at[rd, k],
                device_id=peer, device_id_type=mesh_id,
            )
            copy.start()
            copies.append(copy)
        return copies

    edge_pass(rows, c_ref, row_edge.at[0], col_edge.at[0])
    edge_pass(rows, v_ref, row_edge.at[1], col_edge.at[1])
    first = exchange(0) + exchange(1)
    for copy in first:
        copy.wait()
    north_ok = jnp.minimum(lat, 1).astype(jnp.float32)
    south_ok = jnp.minimum(n_lat - 1 - lat, 1).astype(jnp.float32)
    scales = (north_ok, south_ok)
    coef_pass(rows, c_ref, (row_halo.at[0], col_halo.at[0]), scales, k_ref)
    slab_pass(rows, v_ref, k_ref, (row_halo.at[1], col_halo.at[1]), scales, mid_ref,
              (row_edge.at[2], col_edge.at[2]))
    for copy in exchange(2):
        copy.wait()
    slab_pass(rows, mid_ref, k_ref, (row_halo.at[2], col_halo.at[2]), scales, out_ref, None)


def diffuse(field, conduct_blocks):
    vals, rows, lanes = field.shape
    groups = vals // GROUP
    blocks = field.reshape(groups, GROUP * rows, lanes)
    rounds = SWEEPS + 1
    out = pl.pallas_call(
        functools.partial(diffuse_kernel, rows),
        in_specs=[VMEM, VMEM],
        out_specs=VMEM,
        out_shape=jax.ShapeDtypeStruct(blocks.shape, jnp.float32),
        scratch_shapes=[
            pltpu.VMEM(blocks.shape, jnp.float32),
            pltpu.VMEM((4, groups, rows, GROUP, lanes), jnp.float32),
            pltpu.VMEM((rounds, 2, groups, GROUP, lanes), jnp.float32),
            pltpu.VMEM((rounds, 2, groups, GROUP, rows), jnp.float32),
            pltpu.VMEM((rounds, 2, groups, GROUP, lanes), jnp.float32),
            pltpu.VMEM((rounds, 2, groups, GROUP, rows), jnp.float32),
            pltpu.SemaphoreType.DMA((rounds, 4)),
            pltpu.SemaphoreType.DMA((rounds, 4)),
        ],
        compiler_params=pltpu.CompilerParams(collective_id=0, has_side_effects=True),
        cost_estimate=pl.CostEstimate(
            flops=50 * field.size, bytes_accessed=12 * field.size, transcendentals=0
        ),
    )(blocks, conduct_blocks)
    return out.reshape(vals, rows, lanes)


def load_row(ref, index):
    return ref[pl.ds(index, 1), :]


def add_row(ref, index, value):
    spot = pl.ds(index, 1)
    ref[spot, :] = ref[spot, :] + value


def select_kernel(index_ref, rows_ref, out_ref):
    cells = rows_ref.shape[0]
    width = out_ref.shape[1]
    sub = lax.broadcasted_iota(jnp.int32, (8, width), 0)

    def body(t, carry):
        tile = jnp.zeros((8, width), jnp.float32)
        for i in range(8):
            source = index_ref[t * 8 + i]
            row = load_row(rows_ref, jnp.minimum(source, cells - 1))
            tile = jnp.where((sub == i) & (source < cells), jnp.broadcast_to(row, (8, width)), tile)
        out_ref[pl.ds(pl.multiple_of(t * 8, 8), 8), :] = tile
        return carry

    lax.fori_loop(0, out_ref.shape[0] // 8, body, 0, unroll=4)


def place_kernel(index_ref, rows_ref, out_ref, *parts):
    cells = out_ref.shape[0]
    for part in parts:
        part[...] = jnp.zeros_like(part)

    def body(t, carry):
        for i, part in enumerate(parts):
            q = t * len(parts) + i
            target = index_ref[q]
            row = load_row(rows_ref, q)
            add_row(part, jnp.minimum(target, cells - 1), jnp.where(target < cells, row, 0.0))
        return carry

    lax.fori_loop(0, rows_ref.shape[0] // len(parts), body, 0, unroll=4)
    total = parts[0][...]
    for part in parts[1:]:
        total = total + part[...]
    out_ref[...] = total


def interp_kernel(slot_ref, weight_ref, received_ref, precision_ref, equiv_ref, returned_ref, *parts):
    taps, obs_count = slot_ref.shape
    width = equiv_ref.shape[1]
    sub = lax.broadcasted_iota(jnp.int32, (8, width), 0)
    for part in parts:
        part[...] = jnp.zeros_like(part)

    def body(t, carry):
        tile = jnp.zeros((8, width), jnp.float32)
        for i in range(8):
            j = t * 8 + i
            slots = [slot_ref[k, j] for k in range(taps)]
            weights = [weight_ref[k, j] for k in range(taps)]
            total = load_row(received_ref, slots[0]) * weights[0]
            for k in range(1, taps):
                total = total + load_row(received_ref, slots[k]) * weights[k]
            tile = jnp.where(sub == i, jnp.broadcast_to(total, (8, width)), tile)
            weighted = load_row(precision_ref, j) * total
            for k in range(taps):
                add_row(parts[k], slots[k], weighted * weights[k])
        equiv_ref[pl.ds(pl.multiple_of(t * 8, 8), 8), :] = tile
        return carry

    lax.fori_loop(0, obs_count // 8, body, 0, unroll=2)
    total = parts[0][...]
    for part in parts[1:]:
        total = total + part[...]
    returned_ref[...] = total


def select_rows(index, rows, count):
    return pl.pallas_call(
        select_kernel,
        in_specs=[SMEM, VMEM],
        out_specs=VMEM,
        out_shape=jax.ShapeDtypeStruct((count, rows.shape[1]), jnp.float32),
    )(index, rows)


def place_rows(index, rows, cells):
    return pl.pallas_call(
        place_kernel,
        in_specs=[SMEM, VMEM],
        out_specs=VMEM,
        out_shape=jax.ShapeDtypeStruct((cells, rows.shape[1]), jnp.float32),
        scratch_shapes=[pltpu.VMEM((cells, rows.shape[1]), jnp.float32) for _ in range(4)],
        compiler_params=pltpu.CompilerParams(vmem_limit_bytes=60 * 1024 * 1024),
    )(index, rows)


def interpolate(obs_slots, obs_weights, received, precision_rows):
    obs_count = obs_slots.shape[1]
    return pl.pallas_call(
        interp_kernel,
        in_specs=[SMEM, SMEM, VMEM, VMEM],
        out_specs=[VMEM, VMEM],
        out_shape=[
            jax.ShapeDtypeStruct((obs_count, received.shape[1]), jnp.float32),
            jax.ShapeDtypeStruct(received.shape, jnp.float32),
        ],
        scratch_shapes=[
            pltpu.VMEM(received.shape, jnp.float32) for _ in range(obs_slots.shape[0])
        ],
        compiler_params=pltpu.CompilerParams(vmem_limit_bytes=60 * 1024 * 1024),
    )(obs_slots, obs_weights, received, precision_rows)


def to_owners(outgoing):
    return lax.all_to_all(outgoing, ("lon", "lat"), split_axis=0, concat_axis=0, tiled=True)


def to_sources(returned):
    return lax.all_to_all(returned, ("lon", "lat"), split_axis=0, concat_axis=0, tiled=True)


def on_device(state, diffusivity, sea_mask, send_cols, obs_slots, obs_weights, obs_precision):
    vals, rows, lanes = state.shape
    cell_count = rows * lanes
    steps = vals // GROUP
    sea_float = sea_mask.astype(jnp.float32)
    conduct = diffusivity * jnp.concatenate([sea_float, sea_float], axis=0)
    conduct_blocks = conduct.reshape(steps, GROUP * rows, lanes)
    smooth = diffuse(state, conduct_blocks)
    rows_of = smooth.transpose(1, 2, 0).reshape(cell_count, vals)
    send_index = send_cols[0]
    outgoing = select_rows(send_index, rows_of, send_index.shape[0])
    received = to_owners(outgoing)
    equivalent_rows, returned = interpolate(obs_slots, obs_weights, received, obs_precision.T)
    equivalents = equivalent_rows.T
    incoming = to_sources(returned)
    adjoint_rows = place_rows(send_index, incoming, cell_count)
    adjoint_field = adjoint_rows.reshape(rows, lanes, vals).transpose(2, 0, 1)
    product = state + diffuse(adjoint_field, conduct_blocks)
    return (product, equivalents)


def solution(mesh):
    placed = (
        P(None, "lat", "lon"),
        P(None, "lat", "lon"),
        P(None, "lat", "lon"),
        P(("lon", "lat"), None),
        P(None, ("lon", "lat")),
        P(None, ("lon", "lat")),
        P(None, ("lon", "lat")),
    )
    return jax.shard_map(
        on_device,
        mesh=mesh,
        in_specs=placed,
        out_specs=(P(None, "lat", "lon"), P(None, ("lon", "lat"))),
        check_vma=False,
    )
```

```python
import functools

import jax
import jax.numpy as jnp
from jax import lax
from jax.experimental import pallas as pl
from jax.experimental.pallas import tpu as pltpu
from jax.sharding import PartitionSpec as P

SWEEPS = 2
GROUP = 30
SMEM = pl.BlockSpec(memory_space=pltpu.SMEM)
VMEM = pl.BlockSpec(memory_space=pltpu.VMEM)


def coef_pass(rows, c_ref, coef_halo, scales, k_ref):
    groups, span, lanes = c_ref.shape
    group = span // rows
    north_ok, south_ok = scales
    coef_rows, coef_cols = coef_halo

    def body(g, carry):
        lane = lax.broadcasted_iota(jnp.int32, (group, lanes), 1)
        cw = coef_cols[0, g]
        ce = coef_cols[1, g]
        c_up = coef_rows[0, g] * north_ok
        c_mid = c_ref[g, pl.ds(0, group, stride=rows), :]
        for r in range(rows):
            if r + 1 < rows:
                c_dn = c_ref[g, pl.ds(r + 1, group, stride=rows), :]
            else:
                c_dn = coef_rows[1, g] * south_ok
            c_w = jnp.where(lane == 0, cw[:, r : r + 1], pltpu.roll(c_mid, 1, 1))
            c_e = jnp.where(lane == lanes - 1, ce[:, r : r + 1], pltpu.roll(c_mid, lanes - 1, 1))
            k_ref[0, g, r] = jnp.minimum(c_mid, c_up)
            k_ref[1, g, r] = jnp.minimum(c_mid, c_dn)
            k_ref[2, g, r] = jnp.minimum(c_mid, c_w)
            k_ref[3, g, r] = jnp.minimum(c_mid, c_e)
            c_up, c_mid = c_mid, c_dn
        return carry

    lax.fori_loop(0, groups, body, 0)


def slab_pass(rows, src_ref, k_ref, field_halo, scales, dst_ref, edges):
    groups, span, lanes = src_ref.shape
    group = span // rows
    north_ok, south_ok = scales
    row_halo, col_halo = field_halo

    def body(g, carry):
        lane = lax.broadcasted_iota(jnp.int32, (group, lanes), 1)
        col = lax.broadcasted_iota(jnp.int32, (group, rows), 1)

        def slab(ref, r):
            return ref[g, pl.ds(r, group, stride=rows), :]

        vw = col_halo[0, g]
        ve = col_halo[1, g]
        left = jnp.zeros((group, rows), jnp.float32)
        right = jnp.zeros((group, rows), jnp.float32)
        x_up = row_halo[0, g] * north_ok
        x_mid = slab(src_ref, 0)
        for r in range(rows):
            if r + 1 < rows:
                x_dn = slab(src_ref, r + 1)
            else:
                x_dn = row_halo[1, g] * south_ok
            x_w = jnp.where(lane == 0, vw[:, r : r + 1], pltpu.roll(x_mid, 1, 1))
            x_e = jnp.where(lane == lanes - 1, ve[:, r : r + 1], pltpu.roll(x_mid, lanes - 1, 1))
            total = k_ref[0, g, r] * (x_up - x_mid)
            total = total + k_ref[1, g, r] * (x_dn - x_mid)
            total = total + k_ref[2, g, r] * (x_w - x_mid)
            total = total + k_ref[3, g, r] * (x_e - x_mid)
            out = x_mid + total
            dst_ref[g, pl.ds(r, group, stride=rows), :] = out
            if edges is not None:
                if r == 0:
                    edges[0][0, g] = out
                if r == rows - 1:
                    edges[0][1, g] = out
                left = jnp.where(col == r, out[:, 0:1], left)
                right = jnp.where(col == r, out[:, lanes - 1 : lanes], right)
            x_up, x_mid = x_mid, x_dn
        if edges is not None:
            edges[1][0, g] = left
            edges[1][1, g] = right
        return carry

    lax.fori_loop(0, groups, body, 0)


def edge_pass(rows, src_ref, row_out, col_out):
    groups, span, lanes = src_ref.shape
    group = span // rows

    def body(g, carry):
        col = lax.broadcasted_iota(jnp.int32, (group, rows), 1)
        left = jnp.zeros((group, rows), jnp.float32)
        right = jnp.zeros((group, rows), jnp.float32)
        for r in range(rows):
            x = src_ref[g, pl.ds(r, group, stride=rows), :]
            if r == 0:
                row_out[0, g] = x
            if r == rows - 1:
                row_out[1, g] = x
            left = jnp.where(col == r, x[:, 0:1], left)
            right = jnp.where(col == r, x[:, lanes - 1 : lanes], right)
        col_out[0, g] = left
        col_out[1, g] = right
        return carry

    lax.fori_loop(0, groups, body, 0)


def diffuse_kernel(rows, v_ref, c_ref, out_ref, mid_ref, k_ref, row_edge, col_edge, row_halo,
                   col_halo, send_sem, recv_sem):
    lon = lax.axis_index("lon")
    lat = lax.axis_index("lat")
    n_lon = lax.axis_size("lon")
    n_lat = lax.axis_size("lat")
    north = {"lat": (lat + n_lat - 1) % n_lat}
    south = {"lat": (lat + 1) % n_lat}
    west = {"lon": (lon + n_lon - 1) % n_lon}
    east = {"lon": (lon + 1) % n_lon}
    mesh_id = pl.DeviceIdType.MESH

    barrier = pltpu.get_barrier_semaphore()
    for peer in (north, south, west, east):
        pl.semaphore_signal(barrier, inc=1, device_id=peer, device_id_type=mesh_id)
    pl.semaphore_wait(barrier, 4)

    def exchange(rd):
        plan = [
            (row_edge.at[rd, 0], row_halo.at[rd, 1], north, 0),
            (row_edge.at[rd, 1], row_halo.at[rd, 0], south, 1),
            (col_edge.at[rd, 0], col_halo.at[rd, 1], west, 2),
            (col_edge.at[rd, 1], col_halo.at[rd, 0], east, 3),
        ]
        copies = []
        for src, dst, peer, k in plan:
            copy = pltpu.make_async_remote_copy(
                src_ref=src, dst_ref=dst, send_sem=send_sem.at[rd, k], recv_sem=recv_sem.at[rd, k],
                device_id=peer, device_id_type=mesh_id,
            )
            copy.start()
            copies.append(copy)
        return copies

    edge_pass(rows, c_ref, row_edge.at[0], col_edge.at[0])
    edge_pass(rows, v_ref, row_edge.at[1], col_edge.at[1])
    first = exchange(0) + exchange(1)
    for copy in first:
        copy.wait()
    north_ok = jnp.minimum(lat, 1).astype(jnp.float32)
    south_ok = jnp.minimum(n_lat - 1 - lat, 1).astype(jnp.float32)
    scales = (north_ok, south_ok)
    coef_pass(rows, c_ref, (row_halo.at[0], col_halo.at[0]), scales, k_ref)
    slab_pass(rows, v_ref, k_ref, (row_halo.at[1], col_halo.at[1]), scales, mid_ref,
              (row_edge.at[2], col_edge.at[2]))
    for copy in exchange(2):
        copy.wait()
    slab_pass(rows, mid_ref, k_ref, (row_halo.at[2], col_halo.at[2]), scales, out_ref, None)


def diffuse(field, conduct_blocks):
    vals, rows, lanes = field.shape
    groups = vals // GROUP
    blocks = field.reshape(groups, GROUP * rows, lanes)
    rounds = SWEEPS + 1
    out = pl.pallas_call(
        functools.partial(diffuse_kernel, rows),
        in_specs=[VMEM, VMEM],
        out_specs=VMEM,
        out_shape=jax.ShapeDtypeStruct(blocks.shape, jnp.float32),
        scratch_shapes=[
            pltpu.VMEM(blocks.shape, jnp.float32),
            pltpu.VMEM((4, groups, rows, GROUP, lanes), jnp.float32),
            pltpu.VMEM((rounds, 2, groups, GROUP, lanes), jnp.float32),
            pltpu.VMEM((rounds, 2, groups, GROUP, rows), jnp.float32),
            pltpu.VMEM((rounds, 2, groups, GROUP, lanes), jnp.float32),
            pltpu.VMEM((rounds, 2, groups, GROUP, rows), jnp.float32),
            pltpu.SemaphoreType.DMA((rounds, 4)),
            pltpu.SemaphoreType.DMA((rounds, 4)),
        ],
        compiler_params=pltpu.CompilerParams(collective_id=0, has_side_effects=True),
        cost_estimate=pl.CostEstimate(
            flops=50 * field.size, bytes_accessed=12 * field.size, transcendentals=0
        ),
    )(blocks, conduct_blocks)
    return out.reshape(vals, rows, lanes)


def load_row(ref, index):
    return ref[pl.ds(index, 1), :]


def add_row(ref, index, value):
    spot = pl.ds(index, 1)
    ref[spot, :] = ref[spot, :] + value


def select_kernel(index_ref, rows_ref, out_ref):
    cells = rows_ref.shape[0]
    width = out_ref.shape[1]
    sub = lax.broadcasted_iota(jnp.int32, (8, width), 0)

    def body(t, carry):
        tile = jnp.zeros((8, width), jnp.float32)
        for i in range(8):
            source = index_ref[t * 8 + i]
            row = load_row(rows_ref, jnp.minimum(source, cells - 1))
            tile = jnp.where((sub == i) & (source < cells), jnp.broadcast_to(row, (8, width)), tile)
        out_ref[pl.ds(pl.multiple_of(t * 8, 8), 8), :] = tile
        return carry

    lax.fori_loop(0, out_ref.shape[0] // 8, body, 0, unroll=8)


def place_kernel(index_ref, rows_ref, out_ref, *parts):
    cells = out_ref.shape[0]
    for part in parts:
        part[...] = jnp.zeros_like(part)

    def body(t, carry):
        for i, part in enumerate(parts):
            q = t * len(parts) + i
            target = index_ref[q]
            row = load_row(rows_ref, q)
            add_row(part, jnp.minimum(target, cells - 1), jnp.where(target < cells, row, 0.0))
        return carry

    lax.fori_loop(0, rows_ref.shape[0] // len(parts), body, 0, unroll=8)
    total = parts[0][...]
    for part in parts[1:]:
        total = total + part[...]
    out_ref[...] = total


def interp_kernel(slot_ref, weight_ref, received_ref, precision_ref, equiv_ref, returned_ref, *parts):
    taps, obs_count = slot_ref.shape
    width = equiv_ref.shape[1]
    sub = lax.broadcasted_iota(jnp.int32, (8, width), 0)
    for part in parts:
        part[...] = jnp.zeros_like(part)

    def body(t, carry):
        tile = jnp.zeros((8, width), jnp.float32)
        for i in range(8):
            j = t * 8 + i
            slots = [slot_ref[k, j] for k in range(taps)]
            weights = [weight_ref[k, j] for k in range(taps)]
            total = load_row(received_ref, slots[0]) * weights[0]
            for k in range(1, taps):
                total = total + load_row(received_ref, slots[k]) * weights[k]
            tile = jnp.where(sub == i, jnp.broadcast_to(total, (8, width)), tile)
            weighted = load_row(precision_ref, j) * total
            for k in range(taps):
                add_row(parts[k], slots[k], weighted * weights[k])
        equiv_ref[pl.ds(pl.multiple_of(t * 8, 8), 8), :] = tile
        return carry

    lax.fori_loop(0, obs_count // 8, body, 0, unroll=2)
    total = parts[0][...]
    for part in parts[1:]:
        total = total + part[...]
    returned_ref[...] = total


def select_rows(index, rows, count):
    return pl.pallas_call(
        select_kernel,
        in_specs=[SMEM, VMEM],
        out_specs=VMEM,
        out_shape=jax.ShapeDtypeStruct((count, rows.shape[1]), jnp.float32),
    )(index, rows)


def place_rows(index, rows, cells):
    return pl.pallas_call(
        place_kernel,
        in_specs=[SMEM, VMEM],
        out_specs=VMEM,
        out_shape=jax.ShapeDtypeStruct((cells, rows.shape[1]), jnp.float32),
        scratch_shapes=[pltpu.VMEM((cells, rows.shape[1]), jnp.float32) for _ in range(4)],
        compiler_params=pltpu.CompilerParams(vmem_limit_bytes=60 * 1024 * 1024),
    )(index, rows)


def interpolate(obs_slots, obs_weights, received, precision_rows):
    obs_count = obs_slots.shape[1]
    return pl.pallas_call(
        interp_kernel,
        in_specs=[SMEM, SMEM, VMEM, VMEM],
        out_specs=[VMEM, VMEM],
        out_shape=[
            jax.ShapeDtypeStruct((obs_count, received.shape[1]), jnp.float32),
            jax.ShapeDtypeStruct(received.shape, jnp.float32),
        ],
        scratch_shapes=[
            pltpu.VMEM(received.shape, jnp.float32) for _ in range(obs_slots.shape[0])
        ],
        compiler_params=pltpu.CompilerParams(vmem_limit_bytes=60 * 1024 * 1024),
    )(obs_slots, obs_weights, received, precision_rows)


def to_owners(outgoing):
    return lax.all_to_all(outgoing, ("lon", "lat"), split_axis=0, concat_axis=0, tiled=True)


def to_sources(returned):
    return lax.all_to_all(returned, ("lon", "lat"), split_axis=0, concat_axis=0, tiled=True)


def on_device(state, diffusivity, sea_mask, send_cols, obs_slots, obs_weights, obs_precision):
    vals, rows, lanes = state.shape
    cell_count = rows * lanes
    steps = vals // GROUP
    sea_float = sea_mask.astype(jnp.float32)
    conduct = diffusivity * jnp.concatenate([sea_float, sea_float], axis=0)
    conduct_blocks = conduct.reshape(steps, GROUP * rows, lanes)
    smooth = diffuse(state, conduct_blocks)
    rows_of = smooth.transpose(1, 2, 0).reshape(cell_count, vals)
    send_index = send_cols[0]
    outgoing = select_rows(send_index, rows_of, send_index.shape[0])
    received = to_owners(outgoing)
    equivalent_rows, returned = interpolate(obs_slots, obs_weights, received, obs_precision.T)
    equivalents = equivalent_rows.T
    incoming = to_sources(returned)
    adjoint_rows = place_rows(send_index, incoming, cell_count)
    adjoint_field = adjoint_rows.reshape(rows, lanes, vals).transpose(2, 0, 1)
    product = state + diffuse(adjoint_field, conduct_blocks)
    return (product, equivalents)


def solution(mesh):
    placed = (
        P(None, "lat", "lon"),
        P(None, "lat", "lon"),
        P(None, "lat", "lon"),
        P(("lon", "lat"), None),
        P(None, ("lon", "lat")),
        P(None, ("lon", "lat")),
        P(None, ("lon", "lat")),
    )
    return jax.shard_map(
        on_device,
        mesh=mesh,
        in_specs=placed,
        out_specs=(P(None, "lat", "lon"), P(None, ("lon", "lat"))),
        check_vma=False,
    )
```

```python
import functools

import jax
import jax.numpy as jnp
from jax import lax
from jax.experimental import pallas as pl
from jax.experimental.pallas import tpu as pltpu
from jax.sharding import PartitionSpec as P

SWEEPS = 2
GROUP = 30
SMEM = pl.BlockSpec(memory_space=pltpu.SMEM)
VMEM = pl.BlockSpec(memory_space=pltpu.VMEM)


def coef_pass(rows, c_ref, coef_halo, scales, k_ref):
    groups, span, lanes = c_ref.shape
    group = span // rows
    north_ok, south_ok = scales
    coef_rows, coef_cols = coef_halo

    def body(g, carry):
        lane = lax.broadcasted_iota(jnp.int32, (group, lanes), 1)
        cw = coef_cols[0, g]
        ce = coef_cols[1, g]
        c_up = coef_rows[0, g] * north_ok
        c_mid = c_ref[g, pl.ds(0, group, stride=rows), :]
        for r in range(rows):
            if r + 1 < rows:
                c_dn = c_ref[g, pl.ds(r + 1, group, stride=rows), :]
            else:
                c_dn = coef_rows[1, g] * south_ok
            c_w = jnp.where(lane == 0, cw[:, r : r + 1], pltpu.roll(c_mid, 1, 1))
            c_e = jnp.where(lane == lanes - 1, ce[:, r : r + 1], pltpu.roll(c_mid, lanes - 1, 1))
            k_ref[0, g, r] = jnp.minimum(c_mid, c_up)
            k_ref[1, g, r] = jnp.minimum(c_mid, c_dn)
            k_ref[2, g, r] = jnp.minimum(c_mid, c_w)
            k_ref[3, g, r] = jnp.minimum(c_mid, c_e)
            c_up, c_mid = c_mid, c_dn
        return carry

    lax.fori_loop(0, groups, body, 0)


def slab_pass(rows, src_ref, k_ref, field_halo, scales, dst_ref, edges):
    groups, span, lanes = src_ref.shape
    group = span // rows
    north_ok, south_ok = scales
    row_halo, col_halo = field_halo

    def body(g, carry):
        lane = lax.broadcasted_iota(jnp.int32, (group, lanes), 1)
        col = lax.broadcasted_iota(jnp.int32, (group, rows), 1)

        def slab(ref, r):
            return ref[g, pl.ds(r, group, stride=rows), :]

        vw = col_halo[0, g]
        ve = col_halo[1, g]
        left = jnp.zeros((group, rows), jnp.float32)
        right = jnp.zeros((group, rows), jnp.float32)
        x_up = row_halo[0, g] * north_ok
        x_mid = slab(src_ref, 0)
        for r in range(rows):
            if r + 1 < rows:
                x_dn = slab(src_ref, r + 1)
            else:
                x_dn = row_halo[1, g] * south_ok
            x_w = jnp.where(lane == 0, vw[:, r : r + 1], pltpu.roll(x_mid, 1, 1))
            x_e = jnp.where(lane == lanes - 1, ve[:, r : r + 1], pltpu.roll(x_mid, lanes - 1, 1))
            total = k_ref[0, g, r] * (x_up - x_mid)
            total = total + k_ref[1, g, r] * (x_dn - x_mid)
            total = total + k_ref[2, g, r] * (x_w - x_mid)
            total = total + k_ref[3, g, r] * (x_e - x_mid)
            out = x_mid + total
            dst_ref[g, pl.ds(r, group, stride=rows), :] = out
            if edges is not None:
                if r == 0:
                    edges[0][0, g] = out
                if r == rows - 1:
                    edges[0][1, g] = out
                left = jnp.where(col == r, out[:, 0:1], left)
                right = jnp.where(col == r, out[:, lanes - 1 : lanes], right)
            x_up, x_mid = x_mid, x_dn
        if edges is not None:
            edges[1][0, g] = left
            edges[1][1, g] = right
        return carry

    lax.fori_loop(0, groups, body, 0)


def edge_pass(rows, src_ref, row_out, col_out):
    groups, span, lanes = src_ref.shape
    group = span // rows

    def body(g, carry):
        col = lax.broadcasted_iota(jnp.int32, (group, rows), 1)
        left = jnp.zeros((group, rows), jnp.float32)
        right = jnp.zeros((group, rows), jnp.float32)
        for r in range(rows):
            x = src_ref[g, pl.ds(r, group, stride=rows), :]
            if r == 0:
                row_out[0, g] = x
            if r == rows - 1:
                row_out[1, g] = x
            left = jnp.where(col == r, x[:, 0:1], left)
            right = jnp.where(col == r, x[:, lanes - 1 : lanes], right)
        col_out[0, g] = left
        col_out[1, g] = right
        return carry

    lax.fori_loop(0, groups, body, 0)


def diffuse_kernel(rows, v_ref, c_ref, out_ref, mid_ref, k_ref, row_edge, col_edge, row_halo,
                   col_halo, send_sem, recv_sem):
    lon = lax.axis_index("lon")
    lat = lax.axis_index("lat")
    n_lon = lax.axis_size("lon")
    n_lat = lax.axis_size("lat")
    north = {"lat": (lat + n_lat - 1) % n_lat}
    south = {"lat": (lat + 1) % n_lat}
    west = {"lon": (lon + n_lon - 1) % n_lon}
    east = {"lon": (lon + 1) % n_lon}
    mesh_id = pl.DeviceIdType.MESH

    barrier = pltpu.get_barrier_semaphore()
    for peer in (north, south, west, east):
        pl.semaphore_signal(barrier, inc=1, device_id=peer, device_id_type=mesh_id)
    pl.semaphore_wait(barrier, 4)

    def exchange(rd):
        plan = [
            (row_edge.at[rd, 0], row_halo.at[rd, 1], north, 0),
            (row_edge.at[rd, 1], row_halo.at[rd, 0], south, 1),
            (col_edge.at[rd, 0], col_halo.at[rd, 1], west, 2),
            (col_edge.at[rd, 1], col_halo.at[rd, 0], east, 3),
        ]
        copies = []
        for src, dst, peer, k in plan:
            copy = pltpu.make_async_remote_copy(
                src_ref=src, dst_ref=dst, send_sem=send_sem.at[rd, k], recv_sem=recv_sem.at[rd, k],
                device_id=peer, device_id_type=mesh_id,
            )
            copy.start()
            copies.append(copy)
        return copies

    edge_pass(rows, c_ref, row_edge.at[0], col_edge.at[0])
    edge_pass(rows, v_ref, row_edge.at[1], col_edge.at[1])
    first = exchange(0) + exchange(1)
    for copy in first:
        copy.wait()
    north_ok = jnp.minimum(lat, 1).astype(jnp.float32)
    south_ok = jnp.minimum(n_lat - 1 - lat, 1).astype(jnp.float32)
    scales = (north_ok, south_ok)
    coef_pass(rows, c_ref, (row_halo.at[0], col_halo.at[0]), scales, k_ref)
    slab_pass(rows, v_ref, k_ref, (row_halo.at[1], col_halo.at[1]), scales, mid_ref,
              (row_edge.at[2], col_edge.at[2]))
    for copy in exchange(2):
        copy.wait()
    slab_pass(rows, mid_ref, k_ref, (row_halo.at[2], col_halo.at[2]), scales, out_ref, None)


def diffuse(field, conduct_blocks):
    vals, rows, lanes = field.shape
    groups = vals // GROUP
    blocks = field.reshape(groups, GROUP * rows, lanes)
    rounds = SWEEPS + 1
    out = pl.pallas_call(
        functools.partial(diffuse_kernel, rows),
        in_specs=[VMEM, VMEM],
        out_specs=VMEM,
        out_shape=jax.ShapeDtypeStruct(blocks.shape, jnp.float32),
        scratch_shapes=[
            pltpu.VMEM(blocks.shape, jnp.float32),
            pltpu.VMEM((4, groups, rows, GROUP, lanes), jnp.float32),
            pltpu.VMEM((rounds, 2, groups, GROUP, lanes), jnp.float32),
            pltpu.VMEM((rounds, 2, groups, GROUP, rows), jnp.float32),
            pltpu.VMEM((rounds, 2, groups, GROUP, lanes), jnp.float32),
            pltpu.VMEM((rounds, 2, groups, GROUP, rows), jnp.float32),
            pltpu.SemaphoreType.DMA((rounds, 4)),
            pltpu.SemaphoreType.DMA((rounds, 4)),
        ],
        compiler_params=pltpu.CompilerParams(collective_id=0, has_side_effects=True),
        cost_estimate=pl.CostEstimate(
            flops=50 * field.size, bytes_accessed=12 * field.size, transcendentals=0
        ),
    )(blocks, conduct_blocks)
    return out.reshape(vals, rows, lanes)


def load_row(ref, index):
    return ref[pl.ds(index, 1), :]


def add_row(ref, index, value):
    spot = pl.ds(index, 1)
    ref[spot, :] = ref[spot, :] + value


def select_kernel(index_ref, rows_ref, out_ref):
    cells = rows_ref.shape[0]
    width = out_ref.shape[1]
    sub = lax.broadcasted_iota(jnp.int32, (8, width), 0)

    def body(t, carry):
        tile = jnp.zeros((8, width), jnp.float32)
        for i in range(8):
            source = index_ref[t * 8 + i]
            row = load_row(rows_ref, jnp.minimum(source, cells - 1))
            tile = jnp.where((sub == i) & (source < cells), jnp.broadcast_to(row, (8, width)), tile)
        out_ref[pl.ds(pl.multiple_of(t * 8, 8), 8), :] = tile
        return carry

    lax.fori_loop(0, out_ref.shape[0] // 8, body, 0, unroll=4)


def place_kernel(index_ref, rows_ref, out_ref, *parts):
    cells = out_ref.shape[0]
    for part in parts:
        part[...] = jnp.zeros_like(part)

    def body(t, carry):
        for i, part in enumerate(parts):
            q = t * len(parts) + i
            target = index_ref[q]
            row = load_row(rows_ref, q)
            add_row(part, jnp.minimum(target, cells - 1), jnp.where(target < cells, row, 0.0))
        return carry

    lax.fori_loop(0, rows_ref.shape[0] // len(parts), body, 0, unroll=4)
    total = parts[0][...]
    for part in parts[1:]:
        total = total + part[...]
    out_ref[...] = total


def interp_kernel(slot_ref, weight_ref, received_ref, precision_ref, equiv_ref, returned_ref, *parts):
    taps, obs_count = slot_ref.shape
    width = equiv_ref.shape[1]
    sub = lax.broadcasted_iota(jnp.int32, (8, width), 0)
    for part in parts:
        part[...] = jnp.zeros_like(part)

    def body(t, carry):
        tile = jnp.zeros((8, width), jnp.float32)
        for i in range(8):
            j = t * 8 + i
            slots = [slot_ref[k, j] for k in range(taps)]
            weights = [weight_ref[k, j] for k in range(taps)]
            total = load_row(received_ref, slots[0]) * weights[0]
            for k in range(1, taps):
                total = total + load_row(received_ref, slots[k]) * weights[k]
            tile = jnp.where(sub == i, jnp.broadcast_to(total, (8, width)), tile)
            weighted = load_row(precision_ref, j) * total
            for k in range(taps):
                add_row(parts[k], slots[k], weighted * weights[k])
        equiv_ref[pl.ds(pl.multiple_of(t * 8, 8), 8), :] = tile
        return carry

    lax.fori_loop(0, obs_count // 8, body, 0, unroll=4)
    total = parts[0][...]
    for part in parts[1:]:
        total = total + part[...]
    returned_ref[...] = total


def select_rows(index, rows, count):
    return pl.pallas_call(
        select_kernel,
        in_specs=[SMEM, VMEM],
        out_specs=VMEM,
        out_shape=jax.ShapeDtypeStruct((count, rows.shape[1]), jnp.float32),
    )(index, rows)


def place_rows(index, rows, cells):
    return pl.pallas_call(
        place_kernel,
        in_specs=[SMEM, VMEM],
        out_specs=VMEM,
        out_shape=jax.ShapeDtypeStruct((cells, rows.shape[1]), jnp.float32),
        scratch_shapes=[pltpu.VMEM((cells, rows.shape[1]), jnp.float32) for _ in range(4)],
        compiler_params=pltpu.CompilerParams(vmem_limit_bytes=60 * 1024 * 1024),
    )(index, rows)


def interpolate(obs_slots, obs_weights, received, precision_rows):
    obs_count = obs_slots.shape[1]
    return pl.pallas_call(
        interp_kernel,
        in_specs=[SMEM, SMEM, VMEM, VMEM],
        out_specs=[VMEM, VMEM],
        out_shape=[
            jax.ShapeDtypeStruct((obs_count, received.shape[1]), jnp.float32),
            jax.ShapeDtypeStruct(received.shape, jnp.float32),
        ],
        scratch_shapes=[
            pltpu.VMEM(received.shape, jnp.float32) for _ in range(obs_slots.shape[0])
        ],
        compiler_params=pltpu.CompilerParams(vmem_limit_bytes=60 * 1024 * 1024),
    )(obs_slots, obs_weights, received, precision_rows)


def to_owners(outgoing):
    return lax.all_to_all(outgoing, ("lon", "lat"), split_axis=0, concat_axis=0, tiled=True)


def to_sources(returned):
    return lax.all_to_all(returned, ("lon", "lat"), split_axis=0, concat_axis=0, tiled=True)


def on_device(state, diffusivity, sea_mask, send_cols, obs_slots, obs_weights, obs_precision):
    vals, rows, lanes = state.shape
    cell_count = rows * lanes
    steps = vals // GROUP
    sea_float = sea_mask.astype(jnp.float32)
    conduct = diffusivity * jnp.concatenate([sea_float, sea_float], axis=0)
    conduct_blocks = conduct.reshape(steps, GROUP * rows, lanes)
    smooth = diffuse(state, conduct_blocks)
    rows_of = smooth.transpose(1, 2, 0).reshape(cell_count, vals)
    send_index = send_cols[0]
    outgoing = select_rows(send_index, rows_of, send_index.shape[0])
    received = to_owners(outgoing)
    equivalent_rows, returned = interpolate(obs_slots, obs_weights, received, obs_precision.T)
    equivalents = equivalent_rows.T
    incoming = to_sources(returned)
    adjoint_rows = place_rows(send_index, incoming, cell_count)
    adjoint_field = adjoint_rows.reshape(rows, lanes, vals).transpose(2, 0, 1)
    product = state + diffuse(adjoint_field, conduct_blocks)
    return (product, equivalents)


def solution(mesh):
    placed = (
        P(None, "lat", "lon"),
        P(None, "lat", "lon"),
        P(None, "lat", "lon"),
        P(("lon", "lat"), None),
        P(None, ("lon", "lat")),
        P(None, ("lon", "lat")),
        P(None, ("lon", "lat")),
    )
    return jax.shard_map(
        on_device,
        mesh=mesh,
        in_specs=placed,
        out_specs=(P(None, "lat", "lon"), P(None, ("lon", "lat"))),
        check_vma=False,
    )
```
